32 devices in a mesh: chan: 4 (over y, x), blk: 8 (over z, core).
Axes of the slice: x: 2, y: 2, z: 4, core: 2. Of those that a mesh axis runs over, the one named last changes fastest.
Arguments:
- coeffs: bfloat16 [12, 2, 3072, 1536], P('chan', None, 'blk'), may hold values from -0.15 to 0.15
- legendre: bfloat16 [4, 768, 256, 1536], P('chan', 'blk'), may hold values from -0.15625 to 0.15625
- m_order: int32 [3072], replicated, may hold values from 0 to 3071, as said below
- sector_len: int32 [512, 16], P(('chan', 'blk')), may hold values from 256 to 4352, as said below
Outputs:
- ilc_map: float32 [512, 8192], P(('chan', 'blk'))
The draws below stay inside these ranges and needn't reach their ends.
Inputs may be any that keep to these rules, and one draw needn't show every extreme that they name: `m_order`: a permutation of 0 to 3071; slots 2 j and 2 j + 1 hold the orders m and 3071 - m. `sector_len`: the 16 lengths of each cycle sum to 8192.
All inputs are finite; a program needn't handle non-finite values.
Results may differ from the reference program's by a relative error of at most 0.0003.
Values may be sent and summed in bfloat16 or wider, within the bound.
A program may use at most 512 MiB of HBM per device.

```python
import jax
import jax.numpy as jnp
from jax import lax

CH = 12
M = 3072
LB = 1536
PIX = 8192
NSEC = 16
RN = 256
GROUPS = 4
N_CHAN = 4
N_BLK = 8


def draw_coeffs(key, part):
    shape_all = (CH, 2, M, LB)
    common_key = jax.random.fold_in(key, 101)
    noise_key = jax.random.fold_in(key, 202)
    spread_key = jax.random.fold_in(key, 303)
    common = jax.random.truncated_normal(common_key, -4.0, 4.0, (1, 2, M, LB), jnp.float32)
    noise_part = jax.random.truncated_normal(noise_key, -4.0, 4.0, shape_all, jnp.float32)
    spread = jnp.exp(jax.random.uniform(spread_key, (CH, 1, 1, 1), jnp.float32, -0.6931472, 0.6931472))
    return (0.0125 * (common + spread * noise_part)).astype(jnp.bfloat16)


def draw_m_order(key, part):
    pair_low = jax.random.permutation(key, M // 2).astype(jnp.int32)
    return jnp.stack([pair_low, M - 1 - pair_low], axis=1).reshape(M).astype(jnp.int32)


def draw_sector_len(key, part):
    cycle_count = 2 * RN
    spare_pixels = PIX // 2
    least_length = PIX // (2 * NSEC)
    inner_cuts = jax.random.randint(jax.random.fold_in(key, 7), (cycle_count, NSEC - 2), 0, spare_pixels + 1, dtype=jnp.int32)
    keep_rows = (jnp.arange(cycle_count, dtype=jnp.int32) > 0).astype(jnp.int32)
    inner_cuts = inner_cuts * keep_rows[:, None]
    cut_points = jnp.sort(jnp.concatenate([jnp.zeros((cycle_count, 1), jnp.int32), inner_cuts], axis=1), axis=1)
    bounds = jnp.concatenate([cut_points, jnp.full((cycle_count, 1), spare_pixels, jnp.int32)], axis=1)
    extra_pixels = bounds - jnp.concatenate([jnp.zeros((cycle_count, 1), jnp.int32), bounds[:, :-1]], axis=1)
    lengths = least_length + extra_pixels
    offset = jax.random.randint(jax.random.fold_in(key, 9), (cycle_count, 1), 0, NSEC, dtype=jnp.int32)
    rotation = (jnp.arange(NSEC, dtype=jnp.int32)[None, :] + offset) % NSEC
    return jnp.take_along_axis(lengths, rotation, axis=1).astype(jnp.int32)


def block_levels(rng, shape, split, smallest, high):
    gain, own = 1.0, jax.random.fold_in(rng, 6)
    for axis_at, shards_of in split:
        draws = jnp.exp(jax.random.uniform(jax.random.fold_in(own, axis_at), (shards_of,), jnp.float32, smallest / len(split), high / len(split)))
        gain = gain * jnp.repeat(draws, shape[axis_at] // shards_of).reshape([-1 if axis == axis_at else 1 for axis in range(len(shape))])
    return gain


def normal_values(key, extent, deviation, limit, split=(), kind=jnp.bfloat16):
    values = deviation * jax.random.normal(key, extent, jnp.float32)
    if split:
        values = values * block_levels(key, extent, split, -0.22, 0.18)
    return jnp.clip(values, -limit, limit).astype(kind)


def setup_inputs(seed: int = 0) -> dict:
    streams_of = jax.random.split(jax.random.key(seed), 5)
    coeffs = draw_coeffs(jax.random.fold_in(streams_of[4], 71), 0)
    legendre = normal_values(streams_of[1], (GROUPS, M // GROUPS, RN, LB), LB ** -0.5, 0.15625, ((0, 4), (1, 8)))
    m_order = draw_m_order(jax.random.fold_in(streams_of[4], 71), 0)
    sector_len = draw_sector_len(jax.random.fold_in(streams_of[4], 71), 0)
    return {"coeffs": coeffs, "legendre": legendre, "m_order": m_order, "sector_len": sector_len}


RIDGE_FACTOR = 0.05
TWO_PI = 6.283185307179586

def legendre_block(coeff_block, operator, orders):
    highest = lax.Precision.HIGHEST
    degree = M - LB + lax.iota(jnp.int32, LB)
    valid_mask = degree[None, :] >= orders[:, None]
    odd_mask = (degree[None, :] + orders[:, None]) % 2 == 1
    zero_value = jnp.zeros((), coeff_block.dtype)
    even_part = jnp.where((valid_mask & ~odd_mask)[None, None], coeff_block, zero_value)
    odd_part = jnp.where((valid_mask & odd_mask)[None, None], coeff_block, zero_value)
    operator_wide = operator.astype(jnp.float32)
    even_sum = jnp.einsum('cpsl,srl->cprs', even_part.astype(jnp.float32), operator_wide, precision=highest)
    odd_sum = jnp.einsum('cpsl,srl->cprs', odd_part.astype(jnp.float32), operator_wide, precision=highest)
    return jnp.concatenate([even_sum + odd_sum, even_sum - odd_sum], axis=2)

def cycle_synthesis(spectra, orders):
    highest = lax.Precision.HIGHEST
    order_count = spectra.shape[-1]
    fine_count = 128
    coarse_count = PIX // fine_count
    coarse_phase = (lax.iota(jnp.int32, coarse_count) * fine_count)[:, None] * orders[None, :] % PIX
    fine_phase = orders[:, None] * lax.iota(jnp.int32, fine_count)[None, :] % PIX
    coarse_angle = coarse_phase.astype(jnp.float32) * (TWO_PI / PIX)
    fine_angle = fine_phase.astype(jnp.float32) * (TWO_PI / PIX)
    weight = jnp.where(orders == 0, 1.0, 2.0).astype(jnp.float32)
    coarse_cos = jnp.cos(coarse_angle)
    coarse_sin = jnp.sin(coarse_angle)
    fine_cos = weight[:, None] * jnp.cos(fine_angle)
    fine_sin = weight[:, None] * jnp.sin(fine_angle)
    real_part = spectra[:, 0].reshape(-1, 1, order_count)
    imag_part = spectra[:, 1].reshape(-1, 1, order_count)
    shifted_real = (real_part * coarse_cos[None] - imag_part * coarse_sin[None]).reshape(-1, order_count)
    shifted_imag = (real_part * coarse_sin[None] + imag_part * coarse_cos[None]).reshape(-1, order_count)
    result = jnp.dot(shifted_real.astype(jnp.float32), fine_cos.astype(jnp.float32), precision=highest, preferred_element_type=jnp.float32)
    result = result - jnp.dot(shifted_imag.astype(jnp.float32), fine_sin.astype(jnp.float32), precision=highest, preferred_element_type=jnp.float32)
    return result.reshape(spectra.shape[0], spectra.shape[2], PIX)

def cycle_combine(cycle_map, lengths):
    highest = lax.Precision.HIGHEST
    channel_count = cycle_map.shape[0]
    sector_end = jnp.cumsum(lengths).astype(jnp.int32)
    sector_start = (sector_end - lengths).astype(jnp.int32)
    pixels = lax.iota(jnp.int32, PIX)
    member = ((pixels[None, :] >= sector_start[:, None]) & (pixels[None, :] < sector_end[:, None])).astype(jnp.float32)
    products = (cycle_map[:, None, :] * cycle_map[None, :, :]).reshape(channel_count * channel_count, PIX)
    moments = jnp.einsum('qx,kx->kq', products, member, precision=highest)
    covariance = moments.reshape(-1, channel_count, channel_count) / lengths.astype(jnp.float32)[:, None, None]
    trace_part = jnp.trace(covariance, axis1=1, axis2=2) * (RIDGE_FACTOR / channel_count)
    regular = covariance + trace_part[:, None, None] * jnp.eye(channel_count, dtype=jnp.float32)
    factor = jnp.linalg.cholesky(regular)
    unit_rhs = jnp.ones((covariance.shape[0], channel_count, 1), jnp.float32)
    forward = lax.linalg.triangular_solve(factor, unit_rhs, left_side=True, lower=True)
    solved = lax.linalg.triangular_solve(factor, forward, left_side=True, lower=True, transpose_a=True)[:, :, 0]
    weights = solved / jnp.sum(solved, axis=1, keepdims=True)
    pixel_weights = jnp.einsum('ka,kx->ax', weights, member, precision=highest)
    return jnp.sum(pixel_weights * cycle_map, axis=0)

def reference(coeffs, legendre, m_order, sector_len):
    slot_count = M // (N_CHAN * N_BLK)
    block_span = N_CHAN * slot_count

    def one_block(block_number):
        coeff_block = lax.dynamic_slice_in_dim(coeffs, block_number * block_span, block_span, 2)
        operator = lax.dynamic_slice_in_dim(legendre, block_number * slot_count, slot_count, 1)
        operator = operator.reshape(block_span, RN, LB)
        orders = lax.dynamic_slice_in_dim(m_order, block_number * block_span, block_span, 0)
        return legendre_block(coeff_block, operator, orders)
    blocks = lax.map(one_block, jnp.arange(N_BLK, dtype=jnp.int32))
    spectra = jnp.moveaxis(blocks, 0, 3).reshape(CH, 2, 2 * RN, M)
    cycle_maps = lax.map(lambda channel: cycle_synthesis(channel[None], m_order)[0], spectra)
    return lax.map(lambda cycle_pair: cycle_combine(cycle_pair[0], cycle_pair[1]), (jnp.moveaxis(cycle_maps, 1, 0), sector_len))
```

```python
import functools

import jax
import jax.numpy as jnp
import numpy as np
from jax import lax
from jax.experimental import pallas as pl
from jax.experimental.pallas import tpu as pltpu
from jax.sharding import PartitionSpec as P

PIX = 8192
LOW = 128
HIGH = PIX // LOW
RIDGE_FACTOR = 0.05
TWO_PI = 6.283185307179586
CHUNK = 1024
GROUP_ROWS = 16
MESH = pl.DeviceIdType.MESH
CHUNK_SLOTS = 16
LOAD_SLOTS = 4
LOAD_BUFFERS = 3
AHEAD = 2
CODE_MAX = 32767.0


def block_transpose(values, lane):
    values = list(values)
    for bit in (1, 2, 4):
        upper = (lane // 16) % (2 * bit) >= bit
        for i in range(8):
            if i & bit:
                continue
            a, b = values[i], values[i | bit]
            values[i] = jnp.where(upper, pltpu.roll(b, 16 * bit, 1), a)
            values[i | bit] = jnp.where(upper, b, pltpu.roll(a, LOW - 16 * bit, 1))
    return values


def tile_rows(channels):
    return [
        [(c, 0) for c in range(8)],
        [(c, 1) for c in range(8)],
        [(c, 0) for c in range(8, channels)] + [(c, 1) for c in range(8, channels)],
    ]


def exchange_kernel(
    groups, blocks, coeffs, legendre, order_ref, data_out, scale_out,
    rbuf, lbuf, valid_ref, sign_ref, xs, sp, msg, inverse, scl, tbuf,
    csend, crecv, lsem, dsend, drecv, ssend, srecv,
):
    chunks, _, local_channels, parts, size, degrees = rbuf.shape
    channels = groups * local_channels
    rows = channels * parts
    slots = chunks * size
    tiles = degrees // LOW
    devices = groups * blocks
    g = lax.axis_index("chan")
    b = lax.axis_index("blk")
    me = g * blocks + b

    def peer(i):
        return lax.rem(g + i // blocks, groups), lax.rem(b + i % blocks, blocks)

    barrier = pltpu.get_barrier_semaphore()

    def greet(i, carry):
        pl.semaphore_signal(barrier, inc=1, device_id=peer(i), device_id_type=MESH)
        return carry

    lax.fori_loop(1, devices, greet, 0)

    def load(t):
        return pltpu.make_async_copy(
            legendre.at[pl.ds(t * LOAD_SLOTS, LOAD_SLOTS)],
            lbuf.at[lax.rem(t, LOAD_BUFFERS)], lsem.at[lax.rem(t, LOAD_BUFFERS)],
        )

    for t in range(LOAD_BUFFERS):
        load(t).start()
    degree = lax.broadcasted_iota(jnp.int32, (slots, degrees), 1)
    order = order_ref[...]
    degree = degree + order_ref.shape[0] * devices - degrees
    keep = jnp.where(degree >= order, 1.0, 0.0)
    valid_ref[...] = keep
    sign_ref[...] = keep * (1 - 2 * ((degree + order) % 2)).astype(jnp.float32)
    pl.semaphore_wait(barrier, devices - 1)

    def start_coeffs(j):
        for i in range(1, groups):
            to = lax.rem(g + i, groups)
            pltpu.make_async_remote_copy(
                src_ref=coeffs.at[:, :, pl.ds(to * slots + j * size, size), :],
                dst_ref=rbuf.at[j, g],
                send_sem=csend, recv_sem=crecv.at[j],
                device_id=(to, b), device_id_type=MESH,
            ).start()
        pltpu.make_async_copy(
            coeffs.at[:, :, pl.ds(g * slots + j * size, size), :], rbuf.at[j, g], crecv.at[j]
        ).start()

    for j in range(AHEAD):
        start_coeffs(j)
    lane = lax.broadcasted_iota(jnp.int32, (size, LOW), 1)
    layout = tile_rows(channels)

    def chunk(j, carry):
        pltpu.make_async_copy(rbuf.at[j], rbuf.at[j], crecv.at[j]).wait()
        for q in range(groups):
            for c in range(local_channels):
                for p in range(parts):
                    row = ((q * local_channels + c) * parts + p) * size
                    wide = rbuf[j, q, c, p].astype(jnp.float32)
                    for t in range(tiles):
                        xs[t, row : row + size, :] = wide[:, t * LOW : (t + 1) * LOW]

        def step(u, carry):
            t = j * (size // LOAD_SLOTS) + u
            load(t).wait()
            for v in range(LOAD_SLOTS):
                s = u * LOAD_SLOTS + v
                x = jnp.concatenate(
                    [xs[i, pl.ds(s, rows, stride=size), :] for i in range(tiles)], axis=1
                )
                at = pl.ds(j * size + s, 1)
                both = jnp.concatenate([x * valid_ref[at, :], x * sign_ref[at, :]], axis=0)
                sums = lax.dot_general(
                    both.astype(jnp.bfloat16), lbuf[lax.rem(t, LOAD_BUFFERS), v],
                    (((1,), (1,)), ((), ())), preferred_element_type=jnp.float32,
                )
                for i in range(sp.shape[0]):
                    sp[i, pl.ds(s, 2 * rows, stride=size), :] = sums[:, i * LOW : (i + 1) * LOW]

            @pl.when(t + LOAD_BUFFERS < slots // LOAD_SLOTS)
            def _():
                load(t + LOAD_BUFFERS).start()

            return carry

        lax.fori_loop(0, size // LOAD_SLOTS, step, 0)

        def piece(half, side, c, p):
            row = (half * rows + c * parts + p) * size
            return sp[side, row : row + size, :]

        scales = jnp.zeros((size, LOW), jnp.float32)
        for c in range(channels):
            top = jnp.abs(piece(0, 0, c, 0))
            for half in range(2):
                for side in range(sp.shape[0]):
                    for p in range(parts):
                        top = jnp.maximum(top, jnp.abs(piece(half, side, c, p)))
            top = jnp.maximum(jnp.max(top, axis=1, keepdims=True), 1e-30)
            unit = (top * (1.0078125 / CODE_MAX)).astype(jnp.bfloat16).astype(jnp.float32)
            inverse[c] = jnp.broadcast_to(1.0 / unit, (size, LOW))
            scales = jnp.where(lane == c, unit, scales)
        scl[pl.ds(pl.multiple_of(j * size, size), size), :] = scales
        for half in range(2):
            for side in range(sp.shape[0]):
                first = (half * sp.shape[0] + side) * blocks
                for tile, members in enumerate(layout):
                    values = block_transpose(
                        [piece(half, side, c, p) * inverse[c] for c, p in members], lane
                    )
                    for k in range(blocks):
                        msg[j, first + k, tile] = jnp.round(values[k]).astype(jnp.int16)

        def send(i, carry):
            to = peer(i)
            pltpu.make_async_remote_copy(
                src_ref=msg.at[j, to[0] * blocks + to[1]], dst_ref=data_out.at[me, j],
                send_sem=dsend, recv_sem=drecv, device_id=to, device_id_type=MESH,
            ).start()
            return carry

        lax.fori_loop(1, devices, send, 0)
        pltpu.make_async_copy(msg.at[j, me], data_out.at[me, j], drecv).start()

        @pl.when(j + AHEAD < chunks)
        def _():
            start_coeffs(j + AHEAD)

        return carry

    lax.fori_loop(0, chunks, chunk, 0)
    turned = jnp.transpose(scl[...])
    tbuf[...] = turned[: tbuf.shape[0]].astype(jnp.bfloat16)

    def send_scale(i, carry):
        pltpu.make_async_remote_copy(
            src_ref=tbuf, dst_ref=scale_out.at[me],
            send_sem=ssend, recv_sem=srecv, device_id=peer(i), device_id_type=MESH,
        ).start()
        return carry

    lax.fori_loop(1, devices, send_scale, 0)
    pltpu.make_async_copy(tbuf, scale_out.at[me], srecv).start()

    def settle(ref, sem):
        pltpu.make_async_copy(ref, ref, sem).wait()

    settle(rbuf.at[:, pl.ds(0, groups - 1)], csend)
    settle(msg.at[:, pl.ds(0, devices - 1)], dsend)
    settle(scale_out.at[pl.ds(0, devices - 1)], ssend)
    settle(data_out, drecv)
    settle(scale_out, srecv)


def exchange(coeffs, operator, orders, groups, blocks):
    local_channels, parts, _, degrees = coeffs.shape
    slots, north, _ = operator.shape
    channels = groups * local_channels
    devices = groups * blocks
    size = CHUNK_SLOTS
    chunks = slots // size
    rows = channels * parts
    sides = north // LOW
    anywhere = pl.BlockSpec(memory_space=pl.ANY)
    dma = pltpu.SemaphoreType.DMA
    return pl.pallas_call(
        functools.partial(exchange_kernel, groups, blocks),
        in_specs=[anywhere, anywhere, pl.BlockSpec(memory_space=pltpu.VMEM)],
        out_specs=[anywhere, anywhere],
        out_shape=[
            jax.ShapeDtypeStruct((devices, chunks, 3, size, LOW), jnp.int16),
            jax.ShapeDtypeStruct((devices, 16, LOW), jnp.bfloat16),
        ],
        scratch_shapes=[
            pltpu.VMEM((chunks, groups, local_channels, parts, size, degrees), jnp.bfloat16),
            pltpu.VMEM((LOAD_BUFFERS, LOAD_SLOTS, north, degrees), jnp.bfloat16),
            pltpu.VMEM((slots, degrees), jnp.float32),
            pltpu.VMEM((slots, degrees), jnp.float32),
            pltpu.VMEM((degrees // LOW, rows * size, LOW), jnp.float32),
            pltpu.VMEM((sides, 2 * rows * size, LOW), jnp.float32),
            pltpu.VMEM((chunks, devices, 3, size, LOW), jnp.int16),
            pltpu.VMEM((channels, size, LOW), jnp.float32),
            pltpu.VMEM((LOW, LOW), jnp.float32),
            pltpu.VMEM((16, LOW), jnp.bfloat16),
            dma, dma((chunks,)), dma((LOAD_BUFFERS,)), dma, dma, dma, dma,
        ],
        compiler_params=pltpu.CompilerParams(
            collective_id=0, has_side_effects=True, vmem_limit_bytes=52 << 20
        ),
    )(coeffs, operator, orders[:, None])


def halves(value):
    upper = value.astype(jnp.bfloat16)
    return upper, (value - upper.astype(jnp.float32)).astype(jnp.bfloat16)


def synthesis_tables(order_count):
    digits = order_count // LOW
    order = np.arange(LOW)[:, None, None] + LOW * np.arange(digits)[None, None, :]
    angle = order * np.arange(HIGH)[None, :, None] % PIX * (2.0 * np.pi / PIX)
    weight = np.where(order == 0, 1.0, 2.0)
    cos, sin = weight * np.cos(angle), weight * np.sin(angle)
    turn = np.stack([np.concatenate([cos, -sin], 2), np.concatenate([sin, cos], 2)], 2)
    turn = turn.reshape(LOW, 2 * HIGH, 2 * digits).astype(np.float32)
    turn_upper = turn.astype(jnp.bfloat16)
    turn_lower = (turn - turn_upper.astype(np.float32)).astype(jnp.bfloat16)
    first = np.concatenate([turn_upper, turn_upper, turn_lower], 2)
    angle = np.arange(LOW)[:, None] * np.arange(LOW)[None, :] % LOW * (2.0 * np.pi / LOW)
    wave = np.concatenate([np.cos(angle), -np.sin(angle)], 1).astype(np.float32)
    wave_upper = wave.astype(jnp.bfloat16)
    wave_lower = (wave - wave_upper.astype(np.float32)).astype(jnp.bfloat16)
    return first, np.concatenate([wave_upper, wave_lower], 0)


def pair_place(a, b):
    if b < 8:
        shift = b - a
        return (shift, a) if shift <= 4 else (8 - shift, b)
    if a < 8:
        return 5 + (b - 8 - a) % 4, a
    a, b = a - 8, b - 8
    shift = b - a
    if shift == 2:
        return 10, a
    return 9, {0: a, 1: 4 + a, 3: 4 + b}[shift]


TILES = 11


def combine_kernel(
    channels, digits, place_ref, data, scale, spread, first_any, wave, lens, out,
    first, spare, order_rows, turned, sums, cov, heads, first_sem,
):
    sources, chunks, _, size, _ = data.shape
    slots = chunks * size
    fetch = pltpu.make_async_copy(first_any, first, first_sem)
    fetch.start()

    def gather(src, carry):
        unit = lax.dot_general(
            scale[src], spread[...], (((0,), (0,)), ((), ())), preferred_element_type=jnp.float32
        )
        for j in range(chunks):
            for t in range(3):
                value = data[src, j, t].astype(jnp.float32)
                value = value * unit[j * size : (j + 1) * size, t * LOW : (t + 1) * LOW]
                spare[pl.ds(j * size * 8 + t, size, stride=8), :] = value
        base = src * slots

        def move(s, carry):
            to = pl.multiple_of(place_ref[base + s], 8)
            order_rows[pl.ds(to, 8), :] = spare[pl.ds(pl.multiple_of(s * 8, 8), 8), :]
            return carry

        return lax.fori_loop(0, slots, move, carry, unroll=16)

    lax.fori_loop(0, sources, gather, 0)
    fetch.wait()
    lane_d = lax.broadcasted_iota(jnp.int32, (digits, LOW), 1)
    wide = LOW * 2 * HIGH

    def turn(l, carry):
        t0, t1, t2 = (
            order_rows[pl.ds(l * (digits * 8) + t, digits, stride=8), :] for t in range(3)
        )
        t3 = pltpu.roll(t2, LOW // 2, 1)
        real = jnp.where(lane_d < LOW // 2, t2, t3)
        imag = jnp.where(lane_d < LOW // 2, t3, t2)
        x = jnp.concatenate(
            [jnp.concatenate([t0, real], 1), jnp.concatenate([t1, imag], 1)], 0
        )
        upper, lower = halves(x)
        y = jnp.dot(
            first[l], jnp.concatenate([upper, lower, upper], 0), preferred_element_type=jnp.float32
        )
        turned[pl.ds(l, 2 * HIGH, stride=LOW), :] = y[:, :LOW]
        turned[pl.ds(wide + l, 2 * HIGH, stride=LOW), :] = y[:, LOW:]
        return carry

    lax.fori_loop(0, LOW, turn, 0, unroll=4)

    def spin(x, carry):
        at = pl.ds(pl.multiple_of(x * 2 * LOW, 2 * LOW), 2 * LOW)
        over = pl.ds(pl.multiple_of(wide + x * 2 * LOW, 2 * LOW), 2 * LOW)
        upper, lower = halves(jnp.concatenate([turned[at, :], turned[over, :]], 1))
        main = jnp.dot(wave[...], upper, preferred_element_type=jnp.float32)
        rest = jnp.dot(wave[:LOW], lower, preferred_element_type=jnp.float32)
        value = main[:LOW] + main[LOW:] + rest
        order_rows[pl.ds(pl.multiple_of(x * LOW, LOW), LOW), :] = value[:, :LOW]
        order_rows[pl.ds(pl.multiple_of(PIX + x * LOW, LOW), LOW), :] = value[:, LOW:]
        return carry

    lax.fori_loop(0, HIGH, spin, 0, unroll=2)

    sectors = lens.shape[0]
    length = lens[...]
    ends = []
    for k in range(sectors):
        ends.append(length[k : k + 1] + ends[-1] if k else length[:1])
    lane = lax.broadcasted_iota(jnp.int32, (8, LOW), 1)
    sub = lax.broadcasted_iota(jnp.int32, (8, LOW), 0)

    def block(j):
        begin = (j * 8 + sub) * HIGH
        sector = jnp.zeros((8, LOW), jnp.int32)
        after = jnp.full((8, LOW), 2 * PIX, jnp.int32)
        for k in range(sectors):
            past = ends[k] <= begin
            sector = sector + jnp.where(past, 1, 0)
            after = jnp.minimum(after, jnp.where(past, 2 * PIX, ends[k]))
        return sector, after - begin

    def pair(j, x):
        at = pl.multiple_of(x * LOW + j * 8, 8)
        return order_rows[pl.ds(at, 8), :], order_rows[pl.ds(PIX + at, 8), :]

    sums[...] = jnp.zeros_like(sums)

    def moments(j, carry):
        sector, limit = block(j)

        def add(x, acc):
            a, b = pair(j, x)
            inside = limit > x
            ah = jnp.where(inside, a, 0.0)
            bh = jnp.where(inside, b, 0.0)
            b1, b2, b3 = (pltpu.roll(b, LOW - 16 * d, 1) for d in (1, 2, 3))
            with_a = [a] + [pltpu.roll(a, LOW - 16 * d, 1) for d in range(1, 5)] + [b, b1, b2, b3]
            with_b = [jnp.where(lane < LOW // 2, b, b1), b2]
            full = [acc[i] + a * v for i, v in enumerate(with_a)]
            full += [acc[9 + i] + b * v for i, v in enumerate(with_b)]
            head = [acc[TILES + i] + ah * v for i, v in enumerate(with_a)]
            head += [acc[TILES + 9 + i] + bh * v for i, v in enumerate(with_b)]
            return tuple(full + head)

        zero = jnp.zeros((8, LOW), jnp.float32)
        acc = lax.fori_loop(0, HIGH, add, (zero,) * (2 * TILES), unroll=2)
        tails = [acc[i] - acc[TILES + i] for i in range(TILES)]
        for i in range(TILES):
            heads[i] = acc[TILES + i]
            heads[TILES + i] = tails[i]

        def assign(k, carry):
            here = sector == k
            there = sector + 1 == k
            for i in range(TILES):
                sums[k, i] += jnp.where(here, heads[i], 0.0) + jnp.where(there, heads[TILES + i], 0.0)
            return carry

        return lax.fori_loop(0, sectors, assign, carry)

    lax.fori_loop(0, LOW // 8, moments, 0)

    def collect(k, carry):
        for i in range(TILES):
            cov[i, pl.ds(k, 1), :] = jnp.sum(sums[k, i], axis=0, keepdims=True)
        return carry

    lax.fori_loop(0, sectors, collect, 0)
    share = 1.0 / length.astype(jnp.float32)

    def entry(a, b):
        tile, group = pair_place(a, b)
        value = cov[tile] * share
        return pltpu.roll(value, LOW - 16 * group, 1) if group else value

    full = {(a, b): entry(a, b) for a in range(channels) for b in range(a, channels)}
    trace = full[0, 0]
    for a in range(1, channels):
        trace = trace + full[a, a]
    ridge = trace * (RIDGE_FACTOR / channels)
    for a in range(channels):
        full[a, a] = full[a, a] + ridge
    rhs = [jnp.ones_like(ridge) for _ in range(channels)]
    inverse = []
    for a in range(channels):
        inverse.append(1.0 / full[a, a])
        for b in range(a + 1, channels):
            factor = full[a, b] * inverse[a]
            for c in range(b, channels):
                full[b, c] = full[b, c] - factor * full[a, c]
            rhs[b] = rhs[b] - factor * rhs[a]
    solved = [None] * channels
    for a in reversed(range(channels)):
        value = rhs[a]
        for b in range(a + 1, channels):
            value = value - full[a, b] * solved[b]
        solved[a] = value * inverse[a]
    total = solved[0]
    for a in range(1, channels):
        total = total + solved[a]
    near = jnp.zeros_like(total)
    far = jnp.zeros_like(total)
    group = lax.broadcasted_iota(jnp.int32, total.shape, 1) // 16
    for a in range(channels):
        weight = solved[a] / total
        place = a % 8
        moved = pltpu.roll(weight, 16 * place, 1) if place else weight
        if a < 8:
            near = jnp.where(group == place, moved, near)
        else:
            far = jnp.where(group == place, moved, far)
    cov[0] = near
    cov[1] = far

    def apply(j, carry):
        sector, limit = block(j)
        picked = [jnp.zeros((8, LOW), jnp.float32) for _ in range(4)]
        for k in range(sectors):
            near_k = cov[0, k : k + 1, :]
            far_k = cov[1, k : k + 1, :]
            here = sector == k
            there = sector + 1 == k
            picked[0] = jnp.where(here, near_k, picked[0])
            picked[1] = jnp.where(here, far_k, picked[1])
            picked[2] = jnp.where(there, near_k, picked[2])
            picked[3] = jnp.where(there, far_k, picked[3])

        def weigh(x, carry):
            a, b = pair(j, x)
            inside = limit > x
            value = jnp.where(inside, picked[0], picked[2]) * a
            value = value + jnp.where(inside, picked[1], picked[3]) * b
            order_rows[pl.ds(2 * PIX + j * 8 * HIGH + x, 8, stride=HIGH), :] = value
            return carry

        return lax.fori_loop(0, HIGH, weigh, carry, unroll=4)

    lax.fori_loop(0, LOW // 8, apply, 0)
    pick = lax.broadcasted_iota(jnp.int32, (16, 2 * LOW), 1) % 16
    pick = jnp.where(pick == lax.broadcasted_iota(jnp.int32, (16, 2 * LOW), 0), 1.0, 0.0)
    pick = pick.astype(jnp.bfloat16)
    for x in range(0, PIX, 256):
        upper, lower = halves(order_rows[2 * PIX + x : 2 * PIX + x + 256, :])
        out[:, x : x + 256] = lax.dot_general(
            pick, jnp.concatenate([upper, lower], 1), (((1,), (1,)), ((), ())),
            preferred_element_type=jnp.float32,
        )


def combine(data, scale, order_joined, sector_len, channels):
    order_count = order_joined.shape[0]
    digits = order_count // LOW
    cycles, sectors = sector_len.shape
    place = ((order_joined % LOW) * digits + order_joined // LOW) * 8
    first, wave = synthesis_tables(order_count)
    spread = np.zeros((16, 3 * LOW), np.float32)
    for tile, members in enumerate(tile_rows(channels)):
        for i, (c, _) in enumerate(members):
            spread[c, tile * LOW + 16 * i : tile * LOW + 16 * i + 16] = 1.0
    lens = jnp.tile(sector_len.T, (1, LOW // cycles))
    vmem = pl.BlockSpec(memory_space=pltpu.VMEM)
    return pl.pallas_call(
        functools.partial(combine_kernel, channels, digits),
        in_specs=[
            pl.BlockSpec(memory_space=pltpu.SMEM), vmem, vmem, vmem,
            pl.BlockSpec(memory_space=pl.ANY), vmem, vmem,
        ],
        out_specs=vmem,
        out_shape=jax.ShapeDtypeStruct((cycles, PIX), jnp.float32),
        scratch_shapes=[
            pltpu.VMEM(first.shape, jnp.bfloat16),
            pltpu.VMEM((data.shape[1] * data.shape[3] * 8, LOW), jnp.float32),
            pltpu.VMEM((max(order_count * 8, 3 * PIX), LOW), jnp.float32),
            pltpu.VMEM((2 * LOW * 2 * HIGH, LOW), jnp.float32),
            pltpu.VMEM((sectors, TILES, 8, LOW), jnp.float32),
            pltpu.VMEM((TILES, sectors, LOW), jnp.float32),
            pltpu.VMEM((2 * TILES, 8, LOW), jnp.float32),
            pltpu.SemaphoreType.DMA,
        ],
        compiler_params=pltpu.CompilerParams(vmem_limit_bytes=56 << 20),
    )(
        place, data, scale, jnp.asarray(spread, jnp.bfloat16), jnp.asarray(first), jnp.asarray(wave), lens
    )


def permute_kernel(order_ref, rows_in, rows_out):
    def step(slot, carry):
        rows_out[pl.ds(order_ref[slot], 1), :] = rows_in[pl.ds(slot, 1), :]
        return carry

    lax.fori_loop(0, rows_in.shape[0], step, 0, unroll=8)


def sort_orders(orders, rows):
    whole = pl.BlockSpec(rows.shape, lambda i, order: (0, 0))
    return pl.pallas_call(
        permute_kernel,
        grid_spec=pltpu.PrefetchScalarGridSpec(
            num_scalar_prefetch=1, grid=(1,), in_specs=[whole], out_specs=whole
        ),
        out_shape=jax.ShapeDtypeStruct(rows.shape, jnp.float32),
        compiler_params=pltpu.CompilerParams(vmem_limit_bytes=32 << 20),
    )(orders, rows)


def split_dot(left, right):
    left_upper, left_lower = halves(left)
    right_upper, right_lower = halves(right)
    return jnp.dot(
        jnp.concatenate([left_upper, left_upper, left_lower], axis=1),
        jnp.concatenate([right_upper, right_lower, right_upper], axis=0),
        preferred_element_type=jnp.float32,
    )


def member_of(start, end, base, count):
    place = lax.broadcasted_iota(jnp.int32, (start.shape[0], count), 1) + base
    pixel = (place % LOW) * HIGH + place // LOW
    return (pixel >= start) & (pixel < end)


def synthesis_kernel(
    channels, shifts, real_ref, imag_ref, d_ref, e_ref, tc_ref, ts_ref, start_ref, end_ref,
    map_ref, moment_ref, z_ref, m_ref, p_ref,
):
    first = split_dot(d_ref[...], jnp.concatenate([real_ref[0], imag_ref[0]], axis=0))
    cos_turn = tc_ref[...]
    sin_turn = ts_ref[...]
    for c in range(channels):
        real = first[:HIGH, c * LOW : (c + 1) * LOW]
        imag = first[HIGH:, c * LOW : (c + 1) * LOW]
        z_ref[c * HIGH : (c + 1) * HIGH, :LOW] = real * cos_turn - imag * sin_turn
        z_ref[c * HIGH : (c + 1) * HIGH, LOW:] = real * sin_turn + imag * cos_turn
    m_ref[...] = split_dot(z_ref[...], e_ref[...])
    for x2 in range(HIGH):
        map_ref[0, :, x2 * LOW : (x2 + 1) * LOW] = m_ref[pl.ds(x2, channels, stride=HIGH), :]
    p_ref[...] = jnp.zeros_like(p_ref)
    start = start_ref[0]
    end = end_ref[0]
    total = jnp.zeros((2 * shifts * GROUP_ROWS, start.shape[0]), jnp.float32)
    for chunk in range(PIX // CHUNK):
        base = chunk * CHUNK
        values = map_ref[0, :, base : base + CHUNK]
        twice = jnp.concatenate([values, values], axis=0)
        for d in range(shifts):
            p_ref[d * GROUP_ROWS : d * GROUP_ROWS + channels, :] = (
                values * twice[d : d + channels]
            )
        product = p_ref[...]
        upper, lower = halves(product)
        member = jnp.where(member_of(start, end, base, CHUNK), 1.0, 0.0).astype(jnp.bfloat16)
        total += lax.dot_general(
            jnp.concatenate([upper, lower], axis=0), member,
            (((1,), (1,)), ((), ())), preferred_element_type=jnp.float32,
        )
    half = shifts * GROUP_ROWS
    moment_ref[0] = total[:half] + total[half:]


def solve_kernel(channels, cov_ref, len_ref, w_ref):
    scale = 1.0 / len_ref[...].astype(jnp.float32)

    def entry(a, b):
        shift = (b - a) % channels
        row = a
        if shift > channels // 2:
            shift, row = channels - shift, b
        return cov_ref[pl.ds(shift * channels + row, 1), :] * scale

    full = {(a, b): entry(a, b) for a in range(channels) for b in range(a, channels)}
    trace = full[0, 0]
    for a in range(1, channels):
        trace = trace + full[a, a]
    ridge = trace * (RIDGE_FACTOR / channels)
    for a in range(channels):
        full[a, a] = full[a, a] + ridge
    rhs = [jnp.ones_like(scale) for _ in range(channels)]
    inverse = []
    for a in range(channels):
        inverse.append(1.0 / full[a, a])
        for b in range(a + 1, channels):
            factor = full[a, b] * inverse[a]
            for c in range(b, channels):
                full[b, c] = full[b, c] - factor * full[a, c]
            rhs[b] = rhs[b] - factor * rhs[a]
    solved = [None] * channels
    for a in reversed(range(channels)):
        value = rhs[a]
        for b in range(a + 1, channels):
            value = value - full[a, b] * solved[b]
        solved[a] = value * inverse[a]
    total = solved[0]
    for a in range(1, channels):
        total = total + solved[a]
    for a in range(channels):
        w_ref[pl.ds(a, 1), :] = solved[a] / total


def general_combine_kernel(map_ref, w_ref, start_ref, end_ref, out_ref):
    start = start_ref[0]
    end = end_ref[0]
    weights = w_ref[0]
    upper, middle = halves(weights)
    lower = weights - upper.astype(jnp.float32) - middle.astype(jnp.float32)
    pieces = jnp.concatenate([upper, middle, lower.astype(jnp.bfloat16)], axis=1)
    for chunk in range(PIX // CHUNK):
        base = chunk * CHUNK
        member = jnp.where(member_of(start, end, base, CHUNK), 1.0, 0.0).astype(jnp.bfloat16)
        pixel_weights = jnp.dot(
            pieces, jnp.concatenate([member, member, member], axis=0),
            preferred_element_type=jnp.float32,
        )
        out_ref[0, :, base : base + CHUNK] = jnp.sum(
            pixel_weights * map_ref[0, :, base : base + CHUNK], axis=0, keepdims=True
        )


def angles(left, right, period):
    phase = left[:, None] * right[None, :] % period
    turned = phase.astype(jnp.float32) * (TWO_PI / period)
    return jnp.cos(turned), jnp.sin(turned)


def synthesize(real, imag, channels, cycles, sector_len):
    order_count = real.shape[0]
    digits = order_count // LOW
    sectors = sector_len.shape[1]
    weight = jnp.where(lax.iota(jnp.int32, order_count) == 0, 1.0, 2.0).astype(jnp.float32)

    def by_cycle(rows):
        rows = (rows * weight[:, None]).reshape(digits, LOW, channels, cycles)
        return rows.transpose(3, 0, 2, 1).reshape(cycles, digits, channels * LOW)

    x_low = lax.iota(jnp.int32, HIGH)
    m_low = lax.iota(jnp.int32, LOW)
    cos_d, sin_d = angles(x_low, lax.iota(jnp.int32, digits), HIGH)
    first = jnp.concatenate(
        [jnp.concatenate([cos_d, -sin_d], 1), jnp.concatenate([sin_d, cos_d], 1)], 0
    )
    cos_t, sin_t = angles(x_low, m_low, PIX)
    cos_e, sin_e = angles(m_low, m_low, LOW)
    second = jnp.concatenate([cos_e, -sin_e], 0)
    upto = lax.iota(jnp.int32, sectors)
    ends = jnp.sum(jnp.where(upto[:, None] >= upto, sector_len[:, None, :], 0), axis=2)
    starts = (ends - sector_len)[:, :, None]
    ends = ends[:, :, None]
    shifts = channels // 2 + 1
    half = shifts * GROUP_ROWS

    def fixed(array):
        return pl.BlockSpec(array.shape, lambda i: (0, 0))

    def each(rows, columns):
        return pl.BlockSpec((1, rows, columns), lambda i: (i, 0, 0))

    maps, moments = pl.pallas_call(
        functools.partial(synthesis_kernel, channels, shifts),
        grid=(cycles,),
        in_specs=[
            each(digits, channels * LOW), each(digits, channels * LOW), fixed(first), fixed(second), fixed(cos_t),
            fixed(sin_t), each(sectors, 1), each(sectors, 1),
        ],
        out_specs=[each(channels, PIX), each(half, sectors)],
        out_shape=[
            jax.ShapeDtypeStruct((cycles, channels, PIX), jnp.float32),
            jax.ShapeDtypeStruct((cycles, half, sectors), jnp.float32),
        ],
        scratch_shapes=[
            pltpu.VMEM((channels * HIGH, 2 * LOW), jnp.float32),
            pltpu.VMEM((channels * HIGH, LOW), jnp.float32),
            pltpu.VMEM((half, CHUNK), jnp.float32),
        ],
        compiler_params=pltpu.CompilerParams(vmem_limit_bytes=48 << 20),
    )(by_cycle(real), by_cycle(imag), first, second, cos_t, sin_t, starts, ends)
    covariance = moments.reshape(cycles, shifts, GROUP_ROWS, sectors)[:, :, :channels]
    covariance = covariance.transpose(1, 2, 0, 3).reshape(shifts * channels, cycles * sectors)
    weights = pl.pallas_call(
        functools.partial(solve_kernel, channels),
        out_shape=jax.ShapeDtypeStruct((channels, cycles * sectors), jnp.float32),
    )(covariance, sector_len.reshape(1, cycles * sectors))
    weights = weights.reshape(channels, cycles, sectors).transpose(1, 0, 2)
    combined = pl.pallas_call(
        general_combine_kernel,
        grid=(cycles,),
        in_specs=[each(channels, PIX), each(channels, sectors), each(sectors, 1), each(sectors, 1)],
        out_specs=each(1, PIX),
        out_shape=jax.ShapeDtypeStruct((cycles, 1, PIX), jnp.float32),
    )(maps, weights, starts, ends)
    return combined.reshape(cycles, HIGH, LOW).transpose(0, 2, 1).reshape(cycles, PIX)


def general_device(coeffs, legendre, m_order, sector_len):
    slot_count, north_count, degree_count = legendre.shape[1:]
    order_count = m_order.shape[0]
    group_count = lax.axis_size("chan")
    block_count = lax.axis_size("blk")
    device_count = group_count * block_count
    channels = coeffs.shape[0] * group_count
    cycles = sector_len.shape[0]
    first_slot = (lax.axis_index("blk") * group_count + lax.axis_index("chan")) * slot_count
    orders = lax.dynamic_slice_in_dim(m_order, first_slot, slot_count, 0)
    operator = legendre[0]
    degree = order_count - degree_count + lax.iota(jnp.int32, degree_count)
    valid_mask = degree[None, :] >= orders[:, None]
    parity = (degree[None, :] + orders[:, None]) % 2
    keep = jnp.stack([valid_mask & (parity == 0), valid_mask & (parity == 1)])
    zero_value = jnp.zeros((), coeffs.dtype)
    order_joined = (
        m_order.reshape(block_count, group_count, slot_count).transpose(1, 0, 2).reshape(-1)
    )
    received = []
    for p in range(2):
        part = lax.all_to_all(coeffs[:, p], "chan", split_axis=1, concat_axis=0, tiled=True)
        masked = jnp.where(keep[:, None], part[None], zero_value)
        sums = jnp.einsum("ecsl,srl->secr", masked, operator, preferred_element_type=jnp.float32)
        even_sum, odd_sum = sums[:, 0], sums[:, 1]
        spectra = jnp.concatenate([even_sum + odd_sum, even_sum - odd_sum], axis=2)
        spectra = spectra.reshape(slot_count, channels, device_count, cycles)
        spectra = spectra.transpose(2, 0, 1, 3).reshape(
            device_count, slot_count, channels * cycles
        )
        spectra = lax.all_to_all(
            spectra, ("chan", "blk"), split_axis=0, concat_axis=0, tiled=True
        )
        received.append(
            sort_orders(order_joined, spectra.reshape(order_count, channels * cycles))
        )
    return synthesize(received[0], received[1], channels, cycles, sector_len)


def per_device(coeffs, legendre, m_order, sector_len):
    slots, north, _ = legendre.shape[1:]
    groups = lax.axis_size("chan")
    blocks = lax.axis_size("blk")
    channels = coeffs.shape[0] * groups
    cycles = sector_len.shape[0]
    fits = (
        slots % CHUNK_SLOTS == 0 and slots <= LOW and blocks == 8 and cycles * blocks == LOW
        and 2 * north == groups * LOW and channels == 12
    )
    if not fits:
        return general_device(coeffs, legendre, m_order, sector_len)
    first_slot = (lax.axis_index("blk") * groups + lax.axis_index("chan")) * slots
    orders = lax.dynamic_slice_in_dim(m_order, first_slot, slots, 0)
    data, scale = exchange(coeffs, legendre[0], orders, groups, blocks)
    joined = m_order.reshape(blocks, groups, slots).transpose(1, 0, 2).reshape(-1)
    return combine(data, scale, joined, sector_len, channels)


def solution(mesh):
    placed = (
        P("chan", None, "blk", None),
        P("chan", "blk", None, None),
        P(),
        P(("chan", "blk"), None),
    )
    return jax.shard_map(
        per_device, mesh=mesh, in_specs=placed, out_specs=P(("chan", "blk"), None), check_vma=False
    )
```

```python
import functools

import jax
import jax.numpy as jnp
import numpy as np
from jax import lax
from jax.experimental import pallas as pl
from jax.experimental.pallas import tpu as pltpu
from jax.sharding import PartitionSpec as P

PIX = 8192
LOW = 128
HIGH = PIX // LOW
RIDGE_FACTOR = 0.05
TWO_PI = 6.283185307179586
CHUNK = 1024
GROUP_ROWS = 16
MESH = pl.DeviceIdType.MESH
CHUNK_SLOTS = 16
LOAD_SLOTS = 4
LOAD_BUFFERS = 3
AHEAD = 6
CODE_MAX = 32767.0


def block_transpose(values, lane):
    values = list(values)
    for bit in (1, 2, 4):
        upper = (lane // 16) % (2 * bit) >= bit
        for i in range(8):
            if i & bit:
                continue
            a, b = values[i], values[i | bit]
            values[i] = jnp.where(upper, pltpu.roll(b, 16 * bit, 1), a)
            values[i | bit] = jnp.where(upper, b, pltpu.roll(a, LOW - 16 * bit, 1))
    return values


def tile_rows(channels):
    return [
        [(c, 0) for c in range(8)],
        [(c, 1) for c in range(8)],
        [(c, 0) for c in range(8, channels)] + [(c, 1) for c in range(8, channels)],
    ]


def exchange_kernel(
    groups, blocks, coeffs, legendre, order_ref, data_out, scale_out,
    rbuf, lbuf, valid_ref, sign_ref, xs, sp, msg, inverse, scl, tbuf,
    csend, crecv, lsem, dsend, drecv, ssend, srecv,
):
    chunks, _, local_channels, parts, size, degrees = rbuf.shape
    channels = groups * local_channels
    rows = channels * parts
    slots = chunks * size
    tiles = degrees // LOW
    devices = groups * blocks
    g = lax.axis_index("chan")
    b = lax.axis_index("blk")
    me = g * blocks + b

    def peer(i):
        return lax.rem(g + i // blocks, groups), lax.rem(b + i % blocks, blocks)

    barrier = pltpu.get_barrier_semaphore()

    def greet(i, carry):
        pl.semaphore_signal(barrier, inc=1, device_id=peer(i), device_id_type=MESH)
        return carry

    lax.fori_loop(1, devices, greet, 0)

    def load(t):
        return pltpu.make_async_copy(
            legendre.at[pl.ds(t * LOAD_SLOTS, LOAD_SLOTS)],
            lbuf.at[lax.rem(t, LOAD_BUFFERS)], lsem.at[lax.rem(t, LOAD_BUFFERS)],
        )

    for t in range(LOAD_BUFFERS):
        load(t).start()
    degree = lax.broadcasted_iota(jnp.int32, (slots, degrees), 1)
    order = order_ref[...]
    degree = degree + order_ref.shape[0] * devices - degrees
    keep = jnp.where(degree >= order, 1.0, 0.0)
    valid_ref[...] = keep
    sign_ref[...] = keep * (1 - 2 * ((degree + order) % 2)).astype(jnp.float32)
    pl.semaphore_wait(barrier, devices - 1)

    def start_coeffs(j):
        for i in range(1, groups):
            to = lax.rem(g + i, groups)
            pltpu.make_async_remote_copy(
                src_ref=coeffs.at[:, :, pl.ds(to * slots + j * size, size), :],
                dst_ref=rbuf.at[j, g],
                send_sem=csend, recv_sem=crecv.at[j],
                device_id=(to, b), device_id_type=MESH,
            ).start()
        pltpu.make_async_copy(
            coeffs.at[:, :, pl.ds(g * slots + j * size, size), :], rbuf.at[j, g], crecv.at[j]
        ).start()

    for j in range(AHEAD):
        start_coeffs(j)
    lane = lax.broadcasted_iota(jnp.int32, (size, LOW), 1)
    layout = tile_rows(channels)

    def chunk(j, carry):
        pltpu.make_async_copy(rbuf.at[j], rbuf.at[j], crecv.at[j]).wait()
        for q in range(groups):
            for c in range(local_channels):
                for p in range(parts):
                    row = ((q * local_channels + c) * parts + p) * size
                    wide = rbuf[j, q, c, p].astype(jnp.float32)
                    for t in range(tiles):
                        xs[t, row : row + size, :] = wide[:, t * LOW : (t + 1) * LOW]

        def step(u, carry):
            t = j * (size // LOAD_SLOTS) + u
            load(t).wait()
            for v in range(LOAD_SLOTS):
                s = u * LOAD_SLOTS + v
                x = jnp.concatenate(
                    [xs[i, pl.ds(s, rows, stride=size), :] for i in range(tiles)], axis=1
                )
                at = pl.ds(j * size + s, 1)
                both = jnp.concatenate([x * valid_ref[at, :], x * sign_ref[at, :]], axis=0)
                sums = lax.dot_general(
                    both.astype(jnp.bfloat16), lbuf[lax.rem(t, LOAD_BUFFERS), v],
                    (((1,), (1,)), ((), ())), preferred_element_type=jnp.float32,
                )
                for i in range(sp.shape[0]):
                    sp[i, pl.ds(s, 2 * rows, stride=size), :] = sums[:, i * LOW : (i + 1) * LOW]

            @pl.when(t + LOAD_BUFFERS < slots // LOAD_SLOTS)
            def _():
                load(t + LOAD_BUFFERS).start()

            return carry

        lax.fori_loop(0, size // LOAD_SLOTS, step, 0)

        def piece(half, side, c, p):
            row = (half * rows + c * parts + p) * size
            return sp[side, row : row + size, :]

        scales = jnp.zeros((size, LOW), jnp.float32)
        for c in range(channels):
            top = jnp.abs(piece(0, 0, c, 0))
            for half in range(2):
                for side in range(sp.shape[0]):
                    for p in range(parts):
                        top = jnp.maximum(top, jnp.abs(piece(half, side, c, p)))
            top = jnp.maximum(jnp.max(top, axis=1, keepdims=True), 1e-30)
            unit = (top * (1.0078125 / CODE_MAX)).astype(jnp.bfloat16).astype(jnp.float32)
            inverse[c] = jnp.broadcast_to(1.0 / unit, (size, LOW))
            scales = jnp.where(lane == c, unit, scales)
        scl[pl.ds(pl.multiple_of(j * size, size), size), :] = scales
        for half in range(2):
            for side in range(sp.shape[0]):
                first = (half * sp.shape[0] + side) * blocks
                for tile, members in enumerate(layout):
                    values = block_transpose(
                        [piece(half, side, c, p) * inverse[c] for c, p in members], lane
                    )
                    for k in range(blocks):
                        msg[j, first + k, tile] = jnp.round(values[k]).astype(jnp.int16)

        def send(i, carry):
            to = peer(i)
            pltpu.make_async_remote_copy(
                src_ref=msg.at[j, to[0] * blocks + to[1]], dst_ref=data_out.at[me, j],
                send_sem=dsend, recv_sem=drecv, device_id=to, device_id_type=MESH,
            ).start()
            return carry

        lax.fori_loop(1, devices, send, 0)
        pltpu.make_async_copy(msg.at[j, me], data_out.at[me, j], drecv).start()

        @pl.when(j + AHEAD < chunks)
        def _():
            start_coeffs(j + AHEAD)

        return carry

    lax.fori_loop(0, chunks, chunk, 0)
    turned = jnp.transpose(scl[...])
    tbuf[...] = turned[: tbuf.shape[0]].astype(jnp.bfloat16)

    def send_scale(i, carry):
        pltpu.make_async_remote_copy(
            src_ref=tbuf, dst_ref=scale_out.at[me],
            send_sem=ssend, recv_sem=srecv, device_id=peer(i), device_id_type=MESH,
        ).start()
        return carry

    lax.fori_loop(1, devices, send_scale, 0)
    pltpu.make_async_copy(tbuf, scale_out.at[me], srecv).start()

    def settle(ref, sem):
        pltpu.make_async_copy(ref, ref, sem).wait()

    settle(rbuf.at[:, pl.ds(0, groups - 1)], csend)
    settle(msg.at[:, pl.ds(0, devices - 1)], dsend)
    settle(scale_out.at[pl.ds(0, devices - 1)], ssend)
    settle(data_out, drecv)
    settle(scale_out, srecv)


def exchange(coeffs, operator, orders, groups, blocks):
    local_channels, parts, _, degrees = coeffs.shape
    slots, north, _ = operator.shape
    channels = groups * local_channels
    devices = groups * blocks
    size = CHUNK_SLOTS
    chunks = slots // size
    rows = channels * parts
    sides = north // LOW
    anywhere = pl.BlockSpec(memory_space=pl.ANY)
    dma = pltpu.SemaphoreType.DMA
    return pl.pallas_call(
        functools.partial(exchange_kernel, groups, blocks),
        in_specs=[anywhere, anywhere, pl.BlockSpec(memory_space=pltpu.VMEM)],
        out_specs=[anywhere, anywhere],
        out_shape=[
            jax.ShapeDtypeStruct((devices, chunks, 3, size, LOW), jnp.int16),
            jax.ShapeDtypeStruct((devices, 16, LOW), jnp.bfloat16),
        ],
        scratch_shapes=[
            pltpu.VMEM((chunks, groups, local_channels, parts, size, degrees), jnp.bfloat16),
            pltpu.VMEM((LOAD_BUFFERS, LOAD_SLOTS, north, degrees), jnp.bfloat16),
            pltpu.VMEM((slots, degrees), jnp.float32),
            pltpu.VMEM((slots, degrees), jnp.float32),
            pltpu.VMEM((degrees // LOW, rows * size, LOW), jnp.float32),
            pltpu.VMEM((sides, 2 * rows * size, LOW), jnp.float32),
            pltpu.VMEM((chunks, devices, 3, size, LOW), jnp.int16),
            pltpu.VMEM((channels, size, LOW), jnp.float32),
            pltpu.VMEM((LOW, LOW), jnp.float32),
            pltpu.VMEM((16, LOW), jnp.bfloat16),
            dma, dma((chunks,)), dma((LOAD_BUFFERS,)), dma, dma, dma, dma,
        ],
        compiler_params=pltpu.CompilerParams(
            collective_id=0, has_side_effects=True, vmem_limit_bytes=52 << 20
        ),
    )(coeffs, operator, orders[:, None])


def halves(value):
    upper = value.astype(jnp.bfloat16)
    return upper, (value - upper.astype(jnp.float32)).astype(jnp.bfloat16)


def synthesis_tables(order_count):
    digits = order_count // LOW
    order = np.arange(LOW)[:, None, None] + LOW * np.arange(digits)[None, None, :]
    angle = order * np.arange(HIGH)[None, :, None] % PIX * (2.0 * np.pi / PIX)
    weight = np.where(order == 0, 1.0, 2.0)
    cos, sin = weight * np.cos(angle), weight * np.sin(angle)
    turn = np.stack([np.concatenate([cos, -sin], 2), np.concatenate([sin, cos], 2)], 2)
    turn = turn.reshape(LOW, 2 * HIGH, 2 * digits).astype(np.float32)
    turn_upper = turn.astype(jnp.bfloat16)
    turn_lower = (turn - turn_upper.astype(np.float32)).astype(jnp.bfloat16)
    first = np.concatenate([turn_upper, turn_upper, turn_lower], 2)
    angle = np.arange(LOW)[:, None] * np.arange(LOW)[None, :] % LOW * (2.0 * np.pi / LOW)
    wave = np.concatenate([np.cos(angle), -np.sin(angle)], 1).astype(np.float32)
    wave_upper = wave.astype(jnp.bfloat16)
    wave_lower = (wave - wave_upper.astype(np.float32)).astype(jnp.bfloat16)
    return first, np.concatenate([wave_upper, wave_lower], 0)


def pair_place(a, b):
    if b < 8:
        shift = b - a
        return (shift, a) if shift <= 4 else (8 - shift, b)
    if a < 8:
        return 5 + (b - 8 - a) % 4, a
    a, b = a - 8, b - 8
    shift = b - a
    if shift == 2:
        return 10, a
    return 9, {0: a, 1: 4 + a, 3: 4 + b}[shift]


TILES = 11
ROOM = LOW + 8
SPACE = HIGH + 8


def combine_kernel(
    channels, digits, place_ref, data, scale, spread, first_any, wave, lens, out,
    first, spare, order_rows, turned, sums, cov, heads, first_sem,
):
    sources, chunks, _, size, _ = data.shape
    slots = chunks * size
    fetch = pltpu.make_async_copy(first_any, first, first_sem)
    fetch.start()

    def gather(src, carry):
        unit = lax.dot_general(
            scale[src], spread[...], (((0,), (0,)), ((), ())), preferred_element_type=jnp.float32
        )
        for j in range(chunks):
            for t in range(3):
                value = data[src, j, t].astype(jnp.float32)
                value = value * unit[j * size : (j + 1) * size, t * LOW : (t + 1) * LOW]
                spare[pl.ds(j * size * 8 + t, size, stride=8), :] = value
        base = src * slots

        def move(s, carry):
            to = pl.multiple_of(place_ref[base + s], 8)
            order_rows[pl.ds(to, 8), :] = spare[pl.ds(pl.multiple_of(s * 8, 8), 8), :]
            return carry

        return lax.fori_loop(0, slots, move, carry, unroll=16)

    lax.fori_loop(0, sources, gather, 0)
    fetch.wait()
    lane_d = lax.broadcasted_iota(jnp.int32, (digits, LOW), 1)
    wide = ROOM * 2 * HIGH

    def turn(l, carry):
        t0, t1, t2 = (
            order_rows[pl.ds(l * (digits * 8) + t, digits, stride=8), :] for t in range(3)
        )
        t3 = pltpu.roll(t2, LOW // 2, 1)
        real = jnp.where(lane_d < LOW // 2, t2, t3)
        imag = jnp.where(lane_d < LOW // 2, t3, t2)
        x = jnp.concatenate(
            [jnp.concatenate([t0, real], 1), jnp.concatenate([t1, imag], 1)], 0
        )
        upper, lower = halves(x)
        y = jnp.dot(
            first[l], jnp.concatenate([upper, lower, upper], 0), preferred_element_type=jnp.float32
        )
        turned[pl.ds(l, 2 * HIGH, stride=ROOM), :] = y[:, :LOW]
        turned[pl.ds(wide + l, 2 * HIGH, stride=ROOM), :] = y[:, LOW:]
        return carry

    lax.fori_loop(0, LOW, turn, 0, unroll=16)

    def spin(x, carry):
        def part(i):
            at = pl.multiple_of((2 * x + i) * ROOM, 8)
            return jnp.concatenate(
                [turned[pl.ds(at, LOW), :], turned[pl.ds(wide + at, LOW), :]], 1
            )

        upper, lower = halves(jnp.concatenate([part(0), part(1)], 0))
        main = jnp.dot(wave[...], upper, preferred_element_type=jnp.float32)
        rest = jnp.dot(wave[:LOW], lower, preferred_element_type=jnp.float32)
        value = main[:LOW] + main[LOW:] + rest
        order_rows[pl.ds(pl.multiple_of(x * LOW, LOW), LOW), :] = value[:, :LOW]
        order_rows[pl.ds(pl.multiple_of(PIX + x * LOW, LOW), LOW), :] = value[:, LOW:]
        return carry

    lax.fori_loop(0, HIGH, spin, 0, unroll=8)

    sectors = lens.shape[0]
    length = lens[...]
    ends = []
    for k in range(sectors):
        ends.append(length[k : k + 1] + ends[-1] if k else length[:1])
    lane = lax.broadcasted_iota(jnp.int32, (8, LOW), 1)
    sub = lax.broadcasted_iota(jnp.int32, (8, LOW), 0)

    def block(j):
        begin = (j * 8 + sub) * HIGH
        sector = jnp.zeros((8, LOW), jnp.int32)
        after = jnp.full((8, LOW), 2 * PIX, jnp.int32)
        for k in range(sectors):
            past = ends[k] <= begin
            sector = sector + jnp.where(past, 1, 0)
            after = jnp.minimum(after, jnp.where(past, 2 * PIX, ends[k]))
        return sector, after - begin

    def pair(j, x):
        at = pl.multiple_of(x * LOW + j * 8, 8)
        return order_rows[pl.ds(at, 8), :], order_rows[pl.ds(PIX + at, 8), :]

    sums[...] = jnp.zeros_like(sums)

    def moments(j, carry):
        sector, limit = block(j)

        def add(x, acc):
            a, b = pair(j, x)
            inside = limit > x
            ah = jnp.where(inside, a, 0.0)
            bh = jnp.where(inside, b, 0.0)
            b1, b2, b3 = (pltpu.roll(b, LOW - 16 * d, 1) for d in (1, 2, 3))
            with_a = [a] + [pltpu.roll(a, LOW - 16 * d, 1) for d in range(1, 5)] + [b, b1, b2, b3]
            with_b = [jnp.where(lane < LOW // 2, b, b1), b2]
            full = [acc[i] + a * v for i, v in enumerate(with_a)]
            full += [acc[9 + i] + b * v for i, v in enumerate(with_b)]
            head = [acc[TILES + i] + ah * v for i, v in enumerate(with_a)]
            head += [acc[TILES + 9 + i] + bh * v for i, v in enumerate(with_b)]
            return tuple(full + head)

        zero = jnp.zeros((8, LOW), jnp.float32)
        acc = lax.fori_loop(0, HIGH, add, (zero,) * (2 * TILES), unroll=32)
        tails = [acc[i] - acc[TILES + i] for i in range(TILES)]
        for i in range(TILES):
            heads[i] = acc[TILES + i]
            heads[TILES + i] = tails[i]

        def assign(k, carry):
            here = sector == k
            there = sector + 1 == k
            for i in range(TILES):
                sums[k, i] += jnp.where(here, heads[i], 0.0) + jnp.where(there, heads[TILES + i], 0.0)
            return carry

        return lax.fori_loop(0, sectors, assign, carry)

    lax.fori_loop(0, LOW // 8, moments, 0)

    def collect(k, carry):
        for i in range(TILES):
            cov[i, pl.ds(k, 1), :] = jnp.sum(sums[k, i], axis=0, keepdims=True)
        return carry

    lax.fori_loop(0, sectors, collect, 0)
    share = 1.0 / length.astype(jnp.float32)

    def entry(a, b):
        tile, group = pair_place(a, b)
        value = cov[tile] * share
        return pltpu.roll(value, LOW - 16 * group, 1) if group else value

    full = {(a, b): entry(a, b) for a in range(channels) for b in range(a, channels)}
    trace = full[0, 0]
    for a in range(1, channels):
        trace = trace + full[a, a]
    ridge = trace * (RIDGE_FACTOR / channels)
    for a in range(channels):
        full[a, a] = full[a, a] + ridge
    rhs = [jnp.ones_like(ridge) for _ in range(channels)]
    inverse = []
    for a in range(channels):
        inverse.append(1.0 / full[a, a])
        for b in range(a + 1, channels):
            factor = full[a, b] * inverse[a]
            for c in range(b, channels):
                full[b, c] = full[b, c] - factor * full[a, c]
            rhs[b] = rhs[b] - factor * rhs[a]
    solved = [None] * channels
    for a in reversed(range(channels)):
        value = rhs[a]
        for b in range(a + 1, channels):
            value = value - full[a, b] * solved[b]
        solved[a] = value * inverse[a]
    total = solved[0]
    for a in range(1, channels):
        total = total + solved[a]
    near = jnp.zeros_like(total)
    far = jnp.zeros_like(total)
    group = lax.broadcasted_iota(jnp.int32, total.shape, 1) // 16
    for a in range(channels):
        weight = solved[a] / total
        place = a % 8
        moved = pltpu.roll(weight, 16 * place, 1) if place else weight
        if a < 8:
            near = jnp.where(group == place, moved, near)
        else:
            far = jnp.where(group == place, moved, far)
    cov[0] = near
    cov[1] = far

    def apply(j, carry):
        sector, limit = block(j)
        picked = [jnp.zeros((8, LOW), jnp.float32) for _ in range(4)]
        for k in range(sectors):
            near_k = cov[0, k : k + 1, :]
            far_k = cov[1, k : k + 1, :]
            here = sector == k
            there = sector + 1 == k
            picked[0] = jnp.where(here, near_k, picked[0])
            picked[1] = jnp.where(here, far_k, picked[1])
            picked[2] = jnp.where(there, near_k, picked[2])
            picked[3] = jnp.where(there, far_k, picked[3])

        def weigh(x, carry):
            a, b = pair(j, x)
            inside = limit > x
            value = jnp.where(inside, picked[0], picked[2]) * a
            value = value + jnp.where(inside, picked[1], picked[3]) * b
            order_rows[pl.ds(2 * PIX + j * 8 * SPACE + x, 8, stride=SPACE), :] = value
            return carry

        return lax.fori_loop(0, HIGH, weigh, carry, unroll=8)

    lax.fori_loop(0, LOW // 8, apply, 0)
    pick = lax.broadcasted_iota(jnp.int32, (16, 2 * LOW), 1) % 16
    pick = jnp.where(pick == lax.broadcasted_iota(jnp.int32, (16, 2 * LOW), 0), 1.0, 0.0)
    pick = pick.astype(jnp.bfloat16)
    for x in range(0, PIX, 256):
        upper, lower = halves(
            jnp.concatenate(
                [
                    order_rows[2 * PIX + y * SPACE : 2 * PIX + y * SPACE + HIGH, :]
                    for y in range(x // HIGH, (x + 256) // HIGH)
                ],
                0,
            )
        )
        out[:, x : x + 256] = lax.dot_general(
            pick, jnp.concatenate([upper, lower], 1), (((1,), (1,)), ((), ())),
            preferred_element_type=jnp.float32,
        )


def combine(data, scale, order_joined, sector_len, channels):
    order_count = order_joined.shape[0]
    digits = order_count // LOW
    cycles, sectors = sector_len.shape
    place = ((order_joined % LOW) * digits + order_joined // LOW) * 8
    first, wave = synthesis_tables(order_count)
    spread = np.zeros((16, 3 * LOW), np.float32)
    for tile, members in enumerate(tile_rows(channels)):
        for i, (c, _) in enumerate(members):
            spread[c, tile * LOW + 16 * i : tile * LOW + 16 * i + 16] = 1.0
    lens = jnp.tile(sector_len.T, (1, LOW // cycles))
    vmem = pl.BlockSpec(memory_space=pltpu.VMEM)
    return pl.pallas_call(
        functools.partial(combine_kernel, channels, digits),
        in_specs=[
            pl.BlockSpec(memory_space=pltpu.SMEM), vmem, vmem, vmem,
            pl.BlockSpec(memory_space=pl.ANY), vmem, vmem,
        ],
        out_specs=vmem,
        out_shape=jax.ShapeDtypeStruct((cycles, PIX), jnp.float32),
        scratch_shapes=[
            pltpu.VMEM(first.shape, jnp.bfloat16),
            pltpu.VMEM((data.shape[1] * data.shape[3] * 8, LOW), jnp.float32),
            pltpu.VMEM((max(order_count * 8, 2 * PIX + LOW * SPACE), LOW), jnp.float32),
            pltpu.VMEM((2 * ROOM * 2 * HIGH, LOW), jnp.float32),
            pltpu.VMEM((sectors, TILES, 8, LOW), jnp.float32),
            pltpu.VMEM((TILES, sectors, LOW), jnp.float32),
            pltpu.VMEM((2 * TILES, 8, LOW), jnp.float32),
            pltpu.SemaphoreType.DMA,
        ],
        compiler_params=pltpu.CompilerParams(vmem_limit_bytes=56 << 20),
    )(
        place, data, scale, jnp.asarray(spread, jnp.bfloat16), jnp.asarray(first), jnp.asarray(wave), lens
    )


def permute_kernel(order_ref, rows_in, rows_out):
    def step(slot, carry):
        rows_out[pl.ds(order_ref[slot], 1), :] = rows_in[pl.ds(slot, 1), :]
        return carry

    lax.fori_loop(0, rows_in.shape[0], step, 0, unroll=8)


def sort_orders(orders, rows):
    whole = pl.BlockSpec(rows.shape, lambda i, order: (0, 0))
    return pl.pallas_call(
        permute_kernel,
        grid_spec=pltpu.PrefetchScalarGridSpec(
            num_scalar_prefetch=1, grid=(1,), in_specs=[whole], out_specs=whole
        ),
        out_shape=jax.ShapeDtypeStruct(rows.shape, jnp.float32),
        compiler_params=pltpu.CompilerParams(vmem_limit_bytes=32 << 20),
    )(orders, rows)


def split_dot(left, right):
    left_upper, left_lower = halves(left)
    right_upper, right_lower = halves(right)
    return jnp.dot(
        jnp.concatenate([left_upper, left_upper, left_lower], axis=1),
        jnp.concatenate([right_upper, right_lower, right_upper], axis=0),
        preferred_element_type=jnp.float32,
    )


def member_of(start, end, base, count):
    place = lax.broadcasted_iota(jnp.int32, (start.shape[0], count), 1) + base
    pixel = (place % LOW) * HIGH + place // LOW
    return (pixel >= start) & (pixel < end)


def synthesis_kernel(
    channels, shifts, real_ref, imag_ref, d_ref, e_ref, tc_ref, ts_ref, start_ref, end_ref,
    map_ref, moment_ref, z_ref, m_ref, p_ref,
):
    first = split_dot(d_ref[...], jnp.concatenate([real_ref[0], imag_ref[0]], axis=0))
    cos_turn = tc_ref[...]
    sin_turn = ts_ref[...]
    for c in range(channels):
        real = first[:HIGH, c * LOW : (c + 1) * LOW]
        imag = first[HIGH:, c * LOW : (c + 1) * LOW]
        z_ref[c * HIGH : (c + 1) * HIGH, :LOW] = real * cos_turn - imag * sin_turn
        z_ref[c * HIGH : (c + 1) * HIGH, LOW:] = real * sin_turn + imag * cos_turn
    m_ref[...] = split_dot(z_ref[...], e_ref[...])
    for x2 in range(HIGH):
        map_ref[0, :, x2 * LOW : (x2 + 1) * LOW] = m_ref[pl.ds(x2, channels, stride=HIGH), :]
    p_ref[...] = jnp.zeros_like(p_ref)
    start = start_ref[0]
    end = end_ref[0]
    total = jnp.zeros((2 * shifts * GROUP_ROWS, start.shape[0]), jnp.float32)
    for chunk in range(PIX // CHUNK):
        base = chunk * CHUNK
        values = map_ref[0, :, base : base + CHUNK]
        twice = jnp.concatenate([values, values], axis=0)
        for d in range(shifts):
            p_ref[d * GROUP_ROWS : d * GROUP_ROWS + channels, :] = (
                values * twice[d : d + channels]
            )
        product = p_ref[...]
        upper, lower = halves(product)
        member = jnp.where(member_of(start, end, base, CHUNK), 1.0, 0.0).astype(jnp.bfloat16)
        total += lax.dot_general(
            jnp.concatenate([upper, lower], axis=0), member,
            (((1,), (1,)), ((), ())), preferred_element_type=jnp.float32,
        )
    half = shifts * GROUP_ROWS
    moment_ref[0] = total[:half] + total[half:]


def solve_kernel(channels, cov_ref, len_ref, w_ref):
    scale = 1.0 / len_ref[...].astype(jnp.float32)

    def entry(a, b):
        shift = (b - a) % channels
        row = a
        if shift > channels // 2:
            shift, row = channels - shift, b
        return cov_ref[pl.ds(shift * channels + row, 1), :] * scale

    full = {(a, b): entry(a, b) for a in range(channels) for b in range(a, channels)}
    trace = full[0, 0]
    for a in range(1, channels):
        trace = trace + full[a, a]
    ridge = trace * (RIDGE_FACTOR / channels)
    for a in range(channels):
        full[a, a] = full[a, a] + ridge
    rhs = [jnp.ones_like(scale) for _ in range(channels)]
    inverse = []
    for a in range(channels):
        inverse.append(1.0 / full[a, a])
        for b in range(a + 1, channels):
            factor = full[a, b] * inverse[a]
            for c in range(b, channels):
                full[b, c] = full[b, c] - factor * full[a, c]
            rhs[b] = rhs[b] - factor * rhs[a]
    solved = [None] * channels
    for a in reversed(range(channels)):
        value = rhs[a]
        for b in range(a + 1, channels):
            value = value - full[a, b] * solved[b]
        solved[a] = value * inverse[a]
    total = solved[0]
    for a in range(1, channels):
        total = total + solved[a]
    for a in range(channels):
        w_ref[pl.ds(a, 1), :] = solved[a] / total


def general_combine_kernel(map_ref, w_ref, start_ref, end_ref, out_ref):
    start = start_ref[0]
    end = end_ref[0]
    weights = w_ref[0]
    upper, middle = halves(weights)
    lower = weights - upper.astype(jnp.float32) - middle.astype(jnp.float32)
    pieces = jnp.concatenate([upper, middle, lower.astype(jnp.bfloat16)], axis=1)
    for chunk in range(PIX // CHUNK):
        base = chunk * CHUNK
        member = jnp.where(member_of(start, end, base, CHUNK), 1.0, 0.0).astype(jnp.bfloat16)
        pixel_weights = jnp.dot(
            pieces, jnp.concatenate([member, member, member], axis=0),
            preferred_element_type=jnp.float32,
        )
        out_ref[0, :, base : base + CHUNK] = jnp.sum(
            pixel_weights * map_ref[0, :, base : base + CHUNK], axis=0, keepdims=True
        )


def angles(left, right, period):
    phase = left[:, None] * right[None, :] % period
    turned = phase.astype(jnp.float32) * (TWO_PI / period)
    return jnp.cos(turned), jnp.sin(turned)


def synthesize(real, imag, channels, cycles, sector_len):
    order_count = real.shape[0]
    digits = order_count // LOW
    sectors = sector_len.shape[1]
    weight = jnp.where(lax.iota(jnp.int32, order_count) == 0, 1.0, 2.0).astype(jnp.float32)

    def by_cycle(rows):
        rows = (rows * weight[:, None]).reshape(digits, LOW, channels, cycles)
        return rows.transpose(3, 0, 2, 1).reshape(cycles, digits, channels * LOW)

    x_low = lax.iota(jnp.int32, HIGH)
    m_low = lax.iota(jnp.int32, LOW)
    cos_d, sin_d = angles(x_low, lax.iota(jnp.int32, digits), HIGH)
    first = jnp.concatenate(
        [jnp.concatenate([cos_d, -sin_d], 1), jnp.concatenate([sin_d, cos_d], 1)], 0
    )
    cos_t, sin_t = angles(x_low, m_low, PIX)
    cos_e, sin_e = angles(m_low, m_low, LOW)
    second = jnp.concatenate([cos_e, -sin_e], 0)
    upto = lax.iota(jnp.int32, sectors)
    ends = jnp.sum(jnp.where(upto[:, None] >= upto, sector_len[:, None, :], 0), axis=2)
    starts = (ends - sector_len)[:, :, None]
    ends = ends[:, :, None]
    shifts = channels // 2 + 1
    half = shifts * GROUP_ROWS

    def fixed(array):
        return pl.BlockSpec(array.shape, lambda i: (0, 0))

    def each(rows, columns):
        return pl.BlockSpec((1, rows, columns), lambda i: (i, 0, 0))

    maps, moments = pl.pallas_call(
        functools.partial(synthesis_kernel, channels, shifts),
        grid=(cycles,),
        in_specs=[
            each(digits, channels * LOW), each(digits, channels * LOW), fixed(first), fixed(second), fixed(cos_t),
            fixed(sin_t), each(sectors, 1), each(sectors, 1),
        ],
        out_specs=[each(channels, PIX), each(half, sectors)],
        out_shape=[
            jax.ShapeDtypeStruct((cycles, channels, PIX), jnp.float32),
            jax.ShapeDtypeStruct((cycles, half, sectors), jnp.float32),
        ],
        scratch_shapes=[
            pltpu.VMEM((channels * HIGH, 2 * LOW), jnp.float32),
            pltpu.VMEM((channels * HIGH, LOW), jnp.float32),
            pltpu.VMEM((half, CHUNK), jnp.float32),
        ],
        compiler_params=pltpu.CompilerParams(vmem_limit_bytes=48 << 20),
    )(by_cycle(real), by_cycle(imag), first, second, cos_t, sin_t, starts, ends)
    covariance = moments.reshape(cycles, shifts, GROUP_ROWS, sectors)[:, :, :channels]
    covariance = covariance.transpose(1, 2, 0, 3).reshape(shifts * channels, cycles * sectors)
    weights = pl.pallas_call(
        functools.partial(solve_kernel, channels),
        out_shape=jax.ShapeDtypeStruct((channels, cycles * sectors), jnp.float32),
    )(covariance, sector_len.reshape(1, cycles * sectors))
    weights = weights.reshape(channels, cycles, sectors).transpose(1, 0, 2)
    combined = pl.pallas_call(
        general_combine_kernel,
        grid=(cycles,),
        in_specs=[each(channels, PIX), each(channels, sectors), each(sectors, 1), each(sectors, 1)],
        out_specs=each(1, PIX),
        out_shape=jax.ShapeDtypeStruct((cycles, 1, PIX), jnp.float32),
    )(maps, weights, starts, ends)
    return combined.reshape(cycles, HIGH, LOW).transpose(0, 2, 1).reshape(cycles, PIX)


def general_device(coeffs, legendre, m_order, sector_len):
    slot_count, north_count, degree_count = legendre.shape[1:]
    order_count = m_order.shape[0]
    group_count = lax.axis_size("chan")
    block_count = lax.axis_size("blk")
    device_count = group_count * block_count
    channels = coeffs.shape[0] * group_count
    cycles = sector_len.shape[0]
    first_slot = (lax.axis_index("blk") * group_count + lax.axis_index("chan")) * slot_count
    orders = lax.dynamic_slice_in_dim(m_order, first_slot, slot_count, 0)
    operator = legendre[0]
    degree = order_count - degree_count + lax.iota(jnp.int32, degree_count)
    valid_mask = degree[None, :] >= orders[:, None]
    parity = (degree[None, :] + orders[:, None]) % 2
    keep = jnp.stack([valid_mask & (parity == 0), valid_mask & (parity == 1)])
    zero_value = jnp.zeros((), coeffs.dtype)
    order_joined = (
        m_order.reshape(block_count, group_count, slot_count).transpose(1, 0, 2).reshape(-1)
    )
    received = []
    for p in range(2):
        part = lax.all_to_all(coeffs[:, p], "chan", split_axis=1, concat_axis=0, tiled=True)
        masked = jnp.where(keep[:, None], part[None], zero_value)
        sums = jnp.einsum("ecsl,srl->secr", masked, operator, preferred_element_type=jnp.float32)
        even_sum, odd_sum = sums[:, 0], sums[:, 1]
        spectra = jnp.concatenate([even_sum + odd_sum, even_sum - odd_sum], axis=2)
        spectra = spectra.reshape(slot_count, channels, device_count, cycles)
        spectra = spectra.transpose(2, 0, 1, 3).reshape(
            device_count, slot_count, channels * cycles
        )
        spectra = lax.all_to_all(
            spectra, ("chan", "blk"), split_axis=0, concat_axis=0, tiled=True
        )
        received.append(
            sort_orders(order_joined, spectra.reshape(order_count, channels * cycles))
        )
    return synthesize(received[0], received[1], channels, cycles, sector_len)


def per_device(coeffs, legendre, m_order, sector_len):
    slots, north, _ = legendre.shape[1:]
    groups = lax.axis_size("chan")
    blocks = lax.axis_size("blk")
    channels = coeffs.shape[0] * groups
    cycles = sector_len.shape[0]
    fits = (
        slots % CHUNK_SLOTS == 0 and slots <= LOW and blocks == 8 and cycles * blocks == LOW
        and 2 * north == groups * LOW and channels == 12
    )
    if not fits:
        return general_device(coeffs, legendre, m_order, sector_len)
    first_slot = (lax.axis_index("blk") * groups + lax.axis_index("chan")) * slots
    orders = lax.dynamic_slice_in_dim(m_order, first_slot, slots, 0)
    data, scale = exchange(coeffs, legendre[0], orders, groups, blocks)
    joined = m_order.reshape(blocks, groups, slots).transpose(1, 0, 2).reshape(-1)
    return combine(data, scale, joined, sector_len, channels)


def solution(mesh):
    placed = (
        P("chan", None, "blk", None),
        P("chan", "blk", None, None),
        P(),
        P(("chan", "blk"), None),
    )
    return jax.shard_map(
        per_device, mesh=mesh, in_specs=placed, out_specs=P(("chan", "blk"), None), check_vma=False
    )
```

```python
import functools

import jax
import jax.numpy as jnp
import numpy as np
from jax import lax
from jax.experimental import pallas as pl
from jax.experimental.pallas import tpu as pltpu
from jax.sharding import PartitionSpec as P

PIX = 8192
LOW = 128
HIGH = PIX // LOW
RIDGE_FACTOR = 0.05
TWO_PI = 6.283185307179586
CHUNK = 1024
GROUP_ROWS = 16
MESH = pl.DeviceIdType.MESH
CHUNK_SLOTS = 16
LOAD_SLOTS = 4
LOAD_BUFFERS = 3
CODE_MAX = 32767.0


def block_transpose(values, lane):
    values = list(values)
    for bit in (1, 2, 4):
        upper = (lane // 16) % (2 * bit) >= bit
        for i in range(8):
            if i & bit:
                continue
            a, b = values[i], values[i | bit]
            values[i] = jnp.where(upper, pltpu.roll(b, 16 * bit, 1), a)
            values[i | bit] = jnp.where(upper, b, pltpu.roll(a, LOW - 16 * bit, 1))
    return values


def tile_rows(channels):
    return [
        [(c, 0) for c in range(8)],
        [(c, 1) for c in range(8)],
        [(c, 0) for c in range(8, channels)] + [(c, 1) for c in range(8, channels)],
    ]


def exchange_kernel(
    groups, blocks, order_ref, coeffs, legendre, data_out, scale_out,
    rbuf, lbuf, valid_ref, sign_ref, xs, sp, msg, inverse, scl,
    csend, crecv, lsem, dsend, drecv, ssend, srecv,
):
    chunks, _, local_channels, parts, size, degrees = rbuf.shape
    channels = groups * local_channels
    rows = channels * parts
    slots = chunks * size
    tiles = degrees // LOW
    devices = groups * blocks
    g = lax.axis_index("chan")
    b = lax.axis_index("blk")
    me = g * blocks + b

    half_blocks = blocks // 2
    half_devices = devices // 2
    my_half = b // half_blocks

    def near(i):
        at = lax.rem(b + i // groups, half_blocks)
        return lax.rem(g + i % groups, groups), my_half * half_blocks + at

    def far(i):
        at = lax.rem(b + i // groups, half_blocks)
        return lax.rem(g + i % groups, groups), (1 - my_half) * half_blocks + at

    barrier = pltpu.get_barrier_semaphore()

    def to_all(act):
        def to_far(i, carry):
            act(far(i))
            return carry

        def to_near(i, carry):
            act(near(i))
            return carry

        lax.fori_loop(0, half_devices, to_far, 0)
        lax.fori_loop(1, half_devices, to_near, 0)

    def greet(to):
        pl.semaphore_signal(barrier, inc=1, device_id=to, device_id_type=MESH)

    to_all(greet)

    def load(t):
        return pltpu.make_async_copy(
            legendre.at[pl.ds(t * LOAD_SLOTS, LOAD_SLOTS)],
            lbuf.at[lax.rem(t, LOAD_BUFFERS)], lsem.at[lax.rem(t, LOAD_BUFFERS)],
        )

    for t in range(LOAD_BUFFERS):
        load(t).start()
    pl.semaphore_wait(barrier, devices - 1)

    def start_coeffs(j):
        for i in range(1, groups):
            to = lax.rem(g + i, groups)
            pltpu.make_async_remote_copy(
                src_ref=coeffs.at[:, :, pl.ds(to * slots + j * size, size), :],
                dst_ref=rbuf.at[j, g],
                send_sem=csend, recv_sem=crecv.at[j],
                device_id=(to, b), device_id_type=MESH,
            ).start()
        pltpu.make_async_copy(
            coeffs.at[:, :, pl.ds(g * slots + j * size, size), :], rbuf.at[j, g], crecv.at[j]
        ).start()

    for j in range(chunks):
        start_coeffs(j)
    degree = lax.broadcasted_iota(jnp.int32, (1, degrees), 1) + order_ref.shape[0] - degrees
    first_slot = (b * groups + g) * slots

    def masks(s, carry):
        order = order_ref[first_slot + s]
        keep = jnp.where(degree >= order, 1.0, 0.0)
        at = pl.ds(s, 1)
        valid_ref[at, :] = keep
        sign_ref[at, :] = jnp.where((degree + order) % 2 == 0, keep, -keep)
        return carry

    lax.fori_loop(0, slots, masks, 0)
    lane = lax.broadcasted_iota(jnp.int32, (size, LOW), 1)
    scale_lane = lax.broadcasted_iota(jnp.int32, (1, LOW), 1)
    layout = tile_rows(channels)

    def send_near(first, count):
        def send(i, carry):
            to = near(i)
            pltpu.make_async_remote_copy(
                src_ref=msg.at[pl.ds(first, count), to[0] * blocks + to[1]],
                dst_ref=data_out.at[me, pl.ds(first, count)],
                send_sem=dsend, recv_sem=drecv, device_id=to, device_id_type=MESH,
            ).start()
            return carry

        lax.fori_loop(1, half_devices, send, 0)

    def send_scale(to):
        pltpu.make_async_remote_copy(
            src_ref=scl, dst_ref=scale_out.at[me],
            send_sem=ssend, recv_sem=srecv, device_id=to, device_id_type=MESH,
        ).start()

    def chunk(j, last):
        pltpu.make_async_copy(rbuf.at[j], rbuf.at[j], crecv.at[j]).wait()
        if last:
            send_near(0, chunks - 1)
        for q in range(groups):
            for c in range(local_channels):
                for p in range(parts):
                    row = ((q * local_channels + c) * parts + p) * size
                    wide = rbuf[j, q, c, p].astype(jnp.float32)
                    for t in range(tiles):
                        xs[t, row : row + size, :] = wide[:, t * LOW : (t + 1) * LOW]

        def step(u, carry):
            t = j * (size // LOAD_SLOTS) + u
            load(t).wait()
            for v in range(LOAD_SLOTS):
                s = u * LOAD_SLOTS + v
                x = jnp.concatenate(
                    [xs[i, pl.ds(s, rows, stride=size), :] for i in range(tiles)], axis=1
                )
                at = pl.ds(j * size + s, 1)
                both = jnp.concatenate([x * valid_ref[at, :], x * sign_ref[at, :]], axis=0)
                sums = lax.dot_general(
                    both.astype(jnp.bfloat16), lbuf[lax.rem(t, LOAD_BUFFERS), v],
                    (((1,), (1,)), ((), ())), preferred_element_type=jnp.float32,
                )
                for i in range(sp.shape[0]):
                    sp[i, pl.ds(s, 2 * rows, stride=size), :] = sums[:, i * LOW : (i + 1) * LOW]

            @pl.when(t + LOAD_BUFFERS < slots // LOAD_SLOTS)
            def _():
                load(t + LOAD_BUFFERS).start()

            return carry

        lax.fori_loop(0, size // LOAD_SLOTS, step, 0)

        def piece(half, side, c, p):
            row = (half * rows + c * parts + p) * size
            return sp[side, row : row + size, :]

        scales = scl[...]
        for c in range(channels):
            top = jnp.abs(piece(0, 0, c, 0))
            for half in range(2):
                for side in range(sp.shape[0]):
                    for p in range(parts):
                        top = jnp.maximum(top, jnp.abs(piece(half, side, c, p)))
            top = jnp.maximum(jnp.max(top, keepdims=True), 1e-30)
            unit = (top * (1.0078125 / CODE_MAX)).astype(jnp.bfloat16).astype(jnp.float32)
            inverse[c] = jnp.broadcast_to(1.0 / unit, (size, LOW))
            scales = jnp.where(scale_lane == j * 16 + c, unit, scales)
        scl[...] = scales
        if last:
            to_all(send_scale)
        for half in range(2):
            for side in range(sp.shape[0]):
                first = (half * sp.shape[0] + side) * blocks
                for tile, members in enumerate(layout):
                    values = block_transpose(
                        [piece(half, side, c, p) * inverse[c] for c, p in members], lane
                    )
                    for k in range(blocks):
                        msg[j, first + k, tile] = jnp.round(values[k]).astype(jnp.int16)

        def send(i, carry):
            to = far(i)
            pltpu.make_async_remote_copy(
                src_ref=msg.at[j, to[0] * blocks + to[1]], dst_ref=data_out.at[me, j],
                send_sem=dsend, recv_sem=drecv, device_id=to, device_id_type=MESH,
            ).start()
            return carry

        lax.fori_loop(0, half_devices, send, 0)
        if last:
            send_near(j, 1)
        pltpu.make_async_copy(msg.at[j, me], data_out.at[me, j], drecv).start()

    def early(j, carry):
        chunk(j, False)
        return carry

    scl[...] = jnp.zeros_like(scl)
    lax.fori_loop(0, chunks - 1, early, 0)
    chunk(chunks - 1, True)
    pltpu.make_async_copy(scl, scale_out.at[me], srecv).start()

    def settle(ref, sem):
        pltpu.make_async_copy(ref, ref, sem).wait()

    settle(rbuf.at[:, pl.ds(0, groups - 1)], csend)
    settle(msg.at[:, pl.ds(0, devices - 1)], dsend)
    settle(scale_out.at[pl.ds(0, devices - 1)], ssend)
    settle(data_out, drecv)
    settle(scale_out, srecv)


def exchange(coeffs, operator, m_order, groups, blocks):
    local_channels, parts, _, degrees = coeffs.shape
    slots, north, _ = operator.shape
    channels = groups * local_channels
    devices = groups * blocks
    size = CHUNK_SLOTS
    chunks = slots // size
    rows = channels * parts
    sides = north // LOW
    anywhere = pl.BlockSpec(memory_space=pl.ANY)
    dma = pltpu.SemaphoreType.DMA
    return pl.pallas_call(
        functools.partial(exchange_kernel, groups, blocks),
        in_specs=[pl.BlockSpec(memory_space=pltpu.SMEM), anywhere, anywhere],
        out_specs=[anywhere, anywhere],
        out_shape=[
            jax.ShapeDtypeStruct((devices, chunks, 3, size, LOW), jnp.int16),
            jax.ShapeDtypeStruct((devices, 1, LOW), jnp.float32),
        ],
        scratch_shapes=[
            pltpu.VMEM((chunks, groups, local_channels, parts, size, degrees), jnp.bfloat16),
            pltpu.VMEM((LOAD_BUFFERS, LOAD_SLOTS, north, degrees), jnp.bfloat16),
            pltpu.VMEM((slots, degrees), jnp.float32),
            pltpu.VMEM((slots, degrees), jnp.float32),
            pltpu.VMEM((degrees // LOW, rows * size, LOW), jnp.float32),
            pltpu.VMEM((sides, 2 * rows * size, LOW), jnp.float32),
            pltpu.VMEM((chunks, devices, 3, size, LOW), jnp.int16),
            pltpu.VMEM((channels, size, LOW), jnp.float32),
            pltpu.VMEM((1, LOW), jnp.float32),
            dma, dma((chunks,)), dma((LOAD_BUFFERS,)), dma, dma, dma, dma,
        ],
        compiler_params=pltpu.CompilerParams(
            collective_id=0, has_side_effects=True, vmem_limit_bytes=52 << 20
        ),
    )(m_order, coeffs, operator)


def halves(value):
    upper = value.astype(jnp.bfloat16)
    return upper, (value - upper.astype(jnp.float32)).astype(jnp.bfloat16)


def synthesis_tables(order_count):
    digits = order_count // LOW
    order = np.arange(LOW)[:, None, None] + LOW * np.arange(digits)[None, None, :]
    angle = order * np.arange(HIGH)[None, :, None] % PIX * (2.0 * np.pi / PIX)
    weight = np.where(order == 0, 1.0, 2.0)
    cos, sin = weight * np.cos(angle), weight * np.sin(angle)
    turn = np.stack([np.concatenate([cos, -sin], 2), np.concatenate([sin, cos], 2)], 2)
    turn = turn.reshape(LOW, 2 * HIGH, 2 * digits).astype(np.float32)
    turn_upper = turn.astype(jnp.bfloat16)
    turn_lower = (turn - turn_upper.astype(np.float32)).astype(jnp.bfloat16)
    first = np.concatenate([turn_upper, turn_upper, turn_lower], 2)
    angle = np.arange(LOW)[:, None] * np.arange(LOW)[None, :] % LOW * (2.0 * np.pi / LOW)
    wave = np.concatenate([np.cos(angle), -np.sin(angle)], 1).astype(np.float32)
    wave_upper = wave.astype(jnp.bfloat16)
    wave_lower = (wave - wave_upper.astype(np.float32)).astype(jnp.bfloat16)
    return first, np.concatenate([wave_upper, wave_lower], 0)


def pair_place(a, b):
    if b < 8:
        shift = b - a
        if shift > 4:
            shift, a = 8 - shift, b
        return (shift, (a - 1) % 8) if shift == 2 else (shift, a)
    if a < 8:
        tile, move = {0: (5, 0), 1: (6, 3), 2: (7, 3), 3: (8, 1)}[(b - 8 - a) % 4]
        return tile, (a - move) % 8
    a, b = a - 8, b - 8
    shift = b - a
    if shift == 2:
        return 10, a
    return 9, {0: a, 1: 4 + a, 3: 4 + b}[shift]


TILES = 11
ROOM = LOW + 8
SPACE = HIGH + 8


def combine_kernel(
    channels, groups, order_ref, data, scale, spread, first_any, wave, lens, out,
    first, spare, order_rows, turned, sums, cov, heads, first_sem,
):
    sources, chunks, _, size, _ = data.shape
    slots = chunks * size
    blocks = sources // groups
    digits = order_ref.shape[0] // LOW
    fetch = pltpu.make_async_copy(first_any, first, first_sem)
    fetch.start()

    chunk_lane = lax.broadcasted_iota(jnp.int32, (8, LOW), 1) // 16
    chunk_lane = chunk_lane == lax.broadcasted_iota(jnp.int32, (8, LOW), 0)

    def gather(src, carry):
        units = jnp.where(chunk_lane, scale[src], 0.0).astype(jnp.bfloat16)
        unit = jnp.dot(units, spread[...], preferred_element_type=jnp.float32)
        for j in range(chunks):
            for t in range(3):
                value = data[src, j, t].astype(jnp.float32)
                value = value * unit[j : j + 1, t * LOW : (t + 1) * LOW]
                spare[pl.ds(j * size * 8 + t, size, stride=8), :] = value
        base = (lax.rem(src, blocks) * groups + src // blocks) * slots

        def move(s, carry):
            order = order_ref[base + s]
            low = jnp.bitwise_and(order, LOW - 1)
            to = pl.multiple_of((low * digits + lax.shift_right_logical(order, 7)) * 8, 8)
            order_rows[pl.ds(to, 8), :] = spare[pl.ds(pl.multiple_of(s * 8, 8), 8), :]
            return carry

        return lax.fori_loop(0, slots, move, carry, unroll=16)

    lax.fori_loop(0, sources, gather, 0)
    fetch.wait()
    lane_d = lax.broadcasted_iota(jnp.int32, (digits, LOW), 1)
    wide = ROOM * 2 * HIGH

    def turn(l, carry):
        t0, t1, t2 = (
            order_rows[pl.ds(l * (digits * 8) + t, digits, stride=8), :] for t in range(3)
        )
        t3 = pltpu.roll(t2, LOW // 2, 1)
        real = jnp.where(lane_d < LOW // 2, t2, t3)
        imag = jnp.where(lane_d < LOW // 2, t3, t2)
        x = jnp.concatenate(
            [jnp.concatenate([t0, real], 1), jnp.concatenate([t1, imag], 1)], 0
        )
        upper, lower = halves(x)
        y = jnp.dot(
            first[l], jnp.concatenate([upper, lower, upper], 0), preferred_element_type=jnp.float32
        )
        turned[pl.ds(l, 2 * HIGH, stride=ROOM), :] = y[:, :LOW]
        turned[pl.ds(wide + l, 2 * HIGH, stride=ROOM), :] = y[:, LOW:]
        return carry

    lax.fori_loop(0, LOW, turn, 0, unroll=16)

    def spin(x, carry):
        def part(i):
            at = pl.multiple_of((2 * x + i) * ROOM, 8)
            return jnp.concatenate(
                [turned[pl.ds(at, LOW), :], turned[pl.ds(wide + at, LOW), :]], 1
            )

        upper, lower = halves(jnp.concatenate([part(0), part(1)], 0))
        main = jnp.dot(wave[...], upper, preferred_element_type=jnp.float32)
        rest = jnp.dot(wave[:LOW], lower, preferred_element_type=jnp.float32)
        value = main[:LOW] + main[LOW:] + rest
        order_rows[pl.ds(pl.multiple_of(x * LOW, LOW), LOW), :] = value[:, :LOW]
        order_rows[pl.ds(pl.multiple_of(PIX + x * LOW, LOW), LOW), :] = value[:, LOW:]
        return carry

    lax.fori_loop(0, HIGH, spin, 0, unroll=8)

    cycles, sectors = lens.shape
    copies = lax.broadcasted_iota(jnp.int32, (cycles, LOW), 1) % cycles
    copies = copies == lax.broadcasted_iota(jnp.int32, (cycles, LOW), 0)
    copies = jnp.where(copies, 1.0, 0.0).astype(jnp.bfloat16)

    def spread_out(values):
        return lax.dot_general(
            values.astype(jnp.float32).astype(jnp.bfloat16), copies, (((0,), (0,)), ((), ())),
            preferred_element_type=jnp.float32,
        )

    length = 128.0 * spread_out(lax.shift_right_logical(lens[...], 7))
    length = length + spread_out(jnp.bitwise_and(lens[...], 127))
    length = length.astype(jnp.int32)
    ends = []
    for k in range(sectors):
        ends.append(length[k : k + 1] + ends[-1] if k else length[:1])
    lane = lax.broadcasted_iota(jnp.int32, (8, LOW), 1)
    sub = lax.broadcasted_iota(jnp.int32, (8, LOW), 0)

    def block(j):
        begin = (j * 8 + sub) * HIGH
        sector = jnp.zeros((8, LOW), jnp.int32)
        after = jnp.full((8, LOW), 2 * PIX, jnp.int32)
        for k in range(sectors):
            past = ends[k] <= begin
            sector = sector + jnp.where(past, 1, 0)
            after = jnp.minimum(after, jnp.where(past, 2 * PIX, ends[k]))
        return sector, after - begin

    def pair(j, x):
        at = pl.multiple_of(x * LOW + j * 8, 8)
        return order_rows[pl.ds(at, 8), :], order_rows[pl.ds(PIX + at, 8), :]

    sums[...] = jnp.zeros_like(sums)

    def moments(j, carry):
        sector, limit = block(j)

        def add(x, acc):
            a, b = pair(j, x)
            inside = limit > x
            ah = jnp.where(inside, a, 0.0)
            bh = jnp.where(inside, b, 0.0)
            a1, a3, a4 = (pltpu.roll(a, LOW - 16 * d, 1) for d in (1, 3, 4))
            b1, b2 = (pltpu.roll(b, LOW - 16 * d, 1) for d in (1, 2))
            a3h = jnp.where(inside, a3, 0.0)
            bb = jnp.where(lane < LOW // 2, b, b1)
            left = [a, a, a3, a, a, a, a3, a3, b, b, b]
            held = [ah, ah, a3h, ah, ah, ah, a3h, a3h, bh, bh, bh]
            right = [a, a1, a1, a3, a4, b, b, b1, a1, bb, b2]
            full = [acc[i] + left[i] * right[i] for i in range(TILES)]
            head = [acc[TILES + i] + held[i] * right[i] for i in range(TILES)]
            return tuple(full + head)

        zero = jnp.zeros((8, LOW), jnp.float32)
        acc = lax.fori_loop(0, HIGH, add, (zero,) * (2 * TILES), unroll=32)
        tails = [acc[i] - acc[TILES + i] for i in range(TILES)]
        for i in range(TILES):
            heads[i] = acc[TILES + i]
            heads[TILES + i] = tails[i]

        def assign(k, carry):
            here = sector == k
            there = sector + 1 == k
            for i in range(TILES):
                sums[k, i] += jnp.where(here, heads[i], 0.0) + jnp.where(there, heads[TILES + i], 0.0)
            return carry

        return lax.fori_loop(0, sectors, assign, carry)

    lax.fori_loop(0, LOW // 8, moments, 0)

    def collect(k, carry):
        for i in range(TILES):
            cov[i, pl.ds(k, 1), :] = jnp.sum(sums[k, i], axis=0, keepdims=True)
        return carry

    lax.fori_loop(0, sectors, collect, 0)
    share = 1.0 / length.astype(jnp.float32)

    def entry(a, b):
        tile, group = pair_place(a, b)
        value = cov[tile] * share
        return pltpu.roll(value, LOW - 16 * group, 1) if group else value

    full = {(a, b): entry(a, b) for a in range(channels) for b in range(a, channels)}
    trace = full[0, 0]
    for a in range(1, channels):
        trace = trace + full[a, a]
    ridge = trace * (RIDGE_FACTOR / channels)
    for a in range(channels):
        full[a, a] = full[a, a] + ridge
    rhs = [jnp.ones_like(ridge) for _ in range(channels)]
    inverse = []
    for a in range(channels):
        inverse.append(1.0 / full[a, a])
        for b in range(a + 1, channels):
            factor = full[a, b] * inverse[a]
            for c in range(b, channels):
                full[b, c] = full[b, c] - factor * full[a, c]
            rhs[b] = rhs[b] - factor * rhs[a]
    solved = [None] * channels
    for a in reversed(range(channels)):
        value = rhs[a]
        for b in range(a + 1, channels):
            value = value - full[a, b] * solved[b]
        solved[a] = value * inverse[a]
    total = solved[0]
    for a in range(1, channels):
        total = total + solved[a]
    near = jnp.zeros_like(total)
    far = jnp.zeros_like(total)
    group = lax.broadcasted_iota(jnp.int32, total.shape, 1) // 16
    for a in range(channels):
        weight = solved[a] / total
        place = a % 8
        moved = pltpu.roll(weight, 16 * place, 1) if place else weight
        if a < 8:
            near = jnp.where(group == place, moved, near)
        else:
            far = jnp.where(group == place, moved, far)
    cov[0] = near
    cov[1] = far

    def apply(j, carry):
        sector, limit = block(j)
        picked = [jnp.zeros((8, LOW), jnp.float32) for _ in range(4)]
        for k in range(sectors):
            near_k = cov[0, k : k + 1, :]
            far_k = cov[1, k : k + 1, :]
            here = sector == k
            there = sector + 1 == k
            picked[0] = jnp.where(here, near_k, picked[0])
            picked[1] = jnp.where(here, far_k, picked[1])
            picked[2] = jnp.where(there, near_k, picked[2])
            picked[3] = jnp.where(there, far_k, picked[3])

        def weigh(x, carry):
            a, b = pair(j, x)
            inside = limit > x
            value = jnp.where(inside, picked[0], picked[2]) * a
            value = value + jnp.where(inside, picked[1], picked[3]) * b
            order_rows[pl.ds(2 * PIX + j * 8 * SPACE + x, 8, stride=SPACE), :] = value
            return carry

        return lax.fori_loop(0, HIGH, weigh, carry, unroll=8)

    lax.fori_loop(0, LOW // 8, apply, 0)
    pick = lax.broadcasted_iota(jnp.int32, (16, 2 * LOW), 1) % 16
    pick = jnp.where(pick == lax.broadcasted_iota(jnp.int32, (16, 2 * LOW), 0), 1.0, 0.0)
    pick = pick.astype(jnp.bfloat16)
    for x in range(0, PIX, 256):
        upper, lower = halves(
            jnp.concatenate(
                [
                    order_rows[2 * PIX + y * SPACE : 2 * PIX + y * SPACE + HIGH, :]
                    for y in range(x // HIGH, (x + 256) // HIGH)
                ],
                0,
            )
        )
        out[:, x : x + 256] = lax.dot_general(
            pick, jnp.concatenate([upper, lower], 1), (((1,), (1,)), ((), ())),
            preferred_element_type=jnp.float32,
        )


def combine(data, scale, m_order, sector_len, channels, groups):
    order_count = m_order.shape[0]
    cycles, sectors = sector_len.shape
    first, wave = synthesis_tables(order_count)
    spread = np.zeros((16, 3 * LOW), np.float32)
    for tile, members in enumerate(tile_rows(channels)):
        for i, (c, _) in enumerate(members):
            spread[c, tile * LOW + 16 * i : tile * LOW + 16 * i + 16] = 1.0
    spread = np.tile(spread, (8, 1))
    vmem = pl.BlockSpec(memory_space=pltpu.VMEM)
    return pl.pallas_call(
        functools.partial(combine_kernel, channels, groups),
        in_specs=[
            pl.BlockSpec(memory_space=pltpu.SMEM), vmem, vmem, vmem,
            pl.BlockSpec(memory_space=pl.ANY), vmem, vmem,
        ],
        out_specs=vmem,
        out_shape=jax.ShapeDtypeStruct((cycles, PIX), jnp.float32),
        scratch_shapes=[
            pltpu.VMEM(first.shape, jnp.bfloat16),
            pltpu.VMEM((data.shape[1] * data.shape[3] * 8, LOW), jnp.float32),
            pltpu.VMEM((max(order_count * 8, 2 * PIX + LOW * SPACE), LOW), jnp.float32),
            pltpu.VMEM((2 * ROOM * 2 * HIGH, LOW), jnp.float32),
            pltpu.VMEM((sectors, TILES, 8, LOW), jnp.float32),
            pltpu.VMEM((TILES, sectors, LOW), jnp.float32),
            pltpu.VMEM((2 * TILES, 8, LOW), jnp.float32),
            pltpu.SemaphoreType.DMA,
        ],
        compiler_params=pltpu.CompilerParams(vmem_limit_bytes=56 << 20),
    )(
        m_order, data, scale, jnp.asarray(spread, jnp.bfloat16), jnp.asarray(first), jnp.asarray(wave),
        sector_len,
    )


def permute_kernel(order_ref, rows_in, rows_out):
    def step(slot, carry):
        rows_out[pl.ds(order_ref[slot], 1), :] = rows_in[pl.ds(slot, 1), :]
        return carry

    lax.fori_loop(0, rows_in.shape[0], step, 0, unroll=8)


def sort_orders(orders, rows):
    whole = pl.BlockSpec(rows.shape, lambda i, order: (0, 0))
    return pl.pallas_call(
        permute_kernel,
        grid_spec=pltpu.PrefetchScalarGridSpec(
            num_scalar_prefetch=1, grid=(1,), in_specs=[whole], out_specs=whole
        ),
        out_shape=jax.ShapeDtypeStruct(rows.shape, jnp.float32),
        compiler_params=pltpu.CompilerParams(vmem_limit_bytes=32 << 20),
    )(orders, rows)


def split_dot(left, right):
    left_upper, left_lower = halves(left)
    right_upper, right_lower = halves(right)
    return jnp.dot(
        jnp.concatenate([left_upper, left_upper, left_lower], axis=1),
        jnp.concatenate([right_upper, right_lower, right_upper], axis=0),
        preferred_element_type=jnp.float32,
    )


def member_of(start, end, base, count):
    place = lax.broadcasted_iota(jnp.int32, (start.shape[0], count), 1) + base
    pixel = (place % LOW) * HIGH + place // LOW
    return (pixel >= start) & (pixel < end)


def synthesis_kernel(
    channels, shifts, real_ref, imag_ref, d_ref, e_ref, tc_ref, ts_ref, start_ref, end_ref,
    map_ref, moment_ref, z_ref, m_ref, p_ref,
):
    first = split_dot(d_ref[...], jnp.concatenate([real_ref[0], imag_ref[0]], axis=0))
    cos_turn = tc_ref[...]
    sin_turn = ts_ref[...]
    for c in range(channels):
        real = first[:HIGH, c * LOW : (c + 1) * LOW]
        imag = first[HIGH:, c * LOW : (c + 1) * LOW]
        z_ref[c * HIGH : (c + 1) * HIGH, :LOW] = real * cos_turn - imag * sin_turn
        z_ref[c * HIGH : (c + 1) * HIGH, LOW:] = real * sin_turn + imag * cos_turn
    m_ref[...] = split_dot(z_ref[...], e_ref[...])
    for x2 in range(HIGH):
        map_ref[0, :, x2 * LOW : (x2 + 1) * LOW] = m_ref[pl.ds(x2, channels, stride=HIGH), :]
    p_ref[...] = jnp.zeros_like(p_ref)
    start = start_ref[0]
    end = end_ref[0]
    total = jnp.zeros((2 * shifts * GROUP_ROWS, start.shape[0]), jnp.float32)
    for chunk in range(PIX // CHUNK):
        base = chunk * CHUNK
        values = map_ref[0, :, base : base + CHUNK]
        twice = jnp.concatenate([values, values], axis=0)
        for d in range(shifts):
            p_ref[d * GROUP_ROWS : d * GROUP_ROWS + channels, :] = (
                values * twice[d : d + channels]
            )
        product = p_ref[...]
        upper, lower = halves(product)
        member = jnp.where(member_of(start, end, base, CHUNK), 1.0, 0.0).astype(jnp.bfloat16)
        total += lax.dot_general(
            jnp.concatenate([upper, lower], axis=0), member,
            (((1,), (1,)), ((), ())), preferred_element_type=jnp.float32,
        )
    half = shifts * GROUP_ROWS
    moment_ref[0] = total[:half] + total[half:]


def solve_kernel(channels, cov_ref, len_ref, w_ref):
    scale = 1.0 / len_ref[...].astype(jnp.float32)

    def entry(a, b):
        shift = (b - a) % channels
        row = a
        if shift > channels // 2:
            shift, row = channels - shift, b
        return cov_ref[pl.ds(shift * channels + row, 1), :] * scale

    full = {(a, b): entry(a, b) for a in range(channels) for b in range(a, channels)}
    trace = full[0, 0]
    for a in range(1, channels):
        trace = trace + full[a, a]
    ridge = trace * (RIDGE_FACTOR / channels)
    for a in range(channels):
        full[a, a] = full[a, a] + ridge
    rhs = [jnp.ones_like(scale) for _ in range(channels)]
    inverse = []
    for a in range(channels):
        inverse.append(1.0 / full[a, a])
        for b in range(a + 1, channels):
            factor = full[a, b] * inverse[a]
            for c in range(b, channels):
                full[b, c] = full[b, c] - factor * full[a, c]
            rhs[b] = rhs[b] - factor * rhs[a]
    solved = [None] * channels
    for a in reversed(range(channels)):
        value = rhs[a]
        for b in range(a + 1, channels):
            value = value - full[a, b] * solved[b]
        solved[a] = value * inverse[a]
    total = solved[0]
    for a in range(1, channels):
        total = total + solved[a]
    for a in range(channels):
        w_ref[pl.ds(a, 1), :] = solved[a] / total


def general_combine_kernel(map_ref, w_ref, start_ref, end_ref, out_ref):
    start = start_ref[0]
    end = end_ref[0]
    weights = w_ref[0]
    upper, middle = halves(weights)
    lower = weights - upper.astype(jnp.float32) - middle.astype(jnp.float32)
    pieces = jnp.concatenate([upper, middle, lower.astype(jnp.bfloat16)], axis=1)
    for chunk in range(PIX // CHUNK):
        base = chunk * CHUNK
        member = jnp.where(member_of(start, end, base, CHUNK), 1.0, 0.0).astype(jnp.bfloat16)
        pixel_weights = jnp.dot(
            pieces, jnp.concatenate([member, member, member], axis=0),
            preferred_element_type=jnp.float32,
        )
        out_ref[0, :, base : base + CHUNK] = jnp.sum(
            pixel_weights * map_ref[0, :, base : base + CHUNK], axis=0, keepdims=True
        )


def angles(left, right, period):
    phase = left[:, None] * right[None, :] % period
    turned = phase.astype(jnp.float32) * (TWO_PI / period)
    return jnp.cos(turned), jnp.sin(turned)


def synthesize(real, imag, channels, cycles, sector_len):
    order_count = real.shape[0]
    digits = order_count // LOW
    sectors = sector_len.shape[1]
    weight = jnp.where(lax.iota(jnp.int32, order_count) == 0, 1.0, 2.0).astype(jnp.float32)

    def by_cycle(rows):
        rows = (rows * weight[:, None]).reshape(digits, LOW, channels, cycles)
        return rows.transpose(3, 0, 2, 1).reshape(cycles, digits, channels * LOW)

    x_low = lax.iota(jnp.int32, HIGH)
    m_low = lax.iota(jnp.int32, LOW)
    cos_d, sin_d = angles(x_low, lax.iota(jnp.int32, digits), HIGH)
    first = jnp.concatenate(
        [jnp.concatenate([cos_d, -sin_d], 1), jnp.concatenate([sin_d, cos_d], 1)], 0
    )
    cos_t, sin_t = angles(x_low, m_low, PIX)
    cos_e, sin_e = angles(m_low, m_low, LOW)
    second = jnp.concatenate([cos_e, -sin_e], 0)
    upto = lax.iota(jnp.int32, sectors)
    ends = jnp.sum(jnp.where(upto[:, None] >= upto, sector_len[:, None, :], 0), axis=2)
    starts = (ends - sector_len)[:, :, None]
    ends = ends[:, :, None]
    shifts = channels // 2 + 1
    half = shifts * GROUP_ROWS

    def fixed(array):
        return pl.BlockSpec(array.shape, lambda i: (0, 0))

    def each(rows, columns):
        return pl.BlockSpec((1, rows, columns), lambda i: (i, 0, 0))

    maps, moments = pl.pallas_call(
        functools.partial(synthesis_kernel, channels, shifts),
        grid=(cycles,),
        in_specs=[
            each(digits, channels * LOW), each(digits, channels * LOW), fixed(first), fixed(second), fixed(cos_t),
            fixed(sin_t), each(sectors, 1), each(sectors, 1),
        ],
        out_specs=[each(channels, PIX), each(half, sectors)],
        out_shape=[
            jax.ShapeDtypeStruct((cycles, channels, PIX), jnp.float32),
            jax.ShapeDtypeStruct((cycles, half, sectors), jnp.float32),
        ],
        scratch_shapes=[
            pltpu.VMEM((channels * HIGH, 2 * LOW), jnp.float32),
            pltpu.VMEM((channels * HIGH, LOW), jnp.float32),
            pltpu.VMEM((half, CHUNK), jnp.float32),
        ],
        compiler_params=pltpu.CompilerParams(vmem_limit_bytes=48 << 20),
    )(by_cycle(real), by_cycle(imag), first, second, cos_t, sin_t, starts, ends)
    covariance = moments.reshape(cycles, shifts, GROUP_ROWS, sectors)[:, :, :channels]
    covariance = covariance.transpose(1, 2, 0, 3).reshape(shifts * channels, cycles * sectors)
    weights = pl.pallas_call(
        functools.partial(solve_kernel, channels),
        out_shape=jax.ShapeDtypeStruct((channels, cycles * sectors), jnp.float32),
    )(covariance, sector_len.reshape(1, cycles * sectors))
    weights = weights.reshape(channels, cycles, sectors).transpose(1, 0, 2)
    combined = pl.pallas_call(
        general_combine_kernel,
        grid=(cycles,),
        in_specs=[each(channels, PIX), each(channels, sectors), each(sectors, 1), each(sectors, 1)],
        out_specs=each(1, PIX),
        out_shape=jax.ShapeDtypeStruct((cycles, 1, PIX), jnp.float32),
    )(maps, weights, starts, ends)
    return combined.reshape(cycles, HIGH, LOW).transpose(0, 2, 1).reshape(cycles, PIX)


def general_device(coeffs, legendre, m_order, sector_len):
    slot_count, north_count, degree_count = legendre.shape[1:]
    order_count = m_order.shape[0]
    group_count = lax.axis_size("chan")
    block_count = lax.axis_size("blk")
    device_count = group_count * block_count
    channels = coeffs.shape[0] * group_count
    cycles = sector_len.shape[0]
    first_slot = (lax.axis_index("blk") * group_count + lax.axis_index("chan")) * slot_count
    orders = lax.dynamic_slice_in_dim(m_order, first_slot, slot_count, 0)
    operator = legendre[0]
    degree = order_count - degree_count + lax.iota(jnp.int32, degree_count)
    valid_mask = degree[None, :] >= orders[:, None]
    parity = (degree[None, :] + orders[:, None]) % 2
    keep = jnp.stack([valid_mask & (parity == 0), valid_mask & (parity == 1)])
    zero_value = jnp.zeros((), coeffs.dtype)
    order_joined = (
        m_order.reshape(block_count, group_count, slot_count).transpose(1, 0, 2).reshape(-1)
    )
    received = []
    for p in range(2):
        part = lax.all_to_all(coeffs[:, p], "chan", split_axis=1, concat_axis=0, tiled=True)
        masked = jnp.where(keep[:, None], part[None], zero_value)
        sums = jnp.einsum("ecsl,srl->secr", masked, operator, preferred_element_type=jnp.float32)
        even_sum, odd_sum = sums[:, 0], sums[:, 1]
        spectra = jnp.concatenate([even_sum + odd_sum, even_sum - odd_sum], axis=2)
        spectra = spectra.reshape(slot_count, channels, device_count, cycles)
        spectra = spectra.transpose(2, 0, 1, 3).reshape(
            device_count, slot_count, channels * cycles
        )
        spectra = lax.all_to_all(
            spectra, ("chan", "blk"), split_axis=0, concat_axis=0, tiled=True
        )
        received.append(
            sort_orders(order_joined, spectra.reshape(order_count, channels * cycles))
        )
    return synthesize(received[0], received[1], channels, cycles, sector_len)


def per_device(coeffs, legendre, m_order, sector_len):
    slots, north, _ = legendre.shape[1:]
    groups = lax.axis_size("chan")
    blocks = lax.axis_size("blk")
    channels = coeffs.shape[0] * groups
    cycles = sector_len.shape[0]
    fits = (
        slots % CHUNK_SLOTS == 0 and CHUNK_SLOTS < slots <= LOW and blocks == 8 and cycles * blocks == LOW
        and 2 * north == groups * LOW and channels == 12
    )
    if not fits:
        return general_device(coeffs, legendre, m_order, sector_len)
    data, scale = exchange(coeffs, legendre[0], m_order, groups, blocks)
    return combine(data, scale, m_order, sector_len, channels, groups)


def solution(mesh):
    placed = (
        P("chan", None, "blk", None),
        P("chan", "blk", None, None),
        P(),
        P(("chan", "blk"), None),
    )
    return jax.shard_map(
        per_device, mesh=mesh, in_specs=placed, out_specs=P(("chan", "blk"), None), check_vma=False
    )
```

```python
import functools

import jax
import jax.numpy as jnp
import numpy as np
from jax import lax
from jax.experimental import pallas as pl
from jax.experimental.pallas import tpu as pltpu
from jax.sharding import PartitionSpec as P

PIX = 8192
LOW = 128
HIGH = PIX // LOW
RIDGE_FACTOR = 0.05
TWO_PI = 6.283185307179586
CHUNK = 1024
GROUP_ROWS = 16
MESH = pl.DeviceIdType.MESH
CHUNK_SLOTS = 16
LOAD_SLOTS = 4
LOAD_BUFFERS = 3
CODE_MAX = 32767.0


def block_transpose(values, lane):
    values = list(values)
    for bit in (1, 2, 4):
        upper = (lane // 16) % (2 * bit) >= bit
        for i in range(8):
            if i & bit:
                continue
            a, b = values[i], values[i | bit]
            values[i] = jnp.where(upper, pltpu.roll(b, 16 * bit, 1), a)
            values[i | bit] = jnp.where(upper, b, pltpu.roll(a, LOW - 16 * bit, 1))
    return values


def tile_rows(channels):
    return [
        [(c, 0) for c in range(8)],
        [(c, 1) for c in range(8)],
        [(c, 0) for c in range(8, channels)] + [(c, 1) for c in range(8, channels)],
    ]


def exchange_kernel(
    groups, blocks, order_ref, coeffs, legendre, data_out, scale_out,
    rbuf, lbuf, valid_ref, sign_ref, xs, sp, msg, inverse, scl,
    csend, crecv, lsem, dsend, drecv, ssend, srecv,
):
    chunks, _, local_channels, parts, size, degrees = rbuf.shape
    channels = groups * local_channels
    rows = channels * parts
    slots = chunks * size
    tiles = degrees // LOW
    devices = groups * blocks
    g = lax.axis_index("chan")
    b = lax.axis_index("blk")
    me = g * blocks + b

    half_blocks = blocks // 2
    half_devices = devices // 2
    my_half = b // half_blocks

    def near(i):
        at = lax.rem(b + i // groups, half_blocks)
        return lax.rem(g + i % groups, groups), my_half * half_blocks + at

    def far(i):
        at = lax.rem(b + i // groups, half_blocks)
        return lax.rem(g + i % groups, groups), (1 - my_half) * half_blocks + at

    barrier = pltpu.get_barrier_semaphore()

    def to_all(act):
        def to_far(i, carry):
            act(far(i))
            return carry

        def to_near(i, carry):
            act(near(i))
            return carry

        lax.fori_loop(0, half_devices, to_far, 0)
        lax.fori_loop(1, half_devices, to_near, 0)

    def greet(to):
        pl.semaphore_signal(barrier, inc=1, device_id=to, device_id_type=MESH)

    to_all(greet)

    def load(t):
        return pltpu.make_async_copy(
            legendre.at[pl.ds(t * LOAD_SLOTS, LOAD_SLOTS)],
            lbuf.at[lax.rem(t, LOAD_BUFFERS)], lsem.at[lax.rem(t, LOAD_BUFFERS)],
        )

    for t in range(LOAD_BUFFERS):
        load(t).start()
    pl.semaphore_wait(barrier, devices - 1)

    def start_coeffs(j):
        for i in range(1, groups):
            to = lax.rem(g + i, groups)
            pltpu.make_async_remote_copy(
                src_ref=coeffs.at[:, :, pl.ds(to * slots + j * size, size), :],
                dst_ref=rbuf.at[j, g],
                send_sem=csend, recv_sem=crecv.at[j],
                device_id=(to, b), device_id_type=MESH,
            ).start()
        pltpu.make_async_copy(
            coeffs.at[:, :, pl.ds(g * slots + j * size, size), :], rbuf.at[j, g], crecv.at[j]
        ).start()

    for j in range(chunks):
        start_coeffs(j)
    degree = lax.broadcasted_iota(jnp.int32, (1, degrees), 1) + order_ref.shape[0] - degrees
    first_slot = (b * groups + g) * slots

    def masks(s, carry):
        order = order_ref[first_slot + s]
        keep = jnp.where(degree >= order, 1.0, 0.0)
        at = pl.ds(s, 1)
        valid_ref[at, :] = keep
        sign_ref[at, :] = jnp.where((degree + order) % 2 == 0, keep, -keep)
        return carry

    lax.fori_loop(0, slots, masks, 0)
    lane = lax.broadcasted_iota(jnp.int32, (size, LOW), 1)
    scale_lane = lax.broadcasted_iota(jnp.int32, (1, LOW), 1)
    layout = tile_rows(channels)

    def send_near(first, count):
        def send(i, carry):
            to = near(i)
            pltpu.make_async_remote_copy(
                src_ref=msg.at[pl.ds(first, count), to[0] * blocks + to[1]],
                dst_ref=data_out.at[me, pl.ds(first, count)],
                send_sem=dsend, recv_sem=drecv, device_id=to, device_id_type=MESH,
            ).start()
            return carry

        lax.fori_loop(1, half_devices, send, 0)

    def send_scale(to):
        pltpu.make_async_remote_copy(
            src_ref=scl, dst_ref=scale_out.at[me],
            send_sem=ssend, recv_sem=srecv, device_id=to, device_id_type=MESH,
        ).start()

    def chunk(j, last):
        pltpu.make_async_copy(rbuf.at[j], rbuf.at[j], crecv.at[j]).wait()
        if last:
            send_near(0, chunks - 1)
        for q in range(groups):
            for c in range(local_channels):
                for p in range(parts):
                    row = ((q * local_channels + c) * parts + p) * size
                    wide = rbuf[j, q, c, p].astype(jnp.float32)
                    for t in range(tiles):
                        xs[t, row : row + size, :] = wide[:, t * LOW : (t + 1) * LOW]

        def step(u, carry):
            t = j * (size // LOAD_SLOTS) + u
            load(t).wait()
            for v in range(LOAD_SLOTS):
                s = u * LOAD_SLOTS + v
                x = jnp.concatenate(
                    [xs[i, pl.ds(s, rows, stride=size), :] for i in range(tiles)], axis=1
                )
                at = pl.ds(j * size + s, 1)
                both = jnp.concatenate([x * valid_ref[at, :], x * sign_ref[at, :]], axis=0)
                sums = lax.dot_general(
                    both.astype(jnp.bfloat16), lbuf[lax.rem(t, LOAD_BUFFERS), v],
                    (((1,), (1,)), ((), ())), preferred_element_type=jnp.float32,
                )
                for i in range(sp.shape[0]):
                    sp[i, pl.ds(s, 2 * rows, stride=size), :] = sums[:, i * LOW : (i + 1) * LOW]

            @pl.when(t + LOAD_BUFFERS < slots // LOAD_SLOTS)
            def _():
                load(t + LOAD_BUFFERS).start()

            return carry

        lax.fori_loop(0, size // LOAD_SLOTS, step, 0)

        def piece(half, side, c, p):
            row = (half * rows + c * parts + p) * size
            return sp[side, row : row + size, :]

        scales = scl[...]
        for c in range(channels):
            top = jnp.abs(piece(0, 0, c, 0))
            for half in range(2):
                for side in range(sp.shape[0]):
                    for p in range(parts):
                        top = jnp.maximum(top, jnp.abs(piece(half, side, c, p)))
            top = jnp.maximum(jnp.max(top, keepdims=True), 1e-30)
            unit = (top * (1.0078125 / CODE_MAX)).astype(jnp.bfloat16).astype(jnp.float32)
            inverse[c] = jnp.broadcast_to(1.0 / unit, (size, LOW))
            scales = jnp.where(scale_lane == j * 16 + c, unit, scales)
        scl[...] = scales
        if last:
            to_all(send_scale)
        for half in range(2):
            for side in range(sp.shape[0]):
                first = (half * sp.shape[0] + side) * blocks
                for tile, members in enumerate(layout):
                    values = block_transpose(
                        [piece(half, side, c, p) * inverse[c] for c, p in members], lane
                    )
                    for k in range(blocks):
                        msg[j, first + k, tile] = jnp.round(values[k]).astype(jnp.int16)

        def send(i, carry):
            to = far(i)
            pltpu.make_async_remote_copy(
                src_ref=msg.at[j, to[0] * blocks + to[1]], dst_ref=data_out.at[me, j],
                send_sem=dsend, recv_sem=drecv, device_id=to, device_id_type=MESH,
            ).start()
            return carry

        lax.fori_loop(0, half_devices, send, 0)
        if last:
            send_near(j, 1)
        pltpu.make_async_copy(msg.at[j, me], data_out.at[me, j], drecv).start()

    def early(j, carry):
        chunk(j, False)
        return carry

    scl[...] = jnp.zeros_like(scl)
    lax.fori_loop(0, chunks - 1, early, 0)
    chunk(chunks - 1, True)
    pltpu.make_async_copy(scl, scale_out.at[me], srecv).start()

    def settle(ref, sem):
        pltpu.make_async_copy(ref, ref, sem).wait()

    settle(rbuf.at[:, pl.ds(0, groups - 1)], csend)
    settle(msg.at[:, pl.ds(0, devices - 1)], dsend)
    settle(scale_out.at[pl.ds(0, devices - 1)], ssend)
    settle(data_out, drecv)
    settle(scale_out, srecv)


def exchange(coeffs, operator, m_order, groups, blocks):
    local_channels, parts, _, degrees = coeffs.shape
    slots, north, _ = operator.shape
    channels = groups * local_channels
    devices = groups * blocks
    size = CHUNK_SLOTS
    chunks = slots // size
    rows = channels * parts
    sides = north // LOW
    anywhere = pl.BlockSpec(memory_space=pl.ANY)
    dma = pltpu.SemaphoreType.DMA
    return pl.pallas_call(
        functools.partial(exchange_kernel, groups, blocks),
        in_specs=[pl.BlockSpec(memory_space=pltpu.SMEM), anywhere, anywhere],
        out_specs=[anywhere, anywhere],
        out_shape=[
            jax.ShapeDtypeStruct((devices, chunks, 3, size, LOW), jnp.int16),
            jax.ShapeDtypeStruct((devices, 1, LOW), jnp.float32),
        ],
        scratch_shapes=[
            pltpu.VMEM((chunks, groups, local_channels, parts, size, degrees), jnp.bfloat16),
            pltpu.VMEM((LOAD_BUFFERS, LOAD_SLOTS, north, degrees), jnp.bfloat16),
            pltpu.VMEM((slots, degrees), jnp.float32),
            pltpu.VMEM((slots, degrees), jnp.float32),
            pltpu.VMEM((degrees // LOW, rows * size, LOW), jnp.float32),
            pltpu.VMEM((sides, 2 * rows * size, LOW), jnp.float32),
            pltpu.VMEM((chunks, devices, 3, size, LOW), jnp.int16),
            pltpu.VMEM((channels, size, LOW), jnp.float32),
            pltpu.VMEM((1, LOW), jnp.float32),
            dma, dma((chunks,)), dma((LOAD_BUFFERS,)), dma, dma, dma, dma,
        ],
        compiler_params=pltpu.CompilerParams(
            collective_id=0, has_side_effects=True, vmem_limit_bytes=58 << 20
        ),
    )(m_order, coeffs, operator)


def halves(value):
    upper = value.astype(jnp.bfloat16)
    return upper, (value - upper.astype(jnp.float32)).astype(jnp.bfloat16)


def synthesis_tables(order_count):
    digits = order_count // LOW
    order = np.arange(LOW)[:, None, None] + LOW * np.arange(digits)[None, None, :]
    angle = order * np.arange(HIGH)[None, :, None] % PIX * (2.0 * np.pi / PIX)
    weight = np.where(order == 0, 1.0, 2.0)
    cos, sin = weight * np.cos(angle), weight * np.sin(angle)
    turn = np.stack([np.concatenate([cos, -sin], 2), np.concatenate([sin, cos], 2)], 2)
    turn = turn.reshape(LOW, 2 * HIGH, 2 * digits).astype(np.float32)
    turn_upper = turn.astype(jnp.bfloat16)
    turn_lower = (turn - turn_upper.astype(np.float32)).astype(jnp.bfloat16)
    first = np.concatenate([turn_upper, turn_upper, turn_lower], 2)
    angle = np.arange(LOW)[:, None] * np.arange(LOW)[None, :] % LOW * (2.0 * np.pi / LOW)
    wave = np.concatenate([np.cos(angle), -np.sin(angle)], 1).astype(np.float32)
    wave_upper = wave.astype(jnp.bfloat16)
    wave_lower = (wave - wave_upper.astype(np.float32)).astype(jnp.bfloat16)
    return first, np.concatenate([wave_upper, wave_lower], 0)


def pair_place(a, b):
    if b < 8:
        shift = b - a
        if shift > 4:
            shift, a = 8 - shift, b
        return (shift, (a - 1) % 8) if shift == 2 else (shift, a)
    if a < 8:
        tile, move = {0: (5, 0), 1: (6, 3), 2: (7, 3), 3: (8, 1)}[(b - 8 - a) % 4]
        return tile, (a - move) % 8
    a, b = a - 8, b - 8
    shift = b - a
    if shift == 2:
        return 10, a
    return 9, {0: a, 1: 4 + a, 3: 4 + b}[shift]


TILES = 11
ROOM = LOW + 8
SPACE = HIGH + 8


def combine_kernel(
    channels, groups, place_ref, data_any, scale_any, spread, first_any, wave, lens, out,
    data, scale, first, spare, order_rows, weighed, turned, sums, cov, heads,
    data_sem, scale_sem, first_sem,
):
    sources, chunks, _, size, _ = data.shape
    slots = chunks * size
    blocks = sources // groups
    digits = place_ref.shape[0] // LOW
    fetch_scale = pltpu.make_async_copy(scale_any, scale, scale_sem)
    fetch_scale.start()

    def fetch_data(i):
        part = pl.ds(i * blocks, blocks)
        return pltpu.make_async_copy(data_any.at[part], data.at[part], data_sem.at[i])

    for i in range(groups):
        fetch_data(i).start()
    fetch = pltpu.make_async_copy(first_any, first, first_sem)
    fetch.start()
    fetch_scale.wait()

    chunk_lane = lax.broadcasted_iota(jnp.int32, (8, LOW), 1) // 16
    chunk_lane = chunk_lane == lax.broadcasted_iota(jnp.int32, (8, LOW), 0)

    def gather(src, carry):
        @pl.when(lax.rem(src, blocks) == 0)
        def _():
            fetch_data(src // blocks).wait()

        units = jnp.where(chunk_lane, scale[src], 0.0).astype(jnp.bfloat16)
        unit = jnp.dot(units, spread[...], preferred_element_type=jnp.float32)
        for j in range(chunks):
            for t in range(3):
                value = data[src, j, t].astype(jnp.float32)
                value = value * unit[j : j + 1, t * LOW : (t + 1) * LOW]
                spare[pl.ds(j * size * 8 + t, size, stride=8), :] = value
        base = (lax.rem(src, blocks) * groups + src // blocks) * slots

        def move(s, carry):
            to = pl.multiple_of(place_ref[base + s], 8)
            order_rows[pl.ds(to, 8), :] = spare[pl.ds(pl.multiple_of(s * 8, 8), 8), :]
            return carry

        return lax.fori_loop(0, slots, move, carry, unroll=slots)

    lax.fori_loop(0, sources, gather, 0)
    fetch.wait()
    lane_d = lax.broadcasted_iota(jnp.int32, (digits, LOW), 1)
    wide = ROOM * 2 * HIGH

    def turn(l, carry):
        t0, t1, t2 = (
            order_rows[pl.ds(l * (digits * 8) + t, digits, stride=8), :] for t in range(3)
        )
        t3 = pltpu.roll(t2, LOW // 2, 1)
        real = jnp.where(lane_d < LOW // 2, t2, t3)
        imag = jnp.where(lane_d < LOW // 2, t3, t2)
        x = jnp.concatenate(
            [jnp.concatenate([t0, real], 1), jnp.concatenate([t1, imag], 1)], 0
        )
        upper, lower = halves(x)
        y = jnp.dot(
            first[l], jnp.concatenate([upper, lower, upper], 0), preferred_element_type=jnp.float32
        )
        turned[pl.ds(l, 2 * HIGH, stride=ROOM), :] = y[:, :LOW]
        turned[pl.ds(wide + l, 2 * HIGH, stride=ROOM), :] = y[:, LOW:]
        return carry

    lax.fori_loop(0, LOW, turn, 0, unroll=16)

    def spin(x, carry):
        def part(i):
            at = pl.multiple_of((2 * x + i) * ROOM, 8)
            return jnp.concatenate(
                [turned[pl.ds(at, LOW), :], turned[pl.ds(wide + at, LOW), :]], 1
            )

        upper, lower = halves(jnp.concatenate([part(0), part(1)], 0))
        main = jnp.dot(wave[...], upper, preferred_element_type=jnp.float32)
        rest = jnp.dot(wave[:LOW], lower, preferred_element_type=jnp.float32)
        value = main[:LOW] + main[LOW:] + rest
        order_rows[pl.ds(pl.multiple_of(x * LOW, LOW), LOW), :] = value[:, :LOW]
        order_rows[pl.ds(pl.multiple_of(PIX + x * LOW, LOW), LOW), :] = value[:, LOW:]
        return carry

    lax.fori_loop(0, HIGH, spin, 0, unroll=8)

    cycles, sectors = lens.shape
    copies = lax.broadcasted_iota(jnp.int32, (cycles, LOW), 1) % cycles
    copies = copies == lax.broadcasted_iota(jnp.int32, (cycles, LOW), 0)
    copies = jnp.where(copies, 1.0, 0.0).astype(jnp.bfloat16)

    def spread_out(values):
        return lax.dot_general(
            values.astype(jnp.float32).astype(jnp.bfloat16), copies, (((0,), (0,)), ((), ())),
            preferred_element_type=jnp.float32,
        )

    length = 128.0 * spread_out(lax.shift_right_logical(lens[...], 7))
    length = length + spread_out(jnp.bitwise_and(lens[...], 127))
    length = length.astype(jnp.int32)
    ends = []
    for k in range(sectors):
        ends.append(length[k : k + 1] + ends[-1] if k else length[:1])
    lane = lax.broadcasted_iota(jnp.int32, (8, LOW), 1)
    sub = lax.broadcasted_iota(jnp.int32, (8, LOW), 0)

    def block(j):
        begin = (j * 8 + sub) * HIGH
        sector = jnp.zeros((8, LOW), jnp.int32)
        after = jnp.full((8, LOW), 2 * PIX, jnp.int32)
        for k in range(sectors):
            past = ends[k] <= begin
            sector = sector + jnp.where(past, 1, 0)
            after = jnp.minimum(after, jnp.where(past, 2 * PIX, ends[k]))
        return sector, after - begin

    def pair(j, x):
        at = pl.multiple_of(x * LOW + j * 8, 8)
        return order_rows[pl.ds(at, 8), :], order_rows[pl.ds(PIX + at, 8), :]

    sums[...] = jnp.zeros_like(sums)

    def moments(j, carry):
        sector, limit = block(j)

        def add(x, acc):
            a, b = pair(j, x)
            ended = limit == x
            a1, a3, a4 = (pltpu.roll(a, LOW - 16 * d, 1) for d in (1, 3, 4))
            b1, b2 = (pltpu.roll(b, LOW - 16 * d, 1) for d in (1, 2))
            bb = jnp.where(lane < LOW // 2, b, b1)
            left = [a, a, a3, a, a, a, a3, a3, b, b, b]
            right = [a, a1, a1, a3, a4, b, b, b1, a1, bb, b2]
            head = [jnp.where(ended, acc[i], acc[TILES + i]) for i in range(TILES)]
            full = [acc[i] + left[i] * right[i] for i in range(TILES)]
            return tuple(full + head)

        zero = jnp.zeros((8, LOW), jnp.float32)
        acc = lax.fori_loop(0, HIGH, add, (zero,) * (2 * TILES), unroll=HIGH)
        for i in range(TILES):
            head = jnp.where(limit >= HIGH, acc[i], acc[TILES + i])
            heads[i] = head
            heads[TILES + i] = acc[i] - head

        def assign(k, carry):
            here = sector == k
            there = sector + 1 == k
            for i in range(TILES):
                sums[k, i] += jnp.where(here, heads[i], 0.0) + jnp.where(there, heads[TILES + i], 0.0)
            return carry

        return lax.fori_loop(0, sectors, assign, carry)

    lax.fori_loop(0, LOW // 8, moments, 0)

    def collect(k, carry):
        for i in range(TILES):
            cov[i, pl.ds(k, 1), :] = jnp.sum(sums[k, i], axis=0, keepdims=True)
        return carry

    lax.fori_loop(0, sectors, collect, 0)
    share = 1.0 / length.astype(jnp.float32)

    def entry(a, b):
        tile, group = pair_place(a, b)
        value = cov[tile] * share
        return pltpu.roll(value, LOW - 16 * group, 1) if group else value

    full = {(a, b): entry(a, b) for a in range(channels) for b in range(a, channels)}
    trace = full[0, 0]
    for a in range(1, channels):
        trace = trace + full[a, a]
    ridge = trace * (RIDGE_FACTOR / channels)
    for a in range(channels):
        full[a, a] = full[a, a] + ridge
    rhs = [jnp.ones_like(ridge) for _ in range(channels)]
    inverse = []
    for a in range(channels):
        inverse.append(1.0 / full[a, a])
        for b in range(a + 1, channels):
            factor = full[a, b] * inverse[a]
            for c in range(b, channels):
                full[b, c] = full[b, c] - factor * full[a, c]
            rhs[b] = rhs[b] - factor * rhs[a]
    solved = [None] * channels
    for a in reversed(range(channels)):
        value = rhs[a]
        for b in range(a + 1, channels):
            value = value - full[a, b] * solved[b]
        solved[a] = value * inverse[a]
    total = solved[0]
    for a in range(1, channels):
        total = total + solved[a]
    near = jnp.zeros_like(total)
    far = jnp.zeros_like(total)
    group = lax.broadcasted_iota(jnp.int32, total.shape, 1) // 16
    for a in range(channels):
        weight = solved[a] / total
        place = a % 8
        moved = pltpu.roll(weight, 16 * place, 1) if place else weight
        if a < 8:
            near = jnp.where(group == place, moved, near)
        else:
            far = jnp.where(group == place, moved, far)
    cov[0] = near
    cov[1] = far

    def apply(j, carry):
        sector, limit = block(j)
        picked = [jnp.zeros((8, LOW), jnp.float32) for _ in range(4)]
        for k in range(sectors):
            near_k = cov[0, k : k + 1, :]
            far_k = cov[1, k : k + 1, :]
            here = sector == k
            there = sector + 1 == k
            picked[0] = jnp.where(here, near_k, picked[0])
            picked[1] = jnp.where(here, far_k, picked[1])
            picked[2] = jnp.where(there, near_k, picked[2])
            picked[3] = jnp.where(there, far_k, picked[3])

        def weigh(x, carry):
            a, b = pair(j, x)
            inside = limit > x
            value = jnp.where(inside, picked[0], picked[2]) * a
            value = value + jnp.where(inside, picked[1], picked[3]) * b
            weighed[pl.ds(j * 8 * SPACE + x, 8, stride=SPACE), :] = value
            return carry

        return lax.fori_loop(0, HIGH, weigh, carry, unroll=32)

    lax.fori_loop(0, LOW // 8, apply, 0)
    pick = lax.broadcasted_iota(jnp.int32, (16, 2 * LOW), 1) % 16
    pick = jnp.where(pick == lax.broadcasted_iota(jnp.int32, (16, 2 * LOW), 0), 1.0, 0.0)
    pick = pick.astype(jnp.bfloat16)
    for x in range(0, PIX, 256):
        upper, lower = halves(
            jnp.concatenate(
                [
                    weighed[y * SPACE : y * SPACE + HIGH, :]
                    for y in range(x // HIGH, (x + 256) // HIGH)
                ],
                0,
            )
        )
        out[:, x : x + 256] = lax.dot_general(
            pick, jnp.concatenate([upper, lower], 1), (((1,), (1,)), ((), ())),
            preferred_element_type=jnp.float32,
        )


def combine(data, scale, m_order, sector_len, channels, groups):
    order_count = m_order.shape[0]
    cycles, sectors = sector_len.shape
    place = (m_order % LOW * (order_count // LOW) + m_order // LOW) * 8
    first, wave = synthesis_tables(order_count)
    spread = np.zeros((16, 3 * LOW), np.float32)
    for tile, members in enumerate(tile_rows(channels)):
        for i, (c, _) in enumerate(members):
            spread[c, tile * LOW + 16 * i : tile * LOW + 16 * i + 16] = 1.0
    spread = np.tile(spread, (8, 1))
    vmem = pl.BlockSpec(memory_space=pltpu.VMEM)
    anywhere = pl.BlockSpec(memory_space=pl.ANY)
    return pl.pallas_call(
        functools.partial(combine_kernel, channels, groups),
        in_specs=[
            pl.BlockSpec(memory_space=pltpu.SMEM), anywhere, anywhere, vmem, anywhere, vmem, vmem,
        ],
        out_specs=vmem,
        out_shape=jax.ShapeDtypeStruct((cycles, PIX), jnp.float32),
        scratch_shapes=[
            pltpu.VMEM(data.shape, jnp.int16),
            pltpu.VMEM(scale.shape, jnp.float32),
            pltpu.VMEM(first.shape, jnp.bfloat16),
            pltpu.VMEM((data.shape[1] * data.shape[3] * 8, LOW), jnp.float32),
            pltpu.VMEM((max(order_count * 8, 2 * PIX), LOW), jnp.float32),
            pltpu.VMEM((LOW * SPACE, LOW), jnp.float32),
            pltpu.VMEM((2 * ROOM * 2 * HIGH, LOW), jnp.float32),
            pltpu.VMEM((sectors, TILES, 8, LOW), jnp.float32),
            pltpu.VMEM((TILES, sectors, LOW), jnp.float32),
            pltpu.VMEM((2 * TILES, 8, LOW), jnp.float32),
            pltpu.SemaphoreType.DMA((groups,)),
            pltpu.SemaphoreType.DMA,
            pltpu.SemaphoreType.DMA,
        ],
        compiler_params=pltpu.CompilerParams(vmem_limit_bytes=58 << 20),
    )(
        place, data, scale, jnp.asarray(spread, jnp.bfloat16), jnp.asarray(first), jnp.asarray(wave),
        sector_len,
    )


def permute_kernel(order_ref, rows_in, rows_out):
    def step(slot, carry):
        rows_out[pl.ds(order_ref[slot], 1), :] = rows_in[pl.ds(slot, 1), :]
        return carry

    lax.fori_loop(0, rows_in.shape[0], step, 0, unroll=8)


def sort_orders(orders, rows):
    whole = pl.BlockSpec(rows.shape, lambda i, order: (0, 0))
    return pl.pallas_call(
        permute_kernel,
        grid_spec=pltpu.PrefetchScalarGridSpec(
            num_scalar_prefetch=1, grid=(1,), in_specs=[whole], out_specs=whole
        ),
        out_shape=jax.ShapeDtypeStruct(rows.shape, jnp.float32),
        compiler_params=pltpu.CompilerParams(vmem_limit_bytes=32 << 20),
    )(orders, rows)


def split_dot(left, right):
    left_upper, left_lower = halves(left)
    right_upper, right_lower = halves(right)
    return jnp.dot(
        jnp.concatenate([left_upper, left_upper, left_lower], axis=1),
        jnp.concatenate([right_upper, right_lower, right_upper], axis=0),
        preferred_element_type=jnp.float32,
    )


def member_of(start, end, base, count):
    place = lax.broadcasted_iota(jnp.int32, (start.shape[0], count), 1) + base
    pixel = (place % LOW) * HIGH + place // LOW
    return (pixel >= start) & (pixel < end)


def synthesis_kernel(
    channels, shifts, real_ref, imag_ref, d_ref, e_ref, tc_ref, ts_ref, start_ref, end_ref,
    map_ref, moment_ref, z_ref, m_ref, p_ref,
):
    first = split_dot(d_ref[...], jnp.concatenate([real_ref[0], imag_ref[0]], axis=0))
    cos_turn = tc_ref[...]
    sin_turn = ts_ref[...]
    for c in range(channels):
        real = first[:HIGH, c * LOW : (c + 1) * LOW]
        imag = first[HIGH:, c * LOW : (c + 1) * LOW]
        z_ref[c * HIGH : (c + 1) * HIGH, :LOW] = real * cos_turn - imag * sin_turn
        z_ref[c * HIGH : (c + 1) * HIGH, LOW:] = real * sin_turn + imag * cos_turn
    m_ref[...] = split_dot(z_ref[...], e_ref[...])
    for x2 in range(HIGH):
        map_ref[0, :, x2 * LOW : (x2 + 1) * LOW] = m_ref[pl.ds(x2, channels, stride=HIGH), :]
    p_ref[...] = jnp.zeros_like(p_ref)
    start = start_ref[0]
    end = end_ref[0]
    total = jnp.zeros((2 * shifts * GROUP_ROWS, start.shape[0]), jnp.float32)
    for chunk in range(PIX // CHUNK):
        base = chunk * CHUNK
        values = map_ref[0, :, base : base + CHUNK]
        twice = jnp.concatenate([values, values], axis=0)
        for d in range(shifts):
            p_ref[d * GROUP_ROWS : d * GROUP_ROWS + channels, :] = (
                values * twice[d : d + channels]
            )
        product = p_ref[...]
        upper, lower = halves(product)
        member = jnp.where(member_of(start, end, base, CHUNK), 1.0, 0.0).astype(jnp.bfloat16)
        total += lax.dot_general(
            jnp.concatenate([upper, lower], axis=0), member,
            (((1,), (1,)), ((), ())), preferred_element_type=jnp.float32,
        )
    half = shifts * GROUP_ROWS
    moment_ref[0] = total[:half] + total[half:]


def solve_kernel(channels, cov_ref, len_ref, w_ref):
    scale = 1.0 / len_ref[...].astype(jnp.float32)

    def entry(a, b):
        shift = (b - a) % channels
        row = a
        if shift > channels // 2:
            shift, row = channels - shift, b
        return cov_ref[pl.ds(shift * channels + row, 1), :] * scale

    full = {(a, b): entry(a, b) for a in range(channels) for b in range(a, channels)}
    trace = full[0, 0]
    for a in range(1, channels):
        trace = trace + full[a, a]
    ridge = trace * (RIDGE_FACTOR / channels)
    for a in range(channels):
        full[a, a] = full[a, a] + ridge
    rhs = [jnp.ones_like(scale) for _ in range(channels)]
    inverse = []
    for a in range(channels):
        inverse.append(1.0 / full[a, a])
        for b in range(a + 1, channels):
            factor = full[a, b] * inverse[a]
            for c in range(b, channels):
                full[b, c] = full[b, c] - factor * full[a, c]
            rhs[b] = rhs[b] - factor * rhs[a]
    solved = [None] * channels
    for a in reversed(range(channels)):
        value = rhs[a]
        for b in range(a + 1, channels):
            value = value - full[a, b] * solved[b]
        solved[a] = value * inverse[a]
    total = solved[0]
    for a in range(1, channels):
        total = total + solved[a]
    for a in range(channels):
        w_ref[pl.ds(a, 1), :] = solved[a] / total


def general_combine_kernel(map_ref, w_ref, start_ref, end_ref, out_ref):
    start = start_ref[0]
    end = end_ref[0]
    weights = w_ref[0]
    upper, middle = halves(weights)
    lower = weights - upper.astype(jnp.float32) - middle.astype(jnp.float32)
    pieces = jnp.concatenate([upper, middle, lower.astype(jnp.bfloat16)], axis=1)
    for chunk in range(PIX // CHUNK):
        base = chunk * CHUNK
        member = jnp.where(member_of(start, end, base, CHUNK), 1.0, 0.0).astype(jnp.bfloat16)
        pixel_weights = jnp.dot(
            pieces, jnp.concatenate([member, member, member], axis=0),
            preferred_element_type=jnp.float32,
        )
        out_ref[0, :, base : base + CHUNK] = jnp.sum(
            pixel_weights * map_ref[0, :, base : base + CHUNK], axis=0, keepdims=True
        )


def angles(left, right, period):
    phase = left[:, None] * right[None, :] % period
    turned = phase.astype(jnp.float32) * (TWO_PI / period)
    return jnp.cos(turned), jnp.sin(turned)


def synthesize(real, imag, channels, cycles, sector_len):
    order_count = real.shape[0]
    digits = order_count // LOW
    sectors = sector_len.shape[1]
    weight = jnp.where(lax.iota(jnp.int32, order_count) == 0, 1.0, 2.0).astype(jnp.float32)

    def by_cycle(rows):
        rows = (rows * weight[:, None]).reshape(digits, LOW, channels, cycles)
        return rows.transpose(3, 0, 2, 1).reshape(cycles, digits, channels * LOW)

    x_low = lax.iota(jnp.int32, HIGH)
    m_low = lax.iota(jnp.int32, LOW)
    cos_d, sin_d = angles(x_low, lax.iota(jnp.int32, digits), HIGH)
    first = jnp.concatenate(
        [jnp.concatenate([cos_d, -sin_d], 1), jnp.concatenate([sin_d, cos_d], 1)], 0
    )
    cos_t, sin_t = angles(x_low, m_low, PIX)
    cos_e, sin_e = angles(m_low, m_low, LOW)
    second = jnp.concatenate([cos_e, -sin_e], 0)
    upto = lax.iota(jnp.int32, sectors)
    ends = jnp.sum(jnp.where(upto[:, None] >= upto, sector_len[:, None, :], 0), axis=2)
    starts = (ends - sector_len)[:, :, None]
    ends = ends[:, :, None]
    shifts = channels // 2 + 1
    half = shifts * GROUP_ROWS

    def fixed(array):
        return pl.BlockSpec(array.shape, lambda i: (0, 0))

    def each(rows, columns):
        return pl.BlockSpec((1, rows, columns), lambda i: (i, 0, 0))

    maps, moments = pl.pallas_call(
        functools.partial(synthesis_kernel, channels, shifts),
        grid=(cycles,),
        in_specs=[
            each(digits, channels * LOW), each(digits, channels * LOW), fixed(first), fixed(second), fixed(cos_t),
            fixed(sin_t), each(sectors, 1), each(sectors, 1),
        ],
        out_specs=[each(channels, PIX), each(half, sectors)],
        out_shape=[
            jax.ShapeDtypeStruct((cycles, channels, PIX), jnp.float32),
            jax.ShapeDtypeStruct((cycles, half, sectors), jnp.float32),
        ],
        scratch_shapes=[
            pltpu.VMEM((channels * HIGH, 2 * LOW), jnp.float32),
            pltpu.VMEM((channels * HIGH, LOW), jnp.float32),
            pltpu.VMEM((half, CHUNK), jnp.float32),
        ],
        compiler_params=pltpu.CompilerParams(vmem_limit_bytes=48 << 20),
    )(by_cycle(real), by_cycle(imag), first, second, cos_t, sin_t, starts, ends)
    covariance = moments.reshape(cycles, shifts, GROUP_ROWS, sectors)[:, :, :channels]
    covariance = covariance.transpose(1, 2, 0, 3).reshape(shifts * channels, cycles * sectors)
    weights = pl.pallas_call(
        functools.partial(solve_kernel, channels),
        out_shape=jax.ShapeDtypeStruct((channels, cycles * sectors), jnp.float32),
    )(covariance, sector_len.reshape(1, cycles * sectors))
    weights = weights.reshape(channels, cycles, sectors).transpose(1, 0, 2)
    combined = pl.pallas_call(
        general_combine_kernel,
        grid=(cycles,),
        in_specs=[each(channels, PIX), each(channels, sectors), each(sectors, 1), each(sectors, 1)],
        out_specs=each(1, PIX),
        out_shape=jax.ShapeDtypeStruct((cycles, 1, PIX), jnp.float32),
    )(maps, weights, starts, ends)
    return combined.reshape(cycles, HIGH, LOW).transpose(0, 2, 1).reshape(cycles, PIX)


def general_device(coeffs, legendre, m_order, sector_len):
    slot_count, north_count, degree_count = legendre.shape[1:]
    order_count = m_order.shape[0]
    group_count = lax.axis_size("chan")
    block_count = lax.axis_size("blk")
    device_count = group_count * block_count
    channels = coeffs.shape[0] * group_count
    cycles = sector_len.shape[0]
    first_slot = (lax.axis_index("blk") * group_count + lax.axis_index("chan")) * slot_count
    orders = lax.dynamic_slice_in_dim(m_order, first_slot, slot_count, 0)
    operator = legendre[0]
    degree = order_count - degree_count + lax.iota(jnp.int32, degree_count)
    valid_mask = degree[None, :] >= orders[:, None]
    parity = (degree[None, :] + orders[:, None]) % 2
    keep = jnp.stack([valid_mask & (parity == 0), valid_mask & (parity == 1)])
    zero_value = jnp.zeros((), coeffs.dtype)
    order_joined = (
        m_order.reshape(block_count, group_count, slot_count).transpose(1, 0, 2).reshape(-1)
    )
    received = []
    for p in range(2):
        part = lax.all_to_all(coeffs[:, p], "chan", split_axis=1, concat_axis=0, tiled=True)
        masked = jnp.where(keep[:, None], part[None], zero_value)
        sums = jnp.einsum("ecsl,srl->secr", masked, operator, preferred_element_type=jnp.float32)
        even_sum, odd_sum = sums[:, 0], sums[:, 1]
        spectra = jnp.concatenate([even_sum + odd_sum, even_sum - odd_sum], axis=2)
        spectra = spectra.reshape(slot_count, channels, device_count, cycles)
        spectra = spectra.transpose(2, 0, 1, 3).reshape(
            device_count, slot_count, channels * cycles
        )
        spectra = lax.all_to_all(
            spectra, ("chan", "blk"), split_axis=0, concat_axis=0, tiled=True
        )
        received.append(
            sort_orders(order_joined, spectra.reshape(order_count, channels * cycles))
        )
    return synthesize(received[0], received[1], channels, cycles, sector_len)


def per_device(coeffs, legendre, m_order, sector_len):
    slots, north, _ = legendre.shape[1:]
    groups = lax.axis_size("chan")
    blocks = lax.axis_size("blk")
    channels = coeffs.shape[0] * groups
    cycles = sector_len.shape[0]
    fits = (
        slots % CHUNK_SLOTS == 0 and CHUNK_SLOTS < slots <= LOW and blocks == 8 and cycles * blocks == LOW
        and 2 * north == groups * LOW and channels == 12
    )
    if not fits:
        return general_device(coeffs, legendre, m_order, sector_len)
    data, scale = exchange(coeffs, legendre[0], m_order, groups, blocks)
    return combine(data, scale, m_order, sector_len, channels, groups)


def solution(mesh):
    placed = (
        P("chan", None, "blk", None),
        P("chan", "blk", None, None),
        P(),
        P(("chan", "blk"), None),
    )
    return jax.shard_map(
        per_device, mesh=mesh, in_specs=placed, out_specs=P(("chan", "blk"), None), check_vma=False
    )
```

```python
import functools

import jax
import jax.numpy as jnp
import numpy as np
from jax import lax
from jax.experimental import pallas as pl
from jax.experimental.pallas import tpu as pltpu
from jax.sharding import PartitionSpec as P

PIX = 8192
LOW = 128
HIGH = PIX // LOW
RIDGE_FACTOR = 0.05
TWO_PI = 6.283185307179586
CHUNK = 1024
GROUP_ROWS = 16
MESH = pl.DeviceIdType.MESH
CHUNK_SLOTS = 16
LOAD_SLOTS = 4
LOAD_BUFFERS = 3
CODE_MAX = 32767.0


def block_transpose(values, lane):
    values = list(values)
    for bit in (1, 2, 4):
        upper = (lane // 16) % (2 * bit) >= bit
        for i in range(8):
            if i & bit:
                continue
            a, b = values[i], values[i | bit]
            values[i] = jnp.where(upper, pltpu.roll(b, 16 * bit, 1), a)
            values[i | bit] = jnp.where(upper, b, pltpu.roll(a, LOW - 16 * bit, 1))
    return values


def tile_rows(channels):
    return [
        [(c, 0) for c in range(8)],
        [(c, 1) for c in range(8)],
        [(c, 0) for c in range(8, channels)] + [(c, 1) for c in range(8, channels)],
    ]


def exchange_kernel(
    groups, blocks, order_ref, order_rows, coeffs, legendre, data_out, scale_out, place_out,
    rbuf, lbuf, valid_ref, sign_ref, xs, sp, msg, inverse, scl,
    csend, crecv, lsem, dsend, drecv, ssend, srecv,
):
    chunks, _, local_channels, parts, size, degrees = rbuf.shape
    channels = groups * local_channels
    rows = channels * parts
    slots = chunks * size
    tiles = degrees // LOW
    devices = groups * blocks
    g = lax.axis_index("chan")
    b = lax.axis_index("blk")
    me = g * blocks + b

    half_blocks = blocks // 2
    half_devices = devices // 2
    my_half = b // half_blocks

    def near(i):
        at = lax.rem(b + i // groups, half_blocks)
        return lax.rem(g + i % groups, groups), my_half * half_blocks + at

    def far(i):
        at = lax.rem(b + i // groups, half_blocks)
        return lax.rem(g + i % groups, groups), (1 - my_half) * half_blocks + at

    barrier = pltpu.get_barrier_semaphore()

    def to_all(act):
        def to_far(i, carry):
            act(far(i))
            return carry

        def to_near(i, carry):
            act(near(i))
            return carry

        lax.fori_loop(0, half_devices, to_far, 0)
        lax.fori_loop(1, half_devices, to_near, 0)

    def greet(to):
        pl.semaphore_signal(barrier, inc=1, device_id=to, device_id_type=MESH)

    to_all(greet)

    def load(t):
        return pltpu.make_async_copy(
            legendre.at[pl.ds(t * LOAD_SLOTS, LOAD_SLOTS)],
            lbuf.at[lax.rem(t, LOAD_BUFFERS)], lsem.at[lax.rem(t, LOAD_BUFFERS)],
        )

    for t in range(LOAD_BUFFERS):
        load(t).start()
    pl.semaphore_wait(barrier, devices - 1)

    def start_coeffs(j):
        for i in range(1, groups):
            to = lax.rem(g + i, groups)
            pltpu.make_async_remote_copy(
                src_ref=coeffs.at[:, :, pl.ds(to * slots + j * size, size), :],
                dst_ref=rbuf.at[j, g],
                send_sem=csend, recv_sem=crecv.at[j],
                device_id=(to, b), device_id_type=MESH,
            ).start()
        pltpu.make_async_copy(
            coeffs.at[:, :, pl.ds(g * slots + j * size, size), :], rbuf.at[j, g], crecv.at[j]
        ).start()

    for j in range(chunks):
        start_coeffs(j)
    degree = lax.broadcasted_iota(jnp.int32, (1, degrees), 1) + order_ref.shape[0] - degrees
    first_slot = (b * groups + g) * slots

    def masks(s, carry):
        order = order_ref[first_slot + s]
        keep = jnp.where(degree >= order, 1.0, 0.0)
        at = pl.ds(s, 1)
        valid_ref[at, :] = keep
        sign_ref[at, :] = jnp.where((degree + order) % 2 == 0, keep, -keep)
        return carry

    lax.fori_loop(0, slots, masks, 0)
    order = order_rows[...]
    place = jnp.bitwise_and(order, LOW - 1) * (order_ref.shape[0] // LOW)
    place_out[...] = (place + lax.shift_right_logical(order, 7)) * 8
    lane = lax.broadcasted_iota(jnp.int32, (size, LOW), 1)
    scale_lane = lax.broadcasted_iota(jnp.int32, (1, LOW), 1)
    layout = tile_rows(channels)

    def send_near(first, count):
        def send(i, carry):
            to = near(i)
            pltpu.make_async_remote_copy(
                src_ref=msg.at[pl.ds(first, count), to[0] * blocks + to[1]],
                dst_ref=data_out.at[me, pl.ds(first, count)],
                send_sem=dsend, recv_sem=drecv, device_id=to, device_id_type=MESH,
            ).start()
            return carry

        lax.fori_loop(1, half_devices, send, 0)

    def send_scale(to):
        pltpu.make_async_remote_copy(
            src_ref=scl, dst_ref=scale_out.at[me],
            send_sem=ssend, recv_sem=srecv, device_id=to, device_id_type=MESH,
        ).start()

    def chunk(j, last):
        pltpu.make_async_copy(rbuf.at[j], rbuf.at[j], crecv.at[j]).wait()
        if last:
            send_near(0, chunks - 1)
        for q in range(groups):
            for c in range(local_channels):
                for p in range(parts):
                    row = ((q * local_channels + c) * parts + p) * size
                    wide = rbuf[j, q, c, p].astype(jnp.float32)
                    for t in range(tiles):
                        xs[t, row : row + size, :] = wide[:, t * LOW : (t + 1) * LOW]

        def step(u, carry):
            t = j * (size // LOAD_SLOTS) + u
            load(t).wait()
            for v in range(LOAD_SLOTS):
                s = u * LOAD_SLOTS + v
                x = jnp.concatenate(
                    [xs[i, pl.ds(s, rows, stride=size), :] for i in range(tiles)], axis=1
                )
                at = pl.ds(j * size + s, 1)
                both = jnp.concatenate([x * valid_ref[at, :], x * sign_ref[at, :]], axis=0)
                sums = lax.dot_general(
                    both.astype(jnp.bfloat16), lbuf[lax.rem(t, LOAD_BUFFERS), v],
                    (((1,), (1,)), ((), ())), preferred_element_type=jnp.float32,
                )
                for i in range(sp.shape[0]):
                    sp[i, pl.ds(s, 2 * rows, stride=size), :] = sums[:, i * LOW : (i + 1) * LOW]

            @pl.when(t + LOAD_BUFFERS < slots // LOAD_SLOTS)
            def _():
                load(t + LOAD_BUFFERS).start()

            return carry

        lax.fori_loop(0, size // LOAD_SLOTS, step, 0)

        def piece(half, side, c, p):
            row = (half * rows + c * parts + p) * size
            return sp[side, row : row + size, :]

        scales = scl[...]
        for c in range(channels):
            top = jnp.abs(piece(0, 0, c, 0))
            for half in range(2):
                for side in range(sp.shape[0]):
                    for p in range(parts):
                        top = jnp.maximum(top, jnp.abs(piece(half, side, c, p)))
            top = jnp.maximum(jnp.max(top, keepdims=True), 1e-30)
            unit = (top * (1.0078125 / CODE_MAX)).astype(jnp.bfloat16).astype(jnp.float32)
            inverse[c] = jnp.broadcast_to(1.0 / unit, (size, LOW))
            scales = jnp.where(scale_lane == j * 16 + c, unit, scales)
        scl[...] = scales
        if last:
            to_all(send_scale)
        for half in range(2):
            for side in range(sp.shape[0]):
                first = (half * sp.shape[0] + side) * blocks
                for tile, members in enumerate(layout):
                    values = block_transpose(
                        [piece(half, side, c, p) * inverse[c] for c, p in members], lane
                    )
                    for k in range(blocks):
                        msg[j, first + k, tile] = jnp.round(values[k]).astype(jnp.int16)

        def send(i, carry):
            to = far(i)
            pltpu.make_async_remote_copy(
                src_ref=msg.at[j, to[0] * blocks + to[1]], dst_ref=data_out.at[me, j],
                send_sem=dsend, recv_sem=drecv, device_id=to, device_id_type=MESH,
            ).start()
            return carry

        lax.fori_loop(0, half_devices, send, 0)
        if last:
            send_near(j, 1)
        pltpu.make_async_copy(msg.at[j, me], data_out.at[me, j], drecv).start()

    def early(j, carry):
        chunk(j, False)
        return carry

    scl[...] = jnp.zeros_like(scl)
    lax.fori_loop(0, chunks - 1, early, 0)
    chunk(chunks - 1, True)
    pltpu.make_async_copy(scl, scale_out.at[me], srecv).start()

    def settle(ref, sem):
        pltpu.make_async_copy(ref, ref, sem).wait()

    settle(rbuf.at[:, pl.ds(0, groups - 1)], csend)
    settle(msg.at[:, pl.ds(0, devices - 1)], dsend)
    settle(scale_out.at[pl.ds(0, devices - 1)], ssend)
    settle(data_out, drecv)
    settle(scale_out, srecv)


def exchange(coeffs, operator, m_order, groups, blocks):
    local_channels, parts, _, degrees = coeffs.shape
    slots, north, _ = operator.shape
    channels = groups * local_channels
    devices = groups * blocks
    size = CHUNK_SLOTS
    chunks = slots // size
    rows = channels * parts
    sides = north // LOW
    anywhere = pl.BlockSpec(memory_space=pl.ANY)
    vmem = pl.BlockSpec(memory_space=pltpu.VMEM)
    dma = pltpu.SemaphoreType.DMA
    return pl.pallas_call(
        functools.partial(exchange_kernel, groups, blocks),
        in_specs=[pl.BlockSpec(memory_space=pltpu.SMEM), vmem, anywhere, anywhere],
        out_specs=[anywhere, anywhere, vmem],
        out_shape=[
            jax.ShapeDtypeStruct((devices, chunks, 3, size, LOW), jnp.int16),
            jax.ShapeDtypeStruct((devices, 1, LOW), jnp.float32),
            jax.ShapeDtypeStruct((m_order.shape[0] // LOW, LOW), jnp.int32),
        ],
        scratch_shapes=[
            pltpu.VMEM((chunks, groups, local_channels, parts, size, degrees), jnp.bfloat16),
            pltpu.VMEM((LOAD_BUFFERS, LOAD_SLOTS, north, degrees), jnp.bfloat16),
            pltpu.VMEM((slots, degrees), jnp.float32),
            pltpu.VMEM((slots, degrees), jnp.float32),
            pltpu.VMEM((degrees // LOW, rows * size, LOW), jnp.float32),
            pltpu.VMEM((sides, 2 * rows * size, LOW), jnp.float32),
            pltpu.VMEM((chunks, devices, 3, size, LOW), jnp.int16),
            pltpu.VMEM((channels, size, LOW), jnp.float32),
            pltpu.VMEM((1, LOW), jnp.float32),
            dma, dma((chunks,)), dma((LOAD_BUFFERS,)), dma, dma, dma, dma,
        ],
        compiler_params=pltpu.CompilerParams(
            collective_id=0, has_side_effects=True, vmem_limit_bytes=58 << 20
        ),
    )(m_order, m_order.reshape(-1, LOW), coeffs, operator)


def halves(value):
    upper = value.astype(jnp.bfloat16)
    return upper, (value - upper.astype(jnp.float32)).astype(jnp.bfloat16)


def synthesis_tables(order_count):
    digits = order_count // LOW
    order = np.arange(LOW)[:, None, None] + LOW * np.arange(digits)[None, None, :]
    angle = order * np.arange(HIGH)[None, :, None] % PIX * (2.0 * np.pi / PIX)
    weight = np.where(order == 0, 1.0, 2.0)
    cos, sin = weight * np.cos(angle), weight * np.sin(angle)
    turn = np.stack([np.concatenate([cos, -sin], 2), np.concatenate([sin, cos], 2)], 2)
    turn = turn.reshape(LOW, 2 * HIGH, 2 * digits).astype(np.float32)
    turn_upper = turn.astype(jnp.bfloat16)
    turn_lower = (turn - turn_upper.astype(np.float32)).astype(jnp.bfloat16)
    first = np.concatenate([turn_upper, turn_upper, turn_lower], 2)
    angle = np.arange(LOW)[:, None] * np.arange(LOW)[None, :] % LOW * (2.0 * np.pi / LOW)
    wave = np.concatenate([np.cos(angle), -np.sin(angle)], 1).astype(np.float32)
    wave_upper = wave.astype(jnp.bfloat16)
    wave_lower = (wave - wave_upper.astype(np.float32)).astype(jnp.bfloat16)
    return first, np.concatenate([wave_upper, wave_lower], 0)


def pair_place(a, b):
    if b < 8:
        shift = b - a
        if shift > 4:
            shift, a = 8 - shift, b
        return (shift, (a - 1) % 8) if shift == 2 else (shift, a)
    if a < 8:
        tile, move = {0: (5, 0), 1: (6, 3), 2: (7, 3), 3: (8, 1)}[(b - 8 - a) % 4]
        return tile, (a - move) % 8
    a, b = a - 8, b - 8
    shift = b - a
    if shift == 2:
        return 10, a
    return 9, {0: a, 1: 4 + a, 3: 4 + b}[shift]


TILES = 11
ROOM = LOW + 8
SPACE = HIGH + 8


def combine_kernel(
    channels, groups, place_ref, data_any, scale_any, spread, first_any, wave, lens, out,
    data, scale, first, spare, order_rows, late, weighed, turned, partial, held, cov,
    data_sem, scale_sem, first_sem,
):
    sources, chunks, _, size, _ = data.shape
    slots = chunks * size
    blocks = sources // groups
    digits = place_ref.shape[0] // LOW
    fetch_scale = pltpu.make_async_copy(scale_any, scale, scale_sem)
    fetch_scale.start()

    def fetch_data(i):
        part = pl.ds(i * blocks, blocks)
        return pltpu.make_async_copy(data_any.at[part], data.at[part], data_sem.at[i])

    for i in range(groups):
        fetch_data(i).start()
    fetch = pltpu.make_async_copy(first_any, first, first_sem)
    fetch.start()
    fetch_scale.wait()

    chunk_lane = lax.broadcasted_iota(jnp.int32, (8, LOW), 1) // 16
    chunk_lane = chunk_lane == lax.broadcasted_iota(jnp.int32, (8, LOW), 0)

    def gather(src, carry):
        @pl.when(lax.rem(src, blocks) == 0)
        def _():
            fetch_data(src // blocks).wait()

        units = jnp.where(chunk_lane, scale[src], 0.0).astype(jnp.bfloat16)
        unit = jnp.dot(units, spread[...], preferred_element_type=jnp.float32)
        for j in range(chunks):
            for t in range(3):
                value = data[src, j, t].astype(jnp.float32)
                value = value * unit[j : j + 1, t * LOW : (t + 1) * LOW]
                spare[pl.ds(j * size * 8 + t, size, stride=8), :] = value
        base = (lax.rem(src, blocks) * groups + src // blocks) * slots

        def move(s, carry):
            to = pl.multiple_of(place_ref[base + s], 8)
            order_rows[pl.ds(to, 8), :] = spare[pl.ds(pl.multiple_of(s * 8, 8), 8), :]
            return carry

        return lax.fori_loop(0, slots, move, carry, unroll=slots)

    lax.fori_loop(0, sources, gather, 0)
    fetch.wait()
    lane_d = lax.broadcasted_iota(jnp.int32, (digits, LOW), 1)
    wide = ROOM * 2 * HIGH

    def turn(l, carry):
        t0, t1, t2 = (
            order_rows[pl.ds(l * (digits * 8) + t, digits, stride=8), :] for t in range(3)
        )
        t3 = pltpu.roll(t2, LOW // 2, 1)
        real = jnp.where(lane_d < LOW // 2, t2, t3)
        imag = jnp.where(lane_d < LOW // 2, t3, t2)
        x = jnp.concatenate(
            [jnp.concatenate([t0, real], 1), jnp.concatenate([t1, imag], 1)], 0
        )
        upper, lower = halves(x)
        y = jnp.dot(
            first[l], jnp.concatenate([upper, lower, upper], 0), preferred_element_type=jnp.float32
        )
        turned[pl.ds(l, 2 * HIGH, stride=ROOM), :] = y[:, :LOW]
        turned[pl.ds(wide + l, 2 * HIGH, stride=ROOM), :] = y[:, LOW:]
        return carry

    lax.fori_loop(0, LOW, turn, 0, unroll=32)

    early = HIGH // 2
    second = early * LOW

    def spin_into(maps, x, place):
        def part(i):
            at = pl.multiple_of((2 * x + i) * ROOM, 8)
            return jnp.concatenate(
                [turned[pl.ds(at, LOW), :], turned[pl.ds(wide + at, LOW), :]], 1
            )

        upper, lower = halves(jnp.concatenate([part(0), part(1)], 0))
        main = jnp.dot(wave[...], upper, preferred_element_type=jnp.float32)
        rest = jnp.dot(wave[:LOW], lower, preferred_element_type=jnp.float32)
        value = main[:LOW] + main[LOW:] + rest
        maps[pl.ds(pl.multiple_of(place * LOW, LOW), LOW), :] = value[:, :LOW]
        maps[pl.ds(pl.multiple_of(second + place * LOW, LOW), LOW), :] = value[:, LOW:]

    def spin(x, carry):
        spin_into(order_rows, x, x)
        return carry

    lax.fori_loop(0, early, spin, 0, unroll=16)

    cycles, sectors = lens.shape
    copies = lax.broadcasted_iota(jnp.int32, (cycles, LOW), 1) % cycles
    copies = copies == lax.broadcasted_iota(jnp.int32, (cycles, LOW), 0)
    copies = jnp.where(copies, 1.0, 0.0).astype(jnp.bfloat16)

    def spread_out(values):
        return lax.dot_general(
            values.astype(jnp.float32).astype(jnp.bfloat16), copies, (((0,), (0,)), ((), ())),
            preferred_element_type=jnp.float32,
        )

    length = 128.0 * spread_out(lax.shift_right_logical(lens[...], 7))
    length = length + spread_out(jnp.bitwise_and(lens[...], 127))
    length = length.astype(jnp.int32)
    ends = []
    for k in range(sectors):
        ends.append(length[k : k + 1] + ends[-1] if k else length[:1])
    lane = lax.broadcasted_iota(jnp.int32, (8, LOW), 1)
    sub = lax.broadcasted_iota(jnp.int32, (8, LOW), 0)

    def block(j):
        begin = (j * 8 + sub) * HIGH
        sector = jnp.zeros((8, LOW), jnp.int32)
        after = jnp.full((8, LOW), 2 * PIX, jnp.int32)
        for k in range(sectors):
            past = ends[k] <= begin
            sector = sector + jnp.where(past, 1, 0)
            after = jnp.minimum(after, jnp.where(past, 2 * PIX, ends[k]))
        return sector, after - begin

    def pair(maps, j, place):
        at = pl.multiple_of(place * LOW + j * 8, 8)
        return maps[pl.ds(at, 8), :], maps[pl.ds(second + at, 8), :]

    def add(limit, x, values, acc):
        a, b = values
        ended = limit == x
        a1, a3, a4 = (pltpu.roll(a, LOW - 16 * d, 1) for d in (1, 3, 4))
        b1, b2 = (pltpu.roll(b, LOW - 16 * d, 1) for d in (1, 2))
        bb = jnp.where(lane < LOW // 2, b, b1)
        left = [a, a, a3, a, a, a, a3, a3, b, b, b]
        right = [a, a1, a1, a3, a4, b, b, b1, a1, bb, b2]
        head = [jnp.where(ended, acc[i], acc[TILES + i]) for i in range(TILES)]
        return [acc[i] + left[i] * right[i] for i in range(TILES)] + head

    def first_half(j, carry):
        _, limit = block(j)
        acc = [jnp.zeros((8, LOW), jnp.float32)] * (2 * TILES)
        share = early // (LOW // 8)
        for x in range(early):
            if x < share:
                spin_into(late, early + j * share + x, j * share + x)
            acc = add(limit, x, pair(order_rows, j, x), acc)
        for i in range(2 * TILES):
            partial[j, i] = acc[i]
        return carry

    lax.fori_loop(0, LOW // 8, first_half, 0)

    def moments(j, carry):
        sector, limit = block(j)
        acc = [partial[j, i] for i in range(2 * TILES)]
        for x in range(early):
            acc = add(limit, early + x, pair(late, j, x), acc)
        for i in range(TILES):
            head = jnp.where(limit >= HIGH, acc[i], acc[TILES + i])
            partial[j, i] = head
            partial[j, TILES + i] = acc[i] - head
        held[j] = sector
        return carry

    lax.fori_loop(0, LOW // 8, moments, 0)

    def collect(k, carry):
        acc = [jnp.zeros((8, LOW), jnp.float32)] * TILES
        for j in range(LOW // 8):
            here = held[j] == k
            there = held[j] == k - 1
            for i in range(TILES):
                tail = jnp.where(there, partial[j, TILES + i], 0.0)
                acc[i] = acc[i] + jnp.where(here, partial[j, i], tail)
        for i in range(TILES):
            cov[i, pl.ds(k, 1), :] = jnp.sum(acc[i], axis=0, keepdims=True)
        return carry

    lax.fori_loop(0, sectors, collect, 0, unroll=2)
    share = 1.0 / length.astype(jnp.float32)

    def entry(a, b):
        tile, group = pair_place(a, b)
        value = cov[tile] * share
        return pltpu.roll(value, LOW - 16 * group, 1) if group else value

    full = {(a, b): entry(a, b) for a in range(channels) for b in range(a, channels)}
    trace = full[0, 0]
    for a in range(1, channels):
        trace = trace + full[a, a]
    ridge = trace * (RIDGE_FACTOR / channels)
    for a in range(channels):
        full[a, a] = full[a, a] + ridge
    rhs = [jnp.ones_like(ridge) for _ in range(channels)]
    inverse = []
    for a in range(channels):
        inverse.append(1.0 / full[a, a])
        for b in range(a + 1, channels):
            factor = full[a, b] * inverse[a]
            for c in range(b, channels):
                full[b, c] = full[b, c] - factor * full[a, c]
            rhs[b] = rhs[b] - factor * rhs[a]
    solved = [None] * channels
    for a in reversed(range(channels)):
        value = rhs[a]
        for b in range(a + 1, channels):
            value = value - full[a, b] * solved[b]
        solved[a] = value * inverse[a]
    total = solved[0]
    for a in range(1, channels):
        total = total + solved[a]
    near = jnp.zeros_like(total)
    far = jnp.zeros_like(total)
    group = lax.broadcasted_iota(jnp.int32, total.shape, 1) // 16
    for a in range(channels):
        weight = solved[a] / total
        place = a % 8
        moved = pltpu.roll(weight, 16 * place, 1) if place else weight
        if a < 8:
            near = jnp.where(group == place, moved, near)
        else:
            far = jnp.where(group == place, moved, far)
    cov[0] = near
    cov[1] = far

    def apply(j, carry):
        sector, limit = block(j)
        picked = [jnp.zeros((8, LOW), jnp.float32) for _ in range(4)]
        for k in range(sectors):
            near_k = cov[0, k : k + 1, :]
            far_k = cov[1, k : k + 1, :]
            here = sector == k
            there = sector + 1 == k
            picked[0] = jnp.where(here, near_k, picked[0])
            picked[1] = jnp.where(here, far_k, picked[1])
            picked[2] = jnp.where(there, near_k, picked[2])
            picked[3] = jnp.where(there, far_k, picked[3])

        for x in range(HIGH):
            a, b = pair(order_rows, j, x) if x < early else pair(late, j, x - early)
            inside = limit > x
            value = jnp.where(inside, picked[0], picked[2]) * a
            value = value + jnp.where(inside, picked[1], picked[3]) * b
            weighed[pl.ds(j * 8 * SPACE + x, 8, stride=SPACE), :] = value
        return carry

    lax.fori_loop(0, LOW // 8, apply, 0)
    pick = lax.broadcasted_iota(jnp.int32, (16, 2 * LOW), 1) % 16
    pick = jnp.where(pick == lax.broadcasted_iota(jnp.int32, (16, 2 * LOW), 0), 1.0, 0.0)
    pick = pick.astype(jnp.bfloat16)
    for x in range(0, PIX, 256):
        upper, lower = halves(
            jnp.concatenate(
                [
                    weighed[y * SPACE : y * SPACE + HIGH, :]
                    for y in range(x // HIGH, (x + 256) // HIGH)
                ],
                0,
            )
        )
        out[:, x : x + 256] = lax.dot_general(
            pick, jnp.concatenate([upper, lower], 1), (((1,), (1,)), ((), ())),
            preferred_element_type=jnp.float32,
        )


def combine(data, scale, place, sector_len, channels, groups):
    order_count = place.shape[0]
    cycles, sectors = sector_len.shape
    first, wave = synthesis_tables(order_count)
    spread = np.zeros((16, 3 * LOW), np.float32)
    for tile, members in enumerate(tile_rows(channels)):
        for i, (c, _) in enumerate(members):
            spread[c, tile * LOW + 16 * i : tile * LOW + 16 * i + 16] = 1.0
    spread = np.tile(spread, (8, 1))
    vmem = pl.BlockSpec(memory_space=pltpu.VMEM)
    anywhere = pl.BlockSpec(memory_space=pl.ANY)
    return pl.pallas_call(
        functools.partial(combine_kernel, channels, groups),
        in_specs=[
            pl.BlockSpec(memory_space=pltpu.SMEM), anywhere, anywhere, vmem, anywhere, vmem, vmem,
        ],
        out_specs=vmem,
        out_shape=jax.ShapeDtypeStruct((cycles, PIX), jnp.float32),
        scratch_shapes=[
            pltpu.VMEM(data.shape, jnp.int16),
            pltpu.VMEM(scale.shape, jnp.float32),
            pltpu.VMEM(first.shape, jnp.bfloat16),
            pltpu.VMEM((data.shape[1] * data.shape[3] * 8, LOW), jnp.float32),
            pltpu.VMEM((max(order_count * 8, PIX), LOW), jnp.float32),
            pltpu.VMEM((PIX, LOW), jnp.float32),
            pltpu.VMEM((LOW * SPACE, LOW), jnp.float32),
            pltpu.VMEM((2 * ROOM * 2 * HIGH, LOW), jnp.float32),
            pltpu.VMEM((LOW // 8, 2 * TILES, 8, LOW), jnp.float32),
            pltpu.VMEM((LOW // 8, 8, LOW), jnp.int32),
            pltpu.VMEM((TILES, sectors, LOW), jnp.float32),
            pltpu.SemaphoreType.DMA((groups,)),
            pltpu.SemaphoreType.DMA,
            pltpu.SemaphoreType.DMA,
        ],
        compiler_params=pltpu.CompilerParams(vmem_limit_bytes=58 << 20),
    )(
        place, data, scale, jnp.asarray(spread, jnp.bfloat16), jnp.asarray(first), jnp.asarray(wave),
        sector_len,
    )


def permute_kernel(order_ref, rows_in, rows_out):
    def step(slot, carry):
        rows_out[pl.ds(order_ref[slot], 1), :] = rows_in[pl.ds(slot, 1), :]
        return carry

    lax.fori_loop(0, rows_in.shape[0], step, 0, unroll=8)


def sort_orders(orders, rows):
    whole = pl.BlockSpec(rows.shape, lambda i, order: (0, 0))
    return pl.pallas_call(
        permute_kernel,
        grid_spec=pltpu.PrefetchScalarGridSpec(
            num_scalar_prefetch=1, grid=(1,), in_specs=[whole], out_specs=whole
        ),
        out_shape=jax.ShapeDtypeStruct(rows.shape, jnp.float32),
        compiler_params=pltpu.CompilerParams(vmem_limit_bytes=32 << 20),
    )(orders, rows)


def split_dot(left, right):
    left_upper, left_lower = halves(left)
    right_upper, right_lower = halves(right)
    return jnp.dot(
        jnp.concatenate([left_upper, left_upper, left_lower], axis=1),
        jnp.concatenate([right_upper, right_lower, right_upper], axis=0),
        preferred_element_type=jnp.float32,
    )


def member_of(start, end, base, count):
    place = lax.broadcasted_iota(jnp.int32, (start.shape[0], count), 1) + base
    pixel = (place % LOW) * HIGH + place // LOW
    return (pixel >= start) & (pixel < end)


def synthesis_kernel(
    channels, shifts, real_ref, imag_ref, d_ref, e_ref, tc_ref, ts_ref, start_ref, end_ref,
    map_ref, moment_ref, z_ref, m_ref, p_ref,
):
    first = split_dot(d_ref[...], jnp.concatenate([real_ref[0], imag_ref[0]], axis=0))
    cos_turn = tc_ref[...]
    sin_turn = ts_ref[...]
    for c in range(channels):
        real = first[:HIGH, c * LOW : (c + 1) * LOW]
        imag = first[HIGH:, c * LOW : (c + 1) * LOW]
        z_ref[c * HIGH : (c + 1) * HIGH, :LOW] = real * cos_turn - imag * sin_turn
        z_ref[c * HIGH : (c + 1) * HIGH, LOW:] = real * sin_turn + imag * cos_turn
    m_ref[...] = split_dot(z_ref[...], e_ref[...])
    for x2 in range(HIGH):
        map_ref[0, :, x2 * LOW : (x2 + 1) * LOW] = m_ref[pl.ds(x2, channels, stride=HIGH), :]
    p_ref[...] = jnp.zeros_like(p_ref)
    start = start_ref[0]
    end = end_ref[0]
    total = jnp.zeros((2 * shifts * GROUP_ROWS, start.shape[0]), jnp.float32)
    for chunk in range(PIX // CHUNK):
        base = chunk * CHUNK
        values = map_ref[0, :, base : base + CHUNK]
        twice = jnp.concatenate([values, values], axis=0)
        for d in range(shifts):
            p_ref[d * GROUP_ROWS : d * GROUP_ROWS + channels, :] = (
                values * twice[d : d + channels]
            )
        product = p_ref[...]
        upper, lower = halves(product)
        member = jnp.where(member_of(start, end, base, CHUNK), 1.0, 0.0).astype(jnp.bfloat16)
        total += lax.dot_general(
            jnp.concatenate([upper, lower], axis=0), member,
            (((1,), (1,)), ((), ())), preferred_element_type=jnp.float32,
        )
    half = shifts * GROUP_ROWS
    moment_ref[0] = total[:half] + total[half:]


def solve_kernel(channels, cov_ref, len_ref, w_ref):
    scale = 1.0 / len_ref[...].astype(jnp.float32)

    def entry(a, b):
        shift = (b - a) % channels
        row = a
        if shift > channels // 2:
            shift, row = channels - shift, b
        return cov_ref[pl.ds(shift * channels + row, 1), :] * scale

    full = {(a, b): entry(a, b) for a in range(channels) for b in range(a, channels)}
    trace = full[0, 0]
    for a in range(1, channels):
        trace = trace + full[a, a]
    ridge = trace * (RIDGE_FACTOR / channels)
    for a in range(channels):
        full[a, a] = full[a, a] + ridge
    rhs = [jnp.ones_like(scale) for _ in range(channels)]
    inverse = []
    for a in range(channels):
        inverse.append(1.0 / full[a, a])
        for b in range(a + 1, channels):
            factor = full[a, b] * inverse[a]
            for c in range(b, channels):
                full[b, c] = full[b, c] - factor * full[a, c]
            rhs[b] = rhs[b] - factor * rhs[a]
    solved = [None] * channels
    for a in reversed(range(channels)):
        value = rhs[a]
        for b in range(a + 1, channels):
            value = value - full[a, b] * solved[b]
        solved[a] = value * inverse[a]
    total = solved[0]
    for a in range(1, channels):
        total = total + solved[a]
    for a in range(channels):
        w_ref[pl.ds(a, 1), :] = solved[a] / total


def general_combine_kernel(map_ref, w_ref, start_ref, end_ref, out_ref):
    start = start_ref[0]
    end = end_ref[0]
    weights = w_ref[0]
    upper, middle = halves(weights)
    lower = weights - upper.astype(jnp.float32) - middle.astype(jnp.float32)
    pieces = jnp.concatenate([upper, middle, lower.astype(jnp.bfloat16)], axis=1)
    for chunk in range(PIX // CHUNK):
        base = chunk * CHUNK
        member = jnp.where(member_of(start, end, base, CHUNK), 1.0, 0.0).astype(jnp.bfloat16)
        pixel_weights = jnp.dot(
            pieces, jnp.concatenate([member, member, member], axis=0),
            preferred_element_type=jnp.float32,
        )
        out_ref[0, :, base : base + CHUNK] = jnp.sum(
            pixel_weights * map_ref[0, :, base : base + CHUNK], axis=0, keepdims=True
        )


def angles(left, right, period):
    phase = left[:, None] * right[None, :] % period
    turned = phase.astype(jnp.float32) * (TWO_PI / period)
    return jnp.cos(turned), jnp.sin(turned)


def synthesize(real, imag, channels, cycles, sector_len):
    order_count = real.shape[0]
    digits = order_count // LOW
    sectors = sector_len.shape[1]
    weight = jnp.where(lax.iota(jnp.int32, order_count) == 0, 1.0, 2.0).astype(jnp.float32)

    def by_cycle(rows):
        rows = (rows * weight[:, None]).reshape(digits, LOW, channels, cycles)
        return rows.transpose(3, 0, 2, 1).reshape(cycles, digits, channels * LOW)

    x_low = lax.iota(jnp.int32, HIGH)
    m_low = lax.iota(jnp.int32, LOW)
    cos_d, sin_d = angles(x_low, lax.iota(jnp.int32, digits), HIGH)
    first = jnp.concatenate(
        [jnp.concatenate([cos_d, -sin_d], 1), jnp.concatenate([sin_d, cos_d], 1)], 0
    )
    cos_t, sin_t = angles(x_low, m_low, PIX)
    cos_e, sin_e = angles(m_low, m_low, LOW)
    second = jnp.concatenate([cos_e, -sin_e], 0)
    upto = lax.iota(jnp.int32, sectors)
    ends = jnp.sum(jnp.where(upto[:, None] >= upto, sector_len[:, None, :], 0), axis=2)
    starts = (ends - sector_len)[:, :, None]
    ends = ends[:, :, None]
    shifts = channels // 2 + 1
    half = shifts * GROUP_ROWS

    def fixed(array):
        return pl.BlockSpec(array.shape, lambda i: (0, 0))

    def each(rows, columns):
        return pl.BlockSpec((1, rows, columns), lambda i: (i, 0, 0))

    maps, moments = pl.pallas_call(
        functools.partial(synthesis_kernel, channels, shifts),
        grid=(cycles,),
        in_specs=[
            each(digits, channels * LOW), each(digits, channels * LOW), fixed(first), fixed(second), fixed(cos_t),
            fixed(sin_t), each(sectors, 1), each(sectors, 1),
        ],
        out_specs=[each(channels, PIX), each(half, sectors)],
        out_shape=[
            jax.ShapeDtypeStruct((cycles, channels, PIX), jnp.float32),
            jax.ShapeDtypeStruct((cycles, half, sectors), jnp.float32),
        ],
        scratch_shapes=[
            pltpu.VMEM((channels * HIGH, 2 * LOW), jnp.float32),
            pltpu.VMEM((channels * HIGH, LOW), jnp.float32),
            pltpu.VMEM((half, CHUNK), jnp.float32),
        ],
        compiler_params=pltpu.CompilerParams(vmem_limit_bytes=48 << 20),
    )(by_cycle(real), by_cycle(imag), first, second, cos_t, sin_t, starts, ends)
    covariance = moments.reshape(cycles, shifts, GROUP_ROWS, sectors)[:, :, :channels]
    covariance = covariance.transpose(1, 2, 0, 3).reshape(shifts * channels, cycles * sectors)
    weights = pl.pallas_call(
        functools.partial(solve_kernel, channels),
        out_shape=jax.ShapeDtypeStruct((channels, cycles * sectors), jnp.float32),
    )(covariance, sector_len.reshape(1, cycles * sectors))
    weights = weights.reshape(channels, cycles, sectors).transpose(1, 0, 2)
    combined = pl.pallas_call(
        general_combine_kernel,
        grid=(cycles,),
        in_specs=[each(channels, PIX), each(channels, sectors), each(sectors, 1), each(sectors, 1)],
        out_specs=each(1, PIX),
        out_shape=jax.ShapeDtypeStruct((cycles, 1, PIX), jnp.float32),
    )(maps, weights, starts, ends)
    return combined.reshape(cycles, HIGH, LOW).transpose(0, 2, 1).reshape(cycles, PIX)


def general_device(coeffs, legendre, m_order, sector_len):
    slot_count, north_count, degree_count = legendre.shape[1:]
    order_count = m_order.shape[0]
    group_count = lax.axis_size("chan")
    block_count = lax.axis_size("blk")
    device_count = group_count * block_count
    channels = coeffs.shape[0] * group_count
    cycles = sector_len.shape[0]
    first_slot = (lax.axis_index("blk") * group_count + lax.axis_index("chan")) * slot_count
    orders = lax.dynamic_slice_in_dim(m_order, first_slot, slot_count, 0)
    operator = legendre[0]
    degree = order_count - degree_count + lax.iota(jnp.int32, degree_count)
    valid_mask = degree[None, :] >= orders[:, None]
    parity = (degree[None, :] + orders[:, None]) % 2
    keep = jnp.stack([valid_mask & (parity == 0), valid_mask & (parity == 1)])
    zero_value = jnp.zeros((), coeffs.dtype)
    order_joined = (
        m_order.reshape(block_count, group_count, slot_count).transpose(1, 0, 2).reshape(-1)
    )
    received = []
    for p in range(2):
        part = lax.all_to_all(coeffs[:, p], "chan", split_axis=1, concat_axis=0, tiled=True)
        masked = jnp.where(keep[:, None], part[None], zero_value)
        sums = jnp.einsum("ecsl,srl->secr", masked, operator, preferred_element_type=jnp.float32)
        even_sum, odd_sum = sums[:, 0], sums[:, 1]
        spectra = jnp.concatenate([even_sum + odd_sum, even_sum - odd_sum], axis=2)
        spectra = spectra.reshape(slot_count, channels, device_count, cycles)
        spectra = spectra.transpose(2, 0, 1, 3).reshape(
            device_count, slot_count, channels * cycles
        )
        spectra = lax.all_to_all(
            spectra, ("chan", "blk"), split_axis=0, concat_axis=0, tiled=True
        )
        received.append(
            sort_orders(order_joined, spectra.reshape(order_count, channels * cycles))
        )
    return synthesize(received[0], received[1], channels, cycles, sector_len)


def per_device(coeffs, legendre, m_order, sector_len):
    slots, north, _ = legendre.shape[1:]
    groups = lax.axis_size("chan")
    blocks = lax.axis_size("blk")
    channels = coeffs.shape[0] * groups
    cycles = sector_len.shape[0]
    fits = (
        slots % CHUNK_SLOTS == 0 and CHUNK_SLOTS < slots <= LOW and blocks == 8 and cycles * blocks == LOW
        and 2 * north == groups * LOW and channels == 12
    )
    if not fits:
        return general_device(coeffs, legendre, m_order, sector_len)
    data, scale, place = exchange(coeffs, legendre[0], m_order, groups, blocks)
    return combine(data, scale, place.reshape(-1), sector_len, channels, groups)


def solution(mesh):
    placed = (
        P("chan", None, "blk", None),
        P("chan", "blk", None, None),
        P(),
        P(("chan", "blk"), None),
    )
    return jax.shard_map(
        per_device, mesh=mesh, in_specs=placed, out_specs=P(("chan", "blk"), None), check_vma=False
    )
```

```python
import functools

import jax
import jax.numpy as jnp
import numpy as np
from jax import lax
from jax.experimental import pallas as pl
from jax.experimental.pallas import tpu as pltpu
from jax.sharding import PartitionSpec as P

PIX = 8192
LOW = 128
HIGH = PIX // LOW
RIDGE_FACTOR = 0.05
TWO_PI = 6.283185307179586
CHUNK = 1024
GROUP_ROWS = 16
MESH = pl.DeviceIdType.MESH
CHUNK_SLOTS = 16
LOAD_SLOTS = 4
LOAD_BUFFERS = 3
CODE_MAX = 32767.0


def block_transpose(values, lane):
    values = list(values)
    for bit in (1, 2, 4):
        upper = (lane // 16) % (2 * bit) >= bit
        for i in range(8):
            if i & bit:
                continue
            a, b = values[i], values[i | bit]
            values[i] = jnp.where(upper, pltpu.roll(b, 16 * bit, 1), a)
            values[i | bit] = jnp.where(upper, b, pltpu.roll(a, LOW - 16 * bit, 1))
    return values


def tile_rows(channels):
    return [
        [(c, 0) for c in range(8)],
        [(c, 1) for c in range(8)],
        [(c, 0) for c in range(8, channels)] + [(c, 1) for c in range(8, channels)],
    ]


def exchange_kernel(
    groups, blocks, order_ref, order_rows, coeffs, legendre, data_out, scale_out, place_out,
    rbuf, lbuf, valid_ref, sign_ref, xs, sp, msg, inverse, scl,
    csend, crecv, lsem, dsend, drecv, ssend, srecv,
):
    chunks, _, local_channels, parts, size, degrees = rbuf.shape
    channels = groups * local_channels
    rows = channels * parts
    slots = chunks * size
    tiles = degrees // LOW
    devices = groups * blocks
    g = lax.axis_index("chan")
    b = lax.axis_index("blk")
    me = g * blocks + b

    half_blocks = blocks // 2
    half_devices = devices // 2
    my_half = b // half_blocks

    def near(i):
        at = lax.rem(b + i // groups, half_blocks)
        return lax.rem(g + i % groups, groups), my_half * half_blocks + at

    def far(i):
        at = lax.rem(b + i // groups, half_blocks)
        return lax.rem(g + i % groups, groups), (1 - my_half) * half_blocks + at

    barrier = pltpu.get_barrier_semaphore()

    def to_all(act):
        def to_far(i, carry):
            act(far(i))
            return carry

        def to_near(i, carry):
            act(near(i))
            return carry

        lax.fori_loop(0, half_devices, to_far, 0)
        lax.fori_loop(1, half_devices, to_near, 0)

    def greet(to):
        pl.semaphore_signal(barrier, inc=1, device_id=to, device_id_type=MESH)

    to_all(greet)

    def load(t):
        return pltpu.make_async_copy(
            legendre.at[pl.ds(t * LOAD_SLOTS, LOAD_SLOTS)],
            lbuf.at[lax.rem(t, LOAD_BUFFERS)], lsem.at[lax.rem(t, LOAD_BUFFERS)],
        )

    for t in range(LOAD_BUFFERS):
        load(t).start()
    pl.semaphore_wait(barrier, devices - 1)

    def start_coeffs(j):
        for down, right in ((1, 1), (0, 1), (1, 0)):
            to = lax.rem(g // 2 + down, 2) * 2 + lax.rem(g + right, 2)
            pltpu.make_async_remote_copy(
                src_ref=coeffs.at[:, :, pl.ds(to * slots + j * size, size), :],
                dst_ref=rbuf.at[j, g],
                send_sem=csend, recv_sem=crecv.at[j],
                device_id=(to, b), device_id_type=MESH,
            ).start()
        pltpu.make_async_copy(
            coeffs.at[:, :, pl.ds(g * slots + j * size, size), :], rbuf.at[j, g], crecv.at[j]
        ).start()

    for j in range(chunks):
        start_coeffs(j)
    degree = lax.broadcasted_iota(jnp.int32, (1, degrees), 1) + order_ref.shape[0] - degrees
    first_slot = (b * groups + g) * slots

    def masks(s, carry):
        order = order_ref[first_slot + s]
        keep = jnp.where(degree >= order, 1.0, 0.0)
        at = pl.ds(s, 1)
        valid_ref[at, :] = keep
        sign_ref[at, :] = jnp.where((degree + order) % 2 == 0, keep, -keep)
        return carry

    lax.fori_loop(0, slots, masks, 0)
    order = order_rows[...]
    place = jnp.bitwise_and(order, LOW - 1) * (order_ref.shape[0] // LOW)
    place_out[...] = (place + lax.shift_right_logical(order, 7)) * 8
    lane = lax.broadcasted_iota(jnp.int32, (size, LOW), 1)
    scale_lane = lax.broadcasted_iota(jnp.int32, (1, LOW), 1)
    layout = tile_rows(channels)

    def send_near(first, count):
        def send(i, carry):
            to = near(i)
            pltpu.make_async_remote_copy(
                src_ref=msg.at[pl.ds(first, count), to[0] * blocks + to[1]],
                dst_ref=data_out.at[me, pl.ds(first, count)],
                send_sem=dsend, recv_sem=drecv, device_id=to, device_id_type=MESH,
            ).start()
            return carry

        lax.fori_loop(1, half_devices, send, 0)

    def send_scale(to):
        pltpu.make_async_remote_copy(
            src_ref=scl, dst_ref=scale_out.at[me],
            send_sem=ssend, recv_sem=srecv, device_id=to, device_id_type=MESH,
        ).start()

    def chunk(j, last):
        pltpu.make_async_copy(rbuf.at[j], rbuf.at[j], crecv.at[j]).wait()
        if last:
            send_near(0, chunks - 1)
        for q in range(groups):
            for c in range(local_channels):
                for p in range(parts):
                    row = ((q * local_channels + c) * parts + p) * size
                    wide = rbuf[j, q, c, p].astype(jnp.float32)
                    for t in range(tiles):
                        xs[t, row : row + size, :] = wide[:, t * LOW : (t + 1) * LOW]

        def step(u, carry):
            t = j * (size // LOAD_SLOTS) + u
            load(t).wait()
            for v in range(LOAD_SLOTS):
                s = u * LOAD_SLOTS + v
                x = jnp.concatenate(
                    [xs[i, pl.ds(s, rows, stride=size), :] for i in range(tiles)], axis=1
                )
                at = pl.ds(j * size + s, 1)
                both = jnp.concatenate([x * valid_ref[at, :], x * sign_ref[at, :]], axis=0)
                sums = lax.dot_general(
                    both.astype(jnp.bfloat16), lbuf[lax.rem(t, LOAD_BUFFERS), v],
                    (((1,), (1,)), ((), ())), preferred_element_type=jnp.float32,
                )
                for i in range(sp.shape[0]):
                    sp[i, pl.ds(s, 2 * rows, stride=size), :] = sums[:, i * LOW : (i + 1) * LOW]

            @pl.when(t + LOAD_BUFFERS < slots // LOAD_SLOTS)
            def _():
                load(t + LOAD_BUFFERS).start()

            return carry

        lax.fori_loop(0, size // LOAD_SLOTS, step, 0)

        def piece(half, side, c, p):
            row = (half * rows + c * parts + p) * size
            return sp[side, row : row + size, :]

        scales = scl[...]
        for c in range(channels):
            top = jnp.abs(piece(0, 0, c, 0))
            for half in range(2):
                for side in range(sp.shape[0]):
                    for p in range(parts):
                        top = jnp.maximum(top, jnp.abs(piece(half, side, c, p)))
            top = jnp.maximum(jnp.max(top, keepdims=True), 1e-30)
            unit = (top * (1.0078125 / CODE_MAX)).astype(jnp.bfloat16).astype(jnp.float32)
            inverse[c] = jnp.broadcast_to(1.0 / unit, (size, LOW))
            scales = jnp.where(scale_lane == j * 16 + c, unit, scales)
        scl[...] = scales
        if last:
            to_all(send_scale)
        for half in range(2):
            for side in range(sp.shape[0]):
                first = (half * sp.shape[0] + side) * blocks
                for tile, members in enumerate(layout):
                    values = block_transpose(
                        [piece(half, side, c, p) * inverse[c] for c, p in members], lane
                    )
                    for k in range(blocks):
                        msg[j, first + k, tile] = jnp.round(values[k]).astype(jnp.int16)

        def send(i, carry):
            to = far(i)
            pltpu.make_async_remote_copy(
                src_ref=msg.at[j, to[0] * blocks + to[1]], dst_ref=data_out.at[me, j],
                send_sem=dsend, recv_sem=drecv, device_id=to, device_id_type=MESH,
            ).start()
            return carry

        lax.fori_loop(0, half_devices, send, 0)
        if last:
            send_near(j, 1)
        pltpu.make_async_copy(msg.at[j, me], data_out.at[me, j], drecv).start()

    def early(j, carry):
        chunk(j, False)
        return carry

    scl[...] = jnp.zeros_like(scl)
    lax.fori_loop(0, chunks - 1, early, 0)
    chunk(chunks - 1, True)
    pltpu.make_async_copy(scl, scale_out.at[me], srecv).start()

    def settle(ref, sem):
        pltpu.make_async_copy(ref, ref, sem).wait()

    settle(rbuf.at[:, pl.ds(0, groups - 1)], csend)
    settle(msg.at[:, pl.ds(0, devices - 1)], dsend)
    settle(scale_out.at[pl.ds(0, devices - 1)], ssend)
    settle(data_out, drecv)
    settle(scale_out, srecv)


def exchange(coeffs, operator, m_order, groups, blocks):
    local_channels, parts, _, degrees = coeffs.shape
    slots, north, _ = operator.shape
    channels = groups * local_channels
    devices = groups * blocks
    size = CHUNK_SLOTS
    chunks = slots // size
    rows = channels * parts
    sides = north // LOW
    anywhere = pl.BlockSpec(memory_space=pl.ANY)
    vmem = pl.BlockSpec(memory_space=pltpu.VMEM)
    dma = pltpu.SemaphoreType.DMA
    return pl.pallas_call(
        functools.partial(exchange_kernel, groups, blocks),
        in_specs=[pl.BlockSpec(memory_space=pltpu.SMEM), vmem, anywhere, anywhere],
        out_specs=[anywhere, anywhere, vmem],
        out_shape=[
            jax.ShapeDtypeStruct((devices, chunks, 3, size, LOW), jnp.int16),
            jax.ShapeDtypeStruct((devices, 1, LOW), jnp.float32),
            jax.ShapeDtypeStruct((m_order.shape[0] // LOW, LOW), jnp.int32),
        ],
        scratch_shapes=[
            pltpu.VMEM((chunks, groups, local_channels, parts, size, degrees), jnp.bfloat16),
            pltpu.VMEM((LOAD_BUFFERS, LOAD_SLOTS, north, degrees), jnp.bfloat16),
            pltpu.VMEM((slots, degrees), jnp.float32),
            pltpu.VMEM((slots, degrees), jnp.float32),
            pltpu.VMEM((degrees // LOW, rows * size, LOW), jnp.float32),
            pltpu.VMEM((sides, 2 * rows * size, LOW), jnp.float32),
            pltpu.VMEM((chunks, devices, 3, size, LOW), jnp.int16),
            pltpu.VMEM((channels, size, LOW), jnp.float32),
            pltpu.VMEM((1, LOW), jnp.float32),
            dma, dma((chunks,)), dma((LOAD_BUFFERS,)), dma, dma, dma, dma,
        ],
        compiler_params=pltpu.CompilerParams(
            collective_id=0, has_side_effects=True, vmem_limit_bytes=58 << 20
        ),
    )(m_order, m_order.reshape(-1, LOW), coeffs, operator)


def halves(value):
    upper = value.astype(jnp.bfloat16)
    return upper, (value - upper.astype(jnp.float32)).astype(jnp.bfloat16)


def synthesis_tables(order_count):
    digits = order_count // LOW
    order = np.arange(LOW)[:, None, None] + LOW * np.arange(digits)[None, None, :]
    angle = order * np.arange(HIGH)[None, :, None] % PIX * (2.0 * np.pi / PIX)
    weight = np.where(order == 0, 1.0, 2.0)
    cos, sin = weight * np.cos(angle), weight * np.sin(angle)
    turn = np.stack([np.concatenate([cos, -sin], 2), np.concatenate([sin, cos], 2)], 2)
    turn = turn.reshape(LOW, 2 * HIGH, 2 * digits).astype(np.float32)
    turn_upper = turn.astype(jnp.bfloat16)
    turn_lower = (turn - turn_upper.astype(np.float32)).astype(jnp.bfloat16)
    first = np.concatenate([turn_upper, turn_upper, turn_lower], 2)
    angle = np.arange(LOW)[:, None] * np.arange(LOW)[None, :] % LOW * (2.0 * np.pi / LOW)
    wave = np.concatenate([np.cos(angle), -np.sin(angle)], 1).astype(np.float32)
    wave_upper = wave.astype(jnp.bfloat16)
    wave_lower = (wave - wave_upper.astype(np.float32)).astype(jnp.bfloat16)
    return first, np.concatenate([wave_upper, wave_lower], 0)


def pair_place(a, b):
    if b < 8:
        shift = b - a
        if shift > 4:
            shift, a = 8 - shift, b
        return (shift, (a - 1) % 8) if shift == 2 else (shift, a)
    if a < 8:
        tile, move = {0: (5, 0), 1: (6, 3), 2: (7, 3), 3: (8, 1)}[(b - 8 - a) % 4]
        return tile, (a - move) % 8
    a, b = a - 8, b - 8
    shift = b - a
    if shift == 2:
        return 10, a
    return 9, {0: a, 1: 4 + a, 3: 4 + b}[shift]


TILES = 11
ROOM = LOW + 8
SPACE = HIGH + 8


def combine_kernel(
    channels, groups, place_ref, data_any, scale_any, spread, first_any, wave, lens, out,
    data, scale, first, spare, order_rows, late, weighed, turned, partial, held, cov,
    data_sem, scale_sem, first_sem,
):
    sources, chunks, _, size, _ = data.shape
    slots = chunks * size
    blocks = sources // groups
    digits = place_ref.shape[0] // LOW
    fetch_scale = pltpu.make_async_copy(scale_any, scale, scale_sem)
    fetch_scale.start()

    def fetch_data(i):
        part = pl.ds(i * blocks, blocks)
        return pltpu.make_async_copy(data_any.at[part], data.at[part], data_sem.at[i])

    for i in range(groups):
        fetch_data(i).start()
    fetch = pltpu.make_async_copy(first_any, first, first_sem)
    fetch.start()
    fetch_scale.wait()

    chunk_lane = lax.broadcasted_iota(jnp.int32, (8, LOW), 1) // 16
    chunk_lane = chunk_lane == lax.broadcasted_iota(jnp.int32, (8, LOW), 0)

    def gather(src, carry):
        @pl.when(lax.rem(src, blocks) == 0)
        def _():
            fetch_data(src // blocks).wait()

        units = jnp.where(chunk_lane, scale[src], 0.0).astype(jnp.bfloat16)
        unit = jnp.dot(units, spread[...], preferred_element_type=jnp.float32)
        for j in range(chunks):
            for t in range(3):
                value = data[src, j, t].astype(jnp.float32)
                value = value * unit[j : j + 1, t * LOW : (t + 1) * LOW]
                spare[pl.ds(j * size * 8 + t, size, stride=8), :] = value
        base = (lax.rem(src, blocks) * groups + src // blocks) * slots

        def move(s, carry):
            to = pl.multiple_of(place_ref[base + s], 8)
            order_rows[pl.ds(to, 8), :] = spare[pl.ds(pl.multiple_of(s * 8, 8), 8), :]
            return carry

        return lax.fori_loop(0, slots, move, carry, unroll=slots)

    lax.fori_loop(0, sources, gather, 0)
    fetch.wait()
    lane_d = lax.broadcasted_iota(jnp.int32, (digits, LOW), 1)
    wide = ROOM * 2 * HIGH

    def turn(l, carry):
        t0, t1, t2 = (
            order_rows[pl.ds(l * (digits * 8) + t, digits, stride=8), :] for t in range(3)
        )
        t3 = pltpu.roll(t2, LOW // 2, 1)
        real = jnp.where(lane_d < LOW // 2, t2, t3)
        imag = jnp.where(lane_d < LOW // 2, t3, t2)
        x = jnp.concatenate(
            [jnp.concatenate([t0, real], 1), jnp.concatenate([t1, imag], 1)], 0
        )
        upper, lower = halves(x)
        y = jnp.dot(
            first[l], jnp.concatenate([upper, lower, upper], 0), preferred_element_type=jnp.float32
        )
        turned[pl.ds(l, 2 * HIGH, stride=ROOM), :] = y[:, :LOW]
        turned[pl.ds(wide + l, 2 * HIGH, stride=ROOM), :] = y[:, LOW:]
        return carry

    lax.fori_loop(0, LOW, turn, 0, unroll=32)

    early = HIGH // 2
    second = early * LOW

    def spin_into(maps, x, place):
        def part(i):
            at = pl.multiple_of((2 * x + i) * ROOM, 8)
            return jnp.concatenate(
                [turned[pl.ds(at, LOW), :], turned[pl.ds(wide + at, LOW), :]], 1
            )

        upper, lower = halves(jnp.concatenate([part(0), part(1)], 0))
        main = jnp.dot(wave[...], upper, preferred_element_type=jnp.float32)
        rest = jnp.dot(wave[:LOW], lower, preferred_element_type=jnp.float32)
        value = main[:LOW] + main[LOW:] + rest
        maps[pl.ds(pl.multiple_of(place * LOW, LOW), LOW), :] = value[:, :LOW]
        maps[pl.ds(pl.multiple_of(second + place * LOW, LOW), LOW), :] = value[:, LOW:]

    def spin(x, carry):
        spin_into(order_rows, x, x)
        return carry

    lax.fori_loop(0, early, spin, 0, unroll=16)

    cycles, sectors = lens.shape
    copies = lax.broadcasted_iota(jnp.int32, (cycles, LOW), 1) % cycles
    copies = copies == lax.broadcasted_iota(jnp.int32, (cycles, LOW), 0)
    copies = jnp.where(copies, 1.0, 0.0).astype(jnp.bfloat16)

    def spread_out(values):
        return lax.dot_general(
            values.astype(jnp.float32).astype(jnp.bfloat16), copies, (((0,), (0,)), ((), ())),
            preferred_element_type=jnp.float32,
        )

    length = 128.0 * spread_out(lax.shift_right_logical(lens[...], 7))
    length = length + spread_out(jnp.bitwise_and(lens[...], 127))
    length = length.astype(jnp.int32)
    ends = []
    for k in range(sectors):
        ends.append(length[k : k + 1] + ends[-1] if k else length[:1])
    lane = lax.broadcasted_iota(jnp.int32, (8, LOW), 1)
    sub = lax.broadcasted_iota(jnp.int32, (8, LOW), 0)

    def block(j):
        begin = (j * 8 + sub) * HIGH
        sector = jnp.zeros((8, LOW), jnp.int32)
        after = jnp.full((8, LOW), 2 * PIX, jnp.int32)
        for k in range(sectors):
            past = ends[k] <= begin
            sector = sector + jnp.where(past, 1, 0)
            after = jnp.minimum(after, jnp.where(past, 2 * PIX, ends[k]))
        return sector, after - begin

    def pair(maps, j, place):
        at = pl.multiple_of(place * LOW + j * 8, 8)
        return maps[pl.ds(at, 8), :], maps[pl.ds(second + at, 8), :]

    def add(limit, x, values, acc):
        a, b = values
        ended = limit == x
        a1, a3, a4 = (pltpu.roll(a, LOW - 16 * d, 1) for d in (1, 3, 4))
        b1, b2 = (pltpu.roll(b, LOW - 16 * d, 1) for d in (1, 2))
        bb = jnp.where(lane < LOW // 2, b, b1)
        left = [a, a, a3, a, a, a, a3, a3, b, b, b]
        right = [a, a1, a1, a3, a4, b, b, b1, a1, bb, b2]
        head = [jnp.where(ended, acc[i], acc[TILES + i]) for i in range(TILES)]
        return [acc[i] + left[i] * right[i] for i in range(TILES)] + head

    def first_half(j, carry):
        _, limit = block(j)
        acc = [jnp.zeros((8, LOW), jnp.float32)] * (2 * TILES)
        share = early // (LOW // 8)
        for x in range(early):
            if x < share:
                spin_into(late, early + j * share + x, j * share + x)
            acc = add(limit, x, pair(order_rows, j, x), acc)
        for i in range(2 * TILES):
            partial[j, i] = acc[i]
        return carry

    lax.fori_loop(0, LOW // 8, first_half, 0)

    def moments(j, carry):
        sector, limit = block(j)
        acc = [partial[j, i] for i in range(2 * TILES)]
        for x in range(early):
            acc = add(limit, early + x, pair(late, j, x), acc)
        for i in range(TILES):
            head = jnp.where(limit >= HIGH, acc[i], acc[TILES + i])
            partial[j, i] = head
            partial[j, TILES + i] = acc[i] - head
        held[j] = sector
        return carry

    lax.fori_loop(0, LOW // 8, moments, 0)

    def collect(k, carry):
        acc = [jnp.zeros((8, LOW), jnp.float32)] * TILES
        for j in range(LOW // 8):
            here = held[j] == k
            there = held[j] == k - 1
            for i in range(TILES):
                tail = jnp.where(there, partial[j, TILES + i], 0.0)
                acc[i] = acc[i] + jnp.where(here, partial[j, i], tail)
        for i in range(TILES):
            cov[i, pl.ds(k, 1), :] = jnp.sum(acc[i], axis=0, keepdims=True)
        return carry

    lax.fori_loop(0, sectors, collect, 0, unroll=2)
    share = 1.0 / length.astype(jnp.float32)

    def entry(a, b):
        tile, group = pair_place(a, b)
        value = cov[tile] * share
        return pltpu.roll(value, LOW - 16 * group, 1) if group else value

    full = {(a, b): entry(a, b) for a in range(channels) for b in range(a, channels)}
    trace = full[0, 0]
    for a in range(1, channels):
        trace = trace + full[a, a]
    ridge = trace * (RIDGE_FACTOR / channels)
    for a in range(channels):
        full[a, a] = full[a, a] + ridge
    rhs = [jnp.ones_like(ridge) for _ in range(channels)]
    inverse = []
    for a in range(channels):
        inverse.append(1.0 / full[a, a])
        for b in range(a + 1, channels):
            factor = full[a, b] * inverse[a]
            for c in range(b, channels):
                full[b, c] = full[b, c] - factor * full[a, c]
            rhs[b] = rhs[b] - factor * rhs[a]
    solved = [None] * channels
    for a in reversed(range(channels)):
        value = rhs[a]
        for b in range(a + 1, channels):
            value = value - full[a, b] * solved[b]
        solved[a] = value * inverse[a]
    total = solved[0]
    for a in range(1, channels):
        total = total + solved[a]
    near = jnp.zeros_like(total)
    far = jnp.zeros_like(total)
    group = lax.broadcasted_iota(jnp.int32, total.shape, 1) // 16
    for a in range(channels):
        weight = solved[a] / total
        place = a % 8
        moved = pltpu.roll(weight, 16 * place, 1) if place else weight
        if a < 8:
            near = jnp.where(group == place, moved, near)
        else:
            far = jnp.where(group == place, moved, far)
    cov[0] = near
    cov[1] = far

    def apply(j, carry):
        sector, limit = block(j)
        picked = [jnp.zeros((8, LOW), jnp.float32) for _ in range(4)]
        for k in range(sectors):
            near_k = cov[0, k : k + 1, :]
            far_k = cov[1, k : k + 1, :]
            here = sector == k
            there = sector + 1 == k
            picked[0] = jnp.where(here, near_k, picked[0])
            picked[1] = jnp.where(here, far_k, picked[1])
            picked[2] = jnp.where(there, near_k, picked[2])
            picked[3] = jnp.where(there, far_k, picked[3])

        for x in range(HIGH):
            a, b = pair(order_rows, j, x) if x < early else pair(late, j, x - early)
            inside = limit > x
            value = jnp.where(inside, picked[0], picked[2]) * a
            value = value + jnp.where(inside, picked[1], picked[3]) * b
            weighed[pl.ds(j * 8 * SPACE + x, 8, stride=SPACE), :] = value
        return carry

    lax.fori_loop(0, LOW // 8, apply, 0)
    pick = lax.broadcasted_iota(jnp.int32, (16, 2 * LOW), 1) % 16
    pick = jnp.where(pick == lax.broadcasted_iota(jnp.int32, (16, 2 * LOW), 0), 1.0, 0.0)
    pick = pick.astype(jnp.bfloat16)
    for x in range(0, PIX, 256):
        upper, lower = halves(
            jnp.concatenate(
                [
                    weighed[y * SPACE : y * SPACE + HIGH, :]
                    for y in range(x // HIGH, (x + 256) // HIGH)
                ],
                0,
            )
        )
        out[:, x : x + 256] = lax.dot_general(
            pick, jnp.concatenate([upper, lower], 1), (((1,), (1,)), ((), ())),
            preferred_element_type=jnp.float32,
        )


def combine(data, scale, place, sector_len, channels, groups):
    order_count = place.shape[0]
    cycles, sectors = sector_len.shape
    first, wave = synthesis_tables(order_count)
    spread = np.zeros((16, 3 * LOW), np.float32)
    for tile, members in enumerate(tile_rows(channels)):
        for i, (c, _) in enumerate(members):
            spread[c, tile * LOW + 16 * i : tile * LOW + 16 * i + 16] = 1.0
    spread = np.tile(spread, (8, 1))
    vmem = pl.BlockSpec(memory_space=pltpu.VMEM)
    anywhere = pl.BlockSpec(memory_space=pl.ANY)
    return pl.pallas_call(
        functools.partial(combine_kernel, channels, groups),
        in_specs=[
            pl.BlockSpec(memory_space=pltpu.SMEM), anywhere, anywhere, vmem, anywhere, vmem, vmem,
        ],
        out_specs=vmem,
        out_shape=jax.ShapeDtypeStruct((cycles, PIX), jnp.float32),
        scratch_shapes=[
            pltpu.VMEM(data.shape, jnp.int16),
            pltpu.VMEM(scale.shape, jnp.float32),
            pltpu.VMEM(first.shape, jnp.bfloat16),
            pltpu.VMEM((data.shape[1] * data.shape[3] * 8, LOW), jnp.float32),
            pltpu.VMEM((max(order_count * 8, PIX), LOW), jnp.float32),
            pltpu.VMEM((PIX, LOW), jnp.float32),
            pltpu.VMEM((LOW * SPACE, LOW), jnp.float32),
            pltpu.VMEM((2 * ROOM * 2 * HIGH, LOW), jnp.float32),
            pltpu.VMEM((LOW // 8, 2 * TILES, 8, LOW), jnp.float32),
            pltpu.VMEM((LOW // 8, 8, LOW), jnp.int32),
            pltpu.VMEM((TILES, sectors, LOW), jnp.float32),
            pltpu.SemaphoreType.DMA((groups,)),
            pltpu.SemaphoreType.DMA,
            pltpu.SemaphoreType.DMA,
        ],
        compiler_params=pltpu.CompilerParams(vmem_limit_bytes=58 << 20),
    )(
        place, data, scale, jnp.asarray(spread, jnp.bfloat16), jnp.asarray(first), jnp.asarray(wave),
        sector_len,
    )


def permute_kernel(order_ref, rows_in, rows_out):
    def step(slot, carry):
        rows_out[pl.ds(order_ref[slot], 1), :] = rows_in[pl.ds(slot, 1), :]
        return carry

    lax.fori_loop(0, rows_in.shape[0], step, 0, unroll=8)


def sort_orders(orders, rows):
    whole = pl.BlockSpec(rows.shape, lambda i, order: (0, 0))
    return pl.pallas_call(
        permute_kernel,
        grid_spec=pltpu.PrefetchScalarGridSpec(
            num_scalar_prefetch=1, grid=(1,), in_specs=[whole], out_specs=whole
        ),
        out_shape=jax.ShapeDtypeStruct(rows.shape, jnp.float32),
        compiler_params=pltpu.CompilerParams(vmem_limit_bytes=32 << 20),
    )(orders, rows)


def split_dot(left, right):
    left_upper, left_lower = halves(left)
    right_upper, right_lower = halves(right)
    return jnp.dot(
        jnp.concatenate([left_upper, left_upper, left_lower], axis=1),
        jnp.concatenate([right_upper, right_lower, right_upper], axis=0),
        preferred_element_type=jnp.float32,
    )


def member_of(start, end, base, count):
    place = lax.broadcasted_iota(jnp.int32, (start.shape[0], count), 1) + base
    pixel = (place % LOW) * HIGH + place // LOW
    return (pixel >= start) & (pixel < end)


def synthesis_kernel(
    channels, shifts, real_ref, imag_ref, d_ref, e_ref, tc_ref, ts_ref, start_ref, end_ref,
    map_ref, moment_ref, z_ref, m_ref, p_ref,
):
    first = split_dot(d_ref[...], jnp.concatenate([real_ref[0], imag_ref[0]], axis=0))
    cos_turn = tc_ref[...]
    sin_turn = ts_ref[...]
    for c in range(channels):
        real = first[:HIGH, c * LOW : (c + 1) * LOW]
        imag = first[HIGH:, c * LOW : (c + 1) * LOW]
        z_ref[c * HIGH : (c + 1) * HIGH, :LOW] = real * cos_turn - imag * sin_turn
        z_ref[c * HIGH : (c + 1) * HIGH, LOW:] = real * sin_turn + imag * cos_turn
    m_ref[...] = split_dot(z_ref[...], e_ref[...])
    for x2 in range(HIGH):
        map_ref[0, :, x2 * LOW : (x2 + 1) * LOW] = m_ref[pl.ds(x2, channels, stride=HIGH), :]
    p_ref[...] = jnp.zeros_like(p_ref)
    start = start_ref[0]
    end = end_ref[0]
    total = jnp.zeros((2 * shifts * GROUP_ROWS, start.shape[0]), jnp.float32)
    for chunk in range(PIX // CHUNK):
        base = chunk * CHUNK
        values = map_ref[0, :, base : base + CHUNK]
        twice = jnp.concatenate([values, values], axis=0)
        for d in range(shifts):
            p_ref[d * GROUP_ROWS : d * GROUP_ROWS + channels, :] = (
                values * twice[d : d + channels]
            )
        product = p_ref[...]
        upper, lower = halves(product)
        member = jnp.where(member_of(start, end, base, CHUNK), 1.0, 0.0).astype(jnp.bfloat16)
        total += lax.dot_general(
            jnp.concatenate([upper, lower], axis=0), member,
            (((1,), (1,)), ((), ())), preferred_element_type=jnp.float32,
        )
    half = shifts * GROUP_ROWS
    moment_ref[0] = total[:half] + total[half:]


def solve_kernel(channels, cov_ref, len_ref, w_ref):
    scale = 1.0 / len_ref[...].astype(jnp.float32)

    def entry(a, b):
        shift = (b - a) % channels
        row = a
        if shift > channels // 2:
            shift, row = channels - shift, b
        return cov_ref[pl.ds(shift * channels + row, 1), :] * scale

    full = {(a, b): entry(a, b) for a in range(channels) for b in range(a, channels)}
    trace = full[0, 0]
    for a in range(1, channels):
        trace = trace + full[a, a]
    ridge = trace * (RIDGE_FACTOR / channels)
    for a in range(channels):
        full[a, a] = full[a, a] + ridge
    rhs = [jnp.ones_like(scale) for _ in range(channels)]
    inverse = []
    for a in range(channels):
        inverse.append(1.0 / full[a, a])
        for b in range(a + 1, channels):
            factor = full[a, b] * inverse[a]
            for c in range(b, channels):
                full[b, c] = full[b, c] - factor * full[a, c]
            rhs[b] = rhs[b] - factor * rhs[a]
    solved = [None] * channels
    for a in reversed(range(channels)):
        value = rhs[a]
        for b in range(a + 1, channels):
            value = value - full[a, b] * solved[b]
        solved[a] = value * inverse[a]
    total = solved[0]
    for a in range(1, channels):
        total = total + solved[a]
    for a in range(channels):
        w_ref[pl.ds(a, 1), :] = solved[a] / total


def general_combine_kernel(map_ref, w_ref, start_ref, end_ref, out_ref):
    start = start_ref[0]
    end = end_ref[0]
    weights = w_ref[0]
    upper, middle = halves(weights)
    lower = weights - upper.astype(jnp.float32) - middle.astype(jnp.float32)
    pieces = jnp.concatenate([upper, middle, lower.astype(jnp.bfloat16)], axis=1)
    for chunk in range(PIX // CHUNK):
        base = chunk * CHUNK
        member = jnp.where(member_of(start, end, base, CHUNK), 1.0, 0.0).astype(jnp.bfloat16)
        pixel_weights = jnp.dot(
            pieces, jnp.concatenate([member, member, member], axis=0),
            preferred_element_type=jnp.float32,
        )
        out_ref[0, :, base : base + CHUNK] = jnp.sum(
            pixel_weights * map_ref[0, :, base : base + CHUNK], axis=0, keepdims=True
        )


def angles(left, right, period):
    phase = left[:, None] * right[None, :] % period
    turned = phase.astype(jnp.float32) * (TWO_PI / period)
    return jnp.cos(turned), jnp.sin(turned)


def synthesize(real, imag, channels, cycles, sector_len):
    order_count = real.shape[0]
    digits = order_count // LOW
    sectors = sector_len.shape[1]
    weight = jnp.where(lax.iota(jnp.int32, order_count) == 0, 1.0, 2.0).astype(jnp.float32)

    def by_cycle(rows):
        rows = (rows * weight[:, None]).reshape(digits, LOW, channels, cycles)
        return rows.transpose(3, 0, 2, 1).reshape(cycles, digits, channels * LOW)

    x_low = lax.iota(jnp.int32, HIGH)
    m_low = lax.iota(jnp.int32, LOW)
    cos_d, sin_d = angles(x_low, lax.iota(jnp.int32, digits), HIGH)
    first = jnp.concatenate(
        [jnp.concatenate([cos_d, -sin_d], 1), jnp.concatenate([sin_d, cos_d], 1)], 0
    )
    cos_t, sin_t = angles(x_low, m_low, PIX)
    cos_e, sin_e = angles(m_low, m_low, LOW)
    second = jnp.concatenate([cos_e, -sin_e], 0)
    upto = lax.iota(jnp.int32, sectors)
    ends = jnp.sum(jnp.where(upto[:, None] >= upto, sector_len[:, None, :], 0), axis=2)
    starts = (ends - sector_len)[:, :, None]
    ends = ends[:, :, None]
    shifts = channels // 2 + 1
    half = shifts * GROUP_ROWS

    def fixed(array):
        return pl.BlockSpec(array.shape, lambda i: (0, 0))

    def each(rows, columns):
        return pl.BlockSpec((1, rows, columns), lambda i: (i, 0, 0))

    maps, moments = pl.pallas_call(
        functools.partial(synthesis_kernel, channels, shifts),
        grid=(cycles,),
        in_specs=[
            each(digits, channels * LOW), each(digits, channels * LOW), fixed(first), fixed(second), fixed(cos_t),
            fixed(sin_t), each(sectors, 1), each(sectors, 1),
        ],
        out_specs=[each(channels, PIX), each(half, sectors)],
        out_shape=[
            jax.ShapeDtypeStruct((cycles, channels, PIX), jnp.float32),
            jax.ShapeDtypeStruct((cycles, half, sectors), jnp.float32),
        ],
        scratch_shapes=[
            pltpu.VMEM((channels * HIGH, 2 * LOW), jnp.float32),
            pltpu.VMEM((channels * HIGH, LOW), jnp.float32),
            pltpu.VMEM((half, CHUNK), jnp.float32),
        ],
        compiler_params=pltpu.CompilerParams(vmem_limit_bytes=48 << 20),
    )(by_cycle(real), by_cycle(imag), first, second, cos_t, sin_t, starts, ends)
    covariance = moments.reshape(cycles, shifts, GROUP_ROWS, sectors)[:, :, :channels]
    covariance = covariance.transpose(1, 2, 0, 3).reshape(shifts * channels, cycles * sectors)
    weights = pl.pallas_call(
        functools.partial(solve_kernel, channels),
        out_shape=jax.ShapeDtypeStruct((channels, cycles * sectors), jnp.float32),
    )(covariance, sector_len.reshape(1, cycles * sectors))
    weights = weights.reshape(channels, cycles, sectors).transpose(1, 0, 2)
    combined = pl.pallas_call(
        general_combine_kernel,
        grid=(cycles,),
        in_specs=[each(channels, PIX), each(channels, sectors), each(sectors, 1), each(sectors, 1)],
        out_specs=each(1, PIX),
        out_shape=jax.ShapeDtypeStruct((cycles, 1, PIX), jnp.float32),
    )(maps, weights, starts, ends)
    return combined.reshape(cycles, HIGH, LOW).transpose(0, 2, 1).reshape(cycles, PIX)


def general_device(coeffs, legendre, m_order, sector_len):
    slot_count, north_count, degree_count = legendre.shape[1:]
    order_count = m_order.shape[0]
    group_count = lax.axis_size("chan")
    block_count = lax.axis_size("blk")
    device_count = group_count * block_count
    channels = coeffs.shape[0] * group_count
    cycles = sector_len.shape[0]
    first_slot = (lax.axis_index("blk") * group_count + lax.axis_index("chan")) * slot_count
    orders = lax.dynamic_slice_in_dim(m_order, first_slot, slot_count, 0)
    operator = legendre[0]
    degree = order_count - degree_count + lax.iota(jnp.int32, degree_count)
    valid_mask = degree[None, :] >= orders[:, None]
    parity = (degree[None, :] + orders[:, None]) % 2
    keep = jnp.stack([valid_mask & (parity == 0), valid_mask & (parity == 1)])
    zero_value = jnp.zeros((), coeffs.dtype)
    order_joined = (
        m_order.reshape(block_count, group_count, slot_count).transpose(1, 0, 2).reshape(-1)
    )
    received = []
    for p in range(2):
        part = lax.all_to_all(coeffs[:, p], "chan", split_axis=1, concat_axis=0, tiled=True)
        masked = jnp.where(keep[:, None], part[None], zero_value)
        sums = jnp.einsum("ecsl,srl->secr", masked, operator, preferred_element_type=jnp.float32)
        even_sum, odd_sum = sums[:, 0], sums[:, 1]
        spectra = jnp.concatenate([even_sum + odd_sum, even_sum - odd_sum], axis=2)
        spectra = spectra.reshape(slot_count, channels, device_count, cycles)
        spectra = spectra.transpose(2, 0, 1, 3).reshape(
            device_count, slot_count, channels * cycles
        )
        spectra = lax.all_to_all(
            spectra, ("chan", "blk"), split_axis=0, concat_axis=0, tiled=True
        )
        received.append(
            sort_orders(order_joined, spectra.reshape(order_count, channels * cycles))
        )
    return synthesize(received[0], received[1], channels, cycles, sector_len)


def per_device(coeffs, legendre, m_order, sector_len):
    slots, north, _ = legendre.shape[1:]
    groups = lax.axis_size("chan")
    blocks = lax.axis_size("blk")
    channels = coeffs.shape[0] * groups
    cycles = sector_len.shape[0]
    fits = (
        slots % CHUNK_SLOTS == 0 and CHUNK_SLOTS < slots <= LOW and blocks == 8 and cycles * blocks == LOW
        and 2 * north == groups * LOW and channels == 12 and groups == 4
    )
    if not fits:
        return general_device(coeffs, legendre, m_order, sector_len)
    data, scale, place = exchange(coeffs, legendre[0], m_order, groups, blocks)
    return combine(data, scale, place.reshape(-1), sector_len, channels, groups)


def solution(mesh):
    placed = (
        P("chan", None, "blk", None),
        P("chan", "blk", None, None),
        P(),
        P(("chan", "blk"), None),
    )
    return jax.shard_map(
        per_device, mesh=mesh, in_specs=placed, out_specs=P(("chan", "blk"), None), check_vma=False
    )
```

```python
import functools

import jax
import jax.numpy as jnp
import numpy as np
from jax import lax
from jax.experimental import pallas as pl
from jax.experimental.pallas import tpu as pltpu
from jax.sharding import PartitionSpec as P

PIX = 8192
LOW = 128
HIGH = PIX // LOW
RIDGE_FACTOR = 0.05
TWO_PI = 6.283185307179586
CHUNK = 1024
GROUP_ROWS = 16
MESH = pl.DeviceIdType.MESH
CHUNK_SLOTS = 16
LOAD_SLOTS = 4
LOAD_BUFFERS = 3
CODE_MAX = 32767.0


def block_transpose(values, lane):
    values = list(values)
    for bit in (1, 2, 4):
        upper = (lane // 16) % (2 * bit) >= bit
        for i in range(8):
            if i & bit:
                continue
            a, b = values[i], values[i | bit]
            values[i] = jnp.where(upper, pltpu.roll(b, 16 * bit, 1), a)
            values[i | bit] = jnp.where(upper, b, pltpu.roll(a, LOW - 16 * bit, 1))
    return values


def tile_rows(channels):
    return [
        [(c, 0) for c in range(8)],
        [(c, 1) for c in range(8)],
        [(c, 0) for c in range(8, channels)] + [(c, 1) for c in range(8, channels)],
    ]


def exchange_kernel(
    groups, blocks, order_ref, order_rows, coeffs, legendre, data_out, scale_out, place_out,
    rbuf, lbuf, valid_ref, sign_ref, xs, sp, msg, inverse, scl,
    csend, crecv, lsem, dsend, drecv, ssend, srecv,
):
    chunks, _, local_channels, parts, size, degrees = rbuf.shape
    channels = groups * local_channels
    rows = channels * parts
    slots = chunks * size
    tiles = degrees // LOW
    devices = groups * blocks
    g = lax.axis_index("chan")
    b = lax.axis_index("blk")
    me = g * blocks + b

    half_blocks = blocks // 2
    half_devices = devices // 2
    my_half = b // half_blocks

    def near(i):
        at = lax.rem(b + i // groups, half_blocks)
        return lax.rem(g + i % groups, groups), my_half * half_blocks + at

    def far(i):
        at = lax.rem(b + i // groups, half_blocks)
        return lax.rem(g + i % groups, groups), (1 - my_half) * half_blocks + at

    barrier = pltpu.get_barrier_semaphore()

    def to_all(act):
        def to_far(i, carry):
            act(far(i))
            return carry

        def to_near(i, carry):
            act(near(i))
            return carry

        lax.fori_loop(0, half_devices, to_far, 0)
        lax.fori_loop(1, half_devices, to_near, 0)

    def greet(to):
        pl.semaphore_signal(barrier, inc=1, device_id=to, device_id_type=MESH)

    to_all(greet)

    def load(t):
        return pltpu.make_async_copy(
            legendre.at[pl.ds(t * LOAD_SLOTS, LOAD_SLOTS)],
            lbuf.at[lax.rem(t, LOAD_BUFFERS)], lsem.at[lax.rem(t, LOAD_BUFFERS)],
        )

    for t in range(LOAD_BUFFERS):
        load(t).start()
    pl.semaphore_wait(barrier, devices - 1)

    def start_coeffs(j):
        for down, right in ((1, 1), (0, 1), (1, 0)):
            to = lax.rem(g // 2 + down, 2) * 2 + lax.rem(g + right, 2)
            pltpu.make_async_remote_copy(
                src_ref=coeffs.at[:, :, pl.ds(to * slots + j * size, size), :],
                dst_ref=rbuf.at[j, g],
                send_sem=csend, recv_sem=crecv.at[j],
                device_id=(to, b), device_id_type=MESH,
            ).start()
        pltpu.make_async_copy(
            coeffs.at[:, :, pl.ds(g * slots + j * size, size), :], rbuf.at[j, g], crecv.at[j]
        ).start()

    for j in range(chunks):
        start_coeffs(j)
    degree = lax.broadcasted_iota(jnp.int32, (1, degrees), 1) + order_ref.shape[0] - degrees
    first_slot = (b * groups + g) * slots

    def masks(s, carry):
        order = order_ref[first_slot + s]
        keep = jnp.where(degree >= order, 1.0, 0.0)
        at = pl.ds(s, 1)
        valid_ref[at, :] = keep
        sign_ref[at, :] = jnp.where((degree + order) % 2 == 0, keep, -keep)
        return carry

    lax.fori_loop(0, slots, masks, 0)
    order = order_rows[...]
    place = jnp.bitwise_and(order, LOW - 1) * (order_ref.shape[0] // LOW)
    place_out[...] = (place + lax.shift_right_logical(order, 7)) * 8
    lane = lax.broadcasted_iota(jnp.int32, (size, LOW), 1)
    scale_lane = lax.broadcasted_iota(jnp.int32, (1, LOW), 1)
    layout = tile_rows(channels)

    def send_near(first, count):
        def send(i, carry):
            to = near(i)
            pltpu.make_async_remote_copy(
                src_ref=msg.at[pl.ds(first, count), to[0] * blocks + to[1]],
                dst_ref=data_out.at[me, pl.ds(first, count)],
                send_sem=dsend, recv_sem=drecv, device_id=to, device_id_type=MESH,
            ).start()
            return carry

        lax.fori_loop(1, half_devices, send, 0)

    def send_scale(to):
        pltpu.make_async_remote_copy(
            src_ref=scl, dst_ref=scale_out.at[me],
            send_sem=ssend, recv_sem=srecv, device_id=to, device_id_type=MESH,
        ).start()

    def chunk(j, last):
        pltpu.make_async_copy(rbuf.at[j], rbuf.at[j], crecv.at[j]).wait()
        if last:
            send_near(0, chunks - 1)
        for q in range(groups):
            for c in range(local_channels):
                for p in range(parts):
                    row = ((q * local_channels + c) * parts + p) * size
                    wide = rbuf[j, q, c, p].astype(jnp.float32)
                    for t in range(tiles):
                        xs[t, row : row + size, :] = wide[:, t * LOW : (t + 1) * LOW]

        def step(u, carry):
            t = j * (size // LOAD_SLOTS) + u
            load(t).wait()
            for v in range(LOAD_SLOTS):
                s = u * LOAD_SLOTS + v
                x = jnp.concatenate(
                    [xs[i, pl.ds(s, rows, stride=size), :] for i in range(tiles)], axis=1
                )
                at = pl.ds(j * size + s, 1)
                both = jnp.concatenate([x * valid_ref[at, :], x * sign_ref[at, :]], axis=0)
                sums = lax.dot_general(
                    both.astype(jnp.bfloat16), lbuf[lax.rem(t, LOAD_BUFFERS), v],
                    (((1,), (1,)), ((), ())), preferred_element_type=jnp.float32,
                )
                for i in range(sp.shape[0]):
                    sp[i, pl.ds(s, 2 * rows, stride=size), :] = sums[:, i * LOW : (i + 1) * LOW]

            @pl.when(t + LOAD_BUFFERS < slots // LOAD_SLOTS)
            def _():
                load(t + LOAD_BUFFERS).start()

            return carry

        lax.fori_loop(0, size // LOAD_SLOTS, step, 0)

        def piece(half, side, c, p):
            row = (half * rows + c * parts + p) * size
            return sp[side, row : row + size, :]

        scales = scl[...]
        for c in range(channels):
            top = jnp.abs(piece(0, 0, c, 0))
            for half in range(2):
                for side in range(sp.shape[0]):
                    for p in range(parts):
                        top = jnp.maximum(top, jnp.abs(piece(half, side, c, p)))
            top = jnp.maximum(jnp.max(top, keepdims=True), 1e-30)
            unit = (top * (1.0078125 / CODE_MAX)).astype(jnp.bfloat16).astype(jnp.float32)
            inverse[c] = jnp.broadcast_to(1.0 / unit, (size, LOW))
            scales = jnp.where(scale_lane == j * 16 + c, unit, scales)
        scl[...] = scales
        if last:
            to_all(send_scale)
        for half in range(2):
            for side in range(sp.shape[0]):
                first = (half * sp.shape[0] + side) * blocks
                for tile, members in enumerate(layout):
                    values = block_transpose(
                        [piece(half, side, c, p) * inverse[c] for c, p in members], lane
                    )
                    for k in range(blocks):
                        msg[j, first + k, tile] = jnp.round(values[k]).astype(jnp.int16)

        def send(i, carry):
            to = far(i)
            pltpu.make_async_remote_copy(
                src_ref=msg.at[j, to[0] * blocks + to[1]], dst_ref=data_out.at[me, j],
                send_sem=dsend, recv_sem=drecv, device_id=to, device_id_type=MESH,
            ).start()
            return carry

        lax.fori_loop(0, half_devices, send, 0)
        if last:
            send_near(j, 1)
        pltpu.make_async_copy(msg.at[j, me], data_out.at[me, j], drecv).start()

    def early(j, carry):
        chunk(j, False)
        return carry

    scl[...] = jnp.zeros_like(scl)
    lax.fori_loop(0, chunks - 1, early, 0)
    chunk(chunks - 1, True)
    pltpu.make_async_copy(scl, scale_out.at[me], srecv).start()

    def settle(ref, sem):
        pltpu.make_async_copy(ref, ref, sem).wait()

    settle(rbuf.at[:, pl.ds(0, groups - 1)], csend)
    settle(msg.at[:, pl.ds(0, devices - 1)], dsend)
    settle(scale_out.at[pl.ds(0, devices - 1)], ssend)
    settle(data_out, drecv)
    settle(scale_out, srecv)


def exchange(coeffs, operator, m_order, groups, blocks):
    local_channels, parts, _, degrees = coeffs.shape
    slots, north, _ = operator.shape
    channels = groups * local_channels
    devices = groups * blocks
    size = CHUNK_SLOTS
    chunks = slots // size
    rows = channels * parts
    sides = north // LOW
    anywhere = pl.BlockSpec(memory_space=pl.ANY)
    vmem = pl.BlockSpec(memory_space=pltpu.VMEM)
    dma = pltpu.SemaphoreType.DMA
    return pl.pallas_call(
        functools.partial(exchange_kernel, groups, blocks),
        in_specs=[pl.BlockSpec(memory_space=pltpu.SMEM), vmem, anywhere, anywhere],
        out_specs=[anywhere, anywhere, vmem],
        out_shape=[
            jax.ShapeDtypeStruct((devices, chunks, 3, size, LOW), jnp.int16),
            jax.ShapeDtypeStruct((devices, 1, LOW), jnp.float32),
            jax.ShapeDtypeStruct((m_order.shape[0] // LOW, LOW), jnp.int32),
        ],
        scratch_shapes=[
            pltpu.VMEM((chunks, groups, local_channels, parts, size, degrees), jnp.bfloat16),
            pltpu.VMEM((LOAD_BUFFERS, LOAD_SLOTS, north, degrees), jnp.bfloat16),
            pltpu.VMEM((slots, degrees), jnp.float32),
            pltpu.VMEM((slots, degrees), jnp.float32),
            pltpu.VMEM((degrees // LOW, rows * size, LOW), jnp.float32),
            pltpu.VMEM((sides, 2 * rows * size, LOW), jnp.float32),
            pltpu.VMEM((chunks, devices, 3, size, LOW), jnp.int16),
            pltpu.VMEM((channels, size, LOW), jnp.float32),
            pltpu.VMEM((1, LOW), jnp.float32),
            dma, dma((chunks,)), dma((LOAD_BUFFERS,)), dma, dma, dma, dma,
        ],
        compiler_params=pltpu.CompilerParams(
            collective_id=0, has_side_effects=True, vmem_limit_bytes=58 << 20
        ),
    )(m_order, m_order.reshape(-1, LOW), coeffs, operator)


def halves(value):
    upper = value.astype(jnp.bfloat16)
    return upper, (value - upper.astype(jnp.float32)).astype(jnp.bfloat16)


def synthesis_tables(order_count):
    digits = order_count // LOW
    order = np.arange(LOW)[:, None, None] + LOW * np.arange(digits)[None, None, :]
    angle = order * np.arange(HIGH)[None, :, None] % PIX * (2.0 * np.pi / PIX)
    weight = np.where(order == 0, 1.0, 2.0)
    cos, sin = weight * np.cos(angle), weight * np.sin(angle)
    turn = np.stack([np.concatenate([cos, -sin], 2), np.concatenate([sin, cos], 2)], 2)
    turn = turn.reshape(LOW, 2 * HIGH, 2 * digits).astype(np.float32)
    turn_upper = turn.astype(jnp.bfloat16)
    turn_lower = (turn - turn_upper.astype(np.float32)).astype(jnp.bfloat16)
    first = np.concatenate([turn_upper, turn_upper, turn_lower], 2)
    angle = np.arange(LOW)[:, None] * np.arange(LOW)[None, :] % LOW * (2.0 * np.pi / LOW)
    wave = np.concatenate([np.cos(angle), -np.sin(angle)], 1).astype(np.float32)
    wave_upper = wave.astype(jnp.bfloat16)
    wave_lower = (wave - wave_upper.astype(np.float32)).astype(jnp.bfloat16)
    return first, np.concatenate([wave_upper, wave_lower], 0)


def pair_place(a, b):
    if b < 8:
        shift = b - a
        if shift > 4:
            shift, a = 8 - shift, b
        return (shift, (a - 1) % 8) if shift == 2 else (shift, a)
    if a < 8:
        tile, move = {0: (5, 0), 1: (6, 3), 2: (7, 3), 3: (8, 1)}[(b - 8 - a) % 4]
        return tile, (a - move) % 8
    a, b = a - 8, b - 8
    shift = b - a
    if shift == 2:
        return 10, a
    return 9, {0: a, 1: 4 + a, 3: 4 + b}[shift]


TILES = 11
ROOM = LOW + 8
SPACE = HIGH + 8


def combine_kernel(
    channels, groups, place_ref, data_any, scale_any, spread, first_any, wave, lens, out,
    data, scale, first, spare, order_rows, late, weighed, turned, partial, held, cov,
    data_sem, scale_sem, first_sem,
):
    sources, chunks, _, size, _ = data.shape
    slots = chunks * size
    blocks = sources // groups
    digits = place_ref.shape[0] // LOW
    fetch_scale = pltpu.make_async_copy(scale_any, scale, scale_sem)
    fetch_scale.start()

    def fetch_data(i):
        part = pl.ds(i * blocks, blocks)
        return pltpu.make_async_copy(data_any.at[part], data.at[part], data_sem.at[i])

    for i in range(groups):
        fetch_data(i).start()
    fetch = pltpu.make_async_copy(first_any, first, first_sem)
    fetch.start()
    fetch_scale.wait()

    chunk_lane = lax.broadcasted_iota(jnp.int32, (8, LOW), 1) // 16
    chunk_lane = chunk_lane == lax.broadcasted_iota(jnp.int32, (8, LOW), 0)

    def gather(src, carry):
        @pl.when(lax.rem(src, blocks) == 0)
        def _():
            fetch_data(src // blocks).wait()

        units = jnp.where(chunk_lane, scale[src], 0.0).astype(jnp.bfloat16)
        unit = jnp.dot(units, spread[...], preferred_element_type=jnp.float32)
        for j in range(chunks):
            for t in range(3):
                value = data[src, j, t].astype(jnp.float32)
                value = value * unit[j : j + 1, t * LOW : (t + 1) * LOW]
                spare[pl.ds(j * size * 8 + t, size, stride=8), :] = value
        base = (lax.rem(src, blocks) * groups + src // blocks) * slots

        def move(s, carry):
            to = pl.multiple_of(place_ref[base + s], 8)
            order_rows[pl.ds(to, 8), :] = spare[pl.ds(pl.multiple_of(s * 8, 8), 8), :]
            return carry

        return lax.fori_loop(0, slots, move, carry, unroll=slots)

    lax.fori_loop(0, sources, gather, 0)
    fetch.wait()
    lane_d = lax.broadcasted_iota(jnp.int32, (digits, LOW), 1)
    wide = ROOM * 2 * HIGH

    def turn(l, carry):
        t0, t1, t2 = (
            order_rows[pl.ds(l * (digits * 8) + t, digits, stride=8), :] for t in range(3)
        )
        t3 = pltpu.roll(t2, LOW // 2, 1)
        real = jnp.where(lane_d < LOW // 2, t2, t3)
        imag = jnp.where(lane_d < LOW // 2, t3, t2)
        x = jnp.concatenate(
            [jnp.concatenate([t0, real], 1), jnp.concatenate([t1, imag], 1)], 0
        )
        upper, lower = halves(x)
        y = jnp.dot(
            first[l], jnp.concatenate([upper, lower, upper], 0), preferred_element_type=jnp.float32
        )
        turned[pl.ds(l, 2 * HIGH, stride=ROOM), :] = y[:, :LOW]
        turned[pl.ds(wide + l, 2 * HIGH, stride=ROOM), :] = y[:, LOW:]
        return carry

    lax.fori_loop(0, LOW, turn, 0, unroll=64)

    early = HIGH // 2
    second = early * LOW

    def spin_into(maps, x, place):
        def part(i):
            at = pl.multiple_of((2 * x + i) * ROOM, 8)
            return jnp.concatenate(
                [turned[pl.ds(at, LOW), :], turned[pl.ds(wide + at, LOW), :]], 1
            )

        upper, lower = halves(jnp.concatenate([part(0), part(1)], 0))
        main = jnp.dot(wave[...], upper, preferred_element_type=jnp.float32)
        rest = jnp.dot(wave[:LOW], lower, preferred_element_type=jnp.float32)
        value = main[:LOW] + main[LOW:] + rest
        maps[pl.ds(pl.multiple_of(place * LOW, LOW), LOW), :] = value[:, :LOW]
        maps[pl.ds(pl.multiple_of(second + place * LOW, LOW), LOW), :] = value[:, LOW:]

    def spin(x, carry):
        spin_into(order_rows, x, x)
        return carry

    lax.fori_loop(0, early, spin, 0, unroll=32)

    cycles, sectors = lens.shape
    copies = lax.broadcasted_iota(jnp.int32, (cycles, LOW), 1) % cycles
    copies = copies == lax.broadcasted_iota(jnp.int32, (cycles, LOW), 0)
    copies = jnp.where(copies, 1.0, 0.0).astype(jnp.bfloat16)

    def spread_out(values):
        return lax.dot_general(
            values.astype(jnp.float32).astype(jnp.bfloat16), copies, (((0,), (0,)), ((), ())),
            preferred_element_type=jnp.float32,
        )

    length = 128.0 * spread_out(lax.shift_right_logical(lens[...], 7))
    length = length + spread_out(jnp.bitwise_and(lens[...], 127))
    length = length.astype(jnp.int32)
    ends = []
    for k in range(sectors):
        ends.append(length[k : k + 1] + ends[-1] if k else length[:1])
    lane = lax.broadcasted_iota(jnp.int32, (8, LOW), 1)
    sub = lax.broadcasted_iota(jnp.int32, (8, LOW), 0)

    def block(j):
        begin = (j * 8 + sub) * HIGH
        sector = jnp.zeros((8, LOW), jnp.int32)
        after = jnp.full((8, LOW), 2 * PIX, jnp.int32)
        for k in range(sectors):
            past = ends[k] <= begin
            sector = sector + jnp.where(past, 1, 0)
            after = jnp.minimum(after, jnp.where(past, 2 * PIX, ends[k]))
        return sector, after - begin

    def pair(maps, j, place):
        at = pl.multiple_of(place * LOW + j * 8, 8)
        return maps[pl.ds(at, 8), :], maps[pl.ds(second + at, 8), :]

    def add(limit, x, values, acc):
        a, b = values
        ended = limit == x
        a1, a3, a4 = (pltpu.roll(a, LOW - 16 * d, 1) for d in (1, 3, 4))
        b1, b2 = (pltpu.roll(b, LOW - 16 * d, 1) for d in (1, 2))
        bb = jnp.where(lane < LOW // 2, b, b1)
        left = [a, a, a3, a, a, a, a3, a3, b, b, b]
        right = [a, a1, a1, a3, a4, b, b, b1, a1, bb, b2]
        head = [jnp.where(ended, acc[i], acc[TILES + i]) for i in range(TILES)]
        return [acc[i] + left[i] * right[i] for i in range(TILES)] + head

    def first_half(j, carry):
        _, limit = block(j)
        acc = [jnp.zeros((8, LOW), jnp.float32)] * (2 * TILES)
        share = early // (LOW // 8)
        for x in range(early):
            if x < share:
                spin_into(late, early + j * share + x, j * share + x)
            acc = add(limit, x, pair(order_rows, j, x), acc)
        for i in range(2 * TILES):
            partial[j, i] = acc[i]
        return carry

    lax.fori_loop(0, LOW // 8, first_half, 0)

    def moments(j, carry):
        sector, limit = block(j)
        acc = [partial[j, i] for i in range(2 * TILES)]
        for x in range(early):
            acc = add(limit, early + x, pair(late, j, x), acc)
        for i in range(TILES):
            head = jnp.where(limit >= HIGH, acc[i], acc[TILES + i])
            partial[j, i] = head
            partial[j, TILES + i] = acc[i] - head
        held[j] = sector
        return carry

    lax.fori_loop(0, LOW // 8, moments, 0)

    def collect(k, carry):
        acc = [jnp.zeros((8, LOW), jnp.float32)] * TILES
        for j in range(LOW // 8):
            here = held[j] == k
            there = held[j] == k - 1
            for i in range(TILES):
                tail = jnp.where(there, partial[j, TILES + i], 0.0)
                acc[i] = acc[i] + jnp.where(here, partial[j, i], tail)
        for i in range(TILES):
            cov[i, pl.ds(k, 1), :] = jnp.sum(acc[i], axis=0, keepdims=True)
        return carry

    lax.fori_loop(0, sectors, collect, 0, unroll=2)
    share = 1.0 / length.astype(jnp.float32)

    def entry(a, b):
        tile, group = pair_place(a, b)
        value = cov[tile] * share
        return pltpu.roll(value, LOW - 16 * group, 1) if group else value

    full = {(a, b): entry(a, b) for a in range(channels) for b in range(a, channels)}
    trace = full[0, 0]
    for a in range(1, channels):
        trace = trace + full[a, a]
    ridge = trace * (RIDGE_FACTOR / channels)
    for a in range(channels):
        full[a, a] = full[a, a] + ridge
    rhs = [jnp.ones_like(ridge) for _ in range(channels)]
    inverse = []
    for a in range(channels):
        inverse.append(1.0 / full[a, a])
        for b in range(a + 1, channels):
            factor = full[a, b] * inverse[a]
            for c in range(b, channels):
                full[b, c] = full[b, c] - factor * full[a, c]
            rhs[b] = rhs[b] - factor * rhs[a]
    solved = [None] * channels
    for a in reversed(range(channels)):
        value = rhs[a]
        for b in range(a + 1, channels):
            value = value - full[a, b] * solved[b]
        solved[a] = value * inverse[a]
    total = solved[0]
    for a in range(1, channels):
        total = total + solved[a]
    near = jnp.zeros_like(total)
    far = jnp.zeros_like(total)
    group = lax.broadcasted_iota(jnp.int32, total.shape, 1) // 16
    for a in range(channels):
        weight = solved[a] / total
        place = a % 8
        moved = pltpu.roll(weight, 16 * place, 1) if place else weight
        if a < 8:
            near = jnp.where(group == place, moved, near)
        else:
            far = jnp.where(group == place, moved, far)
    cov[0] = near
    cov[1] = far

    def apply(j, carry):
        sector, limit = block(j)
        picked = [jnp.zeros((8, LOW), jnp.float32) for _ in range(4)]
        for k in range(sectors):
            near_k = cov[0, k : k + 1, :]
            far_k = cov[1, k : k + 1, :]
            here = sector == k
            there = sector + 1 == k
            picked[0] = jnp.where(here, near_k, picked[0])
            picked[1] = jnp.where(here, far_k, picked[1])
            picked[2] = jnp.where(there, near_k, picked[2])
            picked[3] = jnp.where(there, far_k, picked[3])

        for x in range(HIGH):
            a, b = pair(order_rows, j, x) if x < early else pair(late, j, x - early)
            inside = limit > x
            value = jnp.where(inside, picked[0], picked[2]) * a
            value = value + jnp.where(inside, picked[1], picked[3]) * b
            weighed[pl.ds(j * 8 * SPACE + x, 8, stride=SPACE), :] = value
        return carry

    lax.fori_loop(0, LOW // 8, apply, 0)
    pick = lax.broadcasted_iota(jnp.int32, (16, 2 * LOW), 1) % 16
    pick = jnp.where(pick == lax.broadcasted_iota(jnp.int32, (16, 2 * LOW), 0), 1.0, 0.0)
    pick = pick.astype(jnp.bfloat16)
    for x in range(0, PIX, 256):
        upper, lower = halves(
            jnp.concatenate(
                [
                    weighed[y * SPACE : y * SPACE + HIGH, :]
                    for y in range(x // HIGH, (x + 256) // HIGH)
                ],
                0,
            )
        )
        out[:, x : x + 256] = lax.dot_general(
            pick, jnp.concatenate([upper, lower], 1), (((1,), (1,)), ((), ())),
            preferred_element_type=jnp.float32,
        )


def combine(data, scale, place, sector_len, channels, groups):
    order_count = place.shape[0]
    cycles, sectors = sector_len.shape
    first, wave = synthesis_tables(order_count)
    spread = np.zeros((16, 3 * LOW), np.float32)
    for tile, members in enumerate(tile_rows(channels)):
        for i, (c, _) in enumerate(members):
            spread[c, tile * LOW + 16 * i : tile * LOW + 16 * i + 16] = 1.0
    spread = np.tile(spread, (8, 1))
    vmem = pl.BlockSpec(memory_space=pltpu.VMEM)
    anywhere = pl.BlockSpec(memory_space=pl.ANY)
    return pl.pallas_call(
        functools.partial(combine_kernel, channels, groups),
        in_specs=[
            pl.BlockSpec(memory_space=pltpu.SMEM), anywhere, anywhere, vmem, anywhere, vmem, vmem,
        ],
        out_specs=vmem,
        out_shape=jax.ShapeDtypeStruct((cycles, PIX), jnp.float32),
        scratch_shapes=[
            pltpu.VMEM(data.shape, jnp.int16),
            pltpu.VMEM(scale.shape, jnp.float32),
            pltpu.VMEM(first.shape, jnp.bfloat16),
            pltpu.VMEM((data.shape[1] * data.shape[3] * 8, LOW), jnp.float32),
            pltpu.VMEM((max(order_count * 8, PIX), LOW), jnp.float32),
            pltpu.VMEM((PIX, LOW), jnp.float32),
            pltpu.VMEM((LOW * SPACE, LOW), jnp.float32),
            pltpu.VMEM((2 * ROOM * 2 * HIGH, LOW), jnp.float32),
            pltpu.VMEM((LOW // 8, 2 * TILES, 8, LOW), jnp.float32),
            pltpu.VMEM((LOW // 8, 8, LOW), jnp.int32),
            pltpu.VMEM((TILES, sectors, LOW), jnp.float32),
            pltpu.SemaphoreType.DMA((groups,)),
            pltpu.SemaphoreType.DMA,
            pltpu.SemaphoreType.DMA,
        ],
        compiler_params=pltpu.CompilerParams(vmem_limit_bytes=58 << 20),
    )(
        place, data, scale, jnp.asarray(spread, jnp.bfloat16), jnp.asarray(first), jnp.asarray(wave),
        sector_len,
    )


def permute_kernel(order_ref, rows_in, rows_out):
    def step(slot, carry):
        rows_out[pl.ds(order_ref[slot], 1), :] = rows_in[pl.ds(slot, 1), :]
        return carry

    lax.fori_loop(0, rows_in.shape[0], step, 0, unroll=8)


def sort_orders(orders, rows):
    whole = pl.BlockSpec(rows.shape, lambda i, order: (0, 0))
    return pl.pallas_call(
        permute_kernel,
        grid_spec=pltpu.PrefetchScalarGridSpec(
            num_scalar_prefetch=1, grid=(1,), in_specs=[whole], out_specs=whole
        ),
        out_shape=jax.ShapeDtypeStruct(rows.shape, jnp.float32),
        compiler_params=pltpu.CompilerParams(vmem_limit_bytes=32 << 20),
    )(orders, rows)


def split_dot(left, right):
    left_upper, left_lower = halves(left)
    right_upper, right_lower = halves(right)
    return jnp.dot(
        jnp.concatenate([left_upper, left_upper, left_lower], axis=1),
        jnp.concatenate([right_upper, right_lower, right_upper], axis=0),
        preferred_element_type=jnp.float32,
    )


def member_of(start, end, base, count):
    place = lax.broadcasted_iota(jnp.int32, (start.shape[0], count), 1) + base
    pixel = (place % LOW) * HIGH + place // LOW
    return (pixel >= start) & (pixel < end)


def synthesis_kernel(
    channels, shifts, real_ref, imag_ref, d_ref, e_ref, tc_ref, ts_ref, start_ref, end_ref,
    map_ref, moment_ref, z_ref, m_ref, p_ref,
):
    first = split_dot(d_ref[...], jnp.concatenate([real_ref[0], imag_ref[0]], axis=0))
    cos_turn = tc_ref[...]
    sin_turn = ts_ref[...]
    for c in range(channels):
        real = first[:HIGH, c * LOW : (c + 1) * LOW]
        imag = first[HIGH:, c * LOW : (c + 1) * LOW]
        z_ref[c * HIGH : (c + 1) * HIGH, :LOW] = real * cos_turn - imag * sin_turn
        z_ref[c * HIGH : (c + 1) * HIGH, LOW:] = real * sin_turn + imag * cos_turn
    m_ref[...] = split_dot(z_ref[...], e_ref[...])
    for x2 in range(HIGH):
        map_ref[0, :, x2 * LOW : (x2 + 1) * LOW] = m_ref[pl.ds(x2, channels, stride=HIGH), :]
    p_ref[...] = jnp.zeros_like(p_ref)
    start = start_ref[0]
    end = end_ref[0]
    total = jnp.zeros((2 * shifts * GROUP_ROWS, start.shape[0]), jnp.float32)
    for chunk in range(PIX // CHUNK):
        base = chunk * CHUNK
        values = map_ref[0, :, base : base + CHUNK]
        twice = jnp.concatenate([values, values], axis=0)
        for d in range(shifts):
            p_ref[d * GROUP_ROWS : d * GROUP_ROWS + channels, :] = (
                values * twice[d : d + channels]
            )
        product = p_ref[...]
        upper, lower = halves(product)
        member = jnp.where(member_of(start, end, base, CHUNK), 1.0, 0.0).astype(jnp.bfloat16)
        total += lax.dot_general(
            jnp.concatenate([upper, lower], axis=0), member,
            (((1,), (1,)), ((), ())), preferred_element_type=jnp.float32,
        )
    half = shifts * GROUP_ROWS
    moment_ref[0] = total[:half] + total[half:]


def solve_kernel(channels, cov_ref, len_ref, w_ref):
    scale = 1.0 / len_ref[...].astype(jnp.float32)

    def entry(a, b):
        shift = (b - a) % channels
        row = a
        if shift > channels // 2:
            shift, row = channels - shift, b
        return cov_ref[pl.ds(shift * channels + row, 1), :] * scale

    full = {(a, b): entry(a, b) for a in range(channels) for b in range(a, channels)}
    trace = full[0, 0]
    for a in range(1, channels):
        trace = trace + full[a, a]
    ridge = trace * (RIDGE_FACTOR / channels)
    for a in range(channels):
        full[a, a] = full[a, a] + ridge
    rhs = [jnp.ones_like(scale) for _ in range(channels)]
    inverse = []
    for a in range(channels):
        inverse.append(1.0 / full[a, a])
        for b in range(a + 1, channels):
            factor = full[a, b] * inverse[a]
            for c in range(b, channels):
                full[b, c] = full[b, c] - factor * full[a, c]
            rhs[b] = rhs[b] - factor * rhs[a]
    solved = [None] * channels
    for a in reversed(range(channels)):
        value = rhs[a]
        for b in range(a + 1, channels):
            value = value - full[a, b] * solved[b]
        solved[a] = value * inverse[a]
    total = solved[0]
    for a in range(1, channels):
        total = total + solved[a]
    for a in range(channels):
        w_ref[pl.ds(a, 1), :] = solved[a] / total


def general_combine_kernel(map_ref, w_ref, start_ref, end_ref, out_ref):
    start = start_ref[0]
    end = end_ref[0]
    weights = w_ref[0]
    upper, middle = halves(weights)
    lower = weights - upper.astype(jnp.float32) - middle.astype(jnp.float32)
    pieces = jnp.concatenate([upper, middle, lower.astype(jnp.bfloat16)], axis=1)
    for chunk in range(PIX // CHUNK):
        base = chunk * CHUNK
        member = jnp.where(member_of(start, end, base, CHUNK), 1.0, 0.0).astype(jnp.bfloat16)
        pixel_weights = jnp.dot(
            pieces, jnp.concatenate([member, member, member], axis=0),
            preferred_element_type=jnp.float32,
        )
        out_ref[0, :, base : base + CHUNK] = jnp.sum(
            pixel_weights * map_ref[0, :, base : base + CHUNK], axis=0, keepdims=True
        )


def angles(left, right, period):
    phase = left[:, None] * right[None, :] % period
    turned = phase.astype(jnp.float32) * (TWO_PI / period)
    return jnp.cos(turned), jnp.sin(turned)


def synthesize(real, imag, channels, cycles, sector_len):
    order_count = real.shape[0]
    digits = order_count // LOW
    sectors = sector_len.shape[1]
    weight = jnp.where(lax.iota(jnp.int32, order_count) == 0, 1.0, 2.0).astype(jnp.float32)

    def by_cycle(rows):
        rows = (rows * weight[:, None]).reshape(digits, LOW, channels, cycles)
        return rows.transpose(3, 0, 2, 1).reshape(cycles, digits, channels * LOW)

    x_low = lax.iota(jnp.int32, HIGH)
    m_low = lax.iota(jnp.int32, LOW)
    cos_d, sin_d = angles(x_low, lax.iota(jnp.int32, digits), HIGH)
    first = jnp.concatenate(
        [jnp.concatenate([cos_d, -sin_d], 1), jnp.concatenate([sin_d, cos_d], 1)], 0
    )
    cos_t, sin_t = angles(x_low, m_low, PIX)
    cos_e, sin_e = angles(m_low, m_low, LOW)
    second = jnp.concatenate([cos_e, -sin_e], 0)
    upto = lax.iota(jnp.int32, sectors)
    ends = jnp.sum(jnp.where(upto[:, None] >= upto, sector_len[:, None, :], 0), axis=2)
    starts = (ends - sector_len)[:, :, None]
    ends = ends[:, :, None]
    shifts = channels // 2 + 1
    half = shifts * GROUP_ROWS

    def fixed(array):
        return pl.BlockSpec(array.shape, lambda i: (0, 0))

    def each(rows, columns):
        return pl.BlockSpec((1, rows, columns), lambda i: (i, 0, 0))

    maps, moments = pl.pallas_call(
        functools.partial(synthesis_kernel, channels, shifts),
        grid=(cycles,),
        in_specs=[
            each(digits, channels * LOW), each(digits, channels * LOW), fixed(first), fixed(second), fixed(cos_t),
            fixed(sin_t), each(sectors, 1), each(sectors, 1),
        ],
        out_specs=[each(channels, PIX), each(half, sectors)],
        out_shape=[
            jax.ShapeDtypeStruct((cycles, channels, PIX), jnp.float32),
            jax.ShapeDtypeStruct((cycles, half, sectors), jnp.float32),
        ],
        scratch_shapes=[
            pltpu.VMEM((channels * HIGH, 2 * LOW), jnp.float32),
            pltpu.VMEM((channels * HIGH, LOW), jnp.float32),
            pltpu.VMEM((half, CHUNK), jnp.float32),
        ],
        compiler_params=pltpu.CompilerParams(vmem_limit_bytes=48 << 20),
    )(by_cycle(real), by_cycle(imag), first, second, cos_t, sin_t, starts, ends)
    covariance = moments.reshape(cycles, shifts, GROUP_ROWS, sectors)[:, :, :channels]
    covariance = covariance.transpose(1, 2, 0, 3).reshape(shifts * channels, cycles * sectors)
    weights = pl.pallas_call(
        functools.partial(solve_kernel, channels),
        out_shape=jax.ShapeDtypeStruct((channels, cycles * sectors), jnp.float32),
    )(covariance, sector_len.reshape(1, cycles * sectors))
    weights = weights.reshape(channels, cycles, sectors).transpose(1, 0, 2)
    combined = pl.pallas_call(
        general_combine_kernel,
        grid=(cycles,),
        in_specs=[each(channels, PIX), each(channels, sectors), each(sectors, 1), each(sectors, 1)],
        out_specs=each(1, PIX),
        out_shape=jax.ShapeDtypeStruct((cycles, 1, PIX), jnp.float32),
    )(maps, weights, starts, ends)
    return combined.reshape(cycles, HIGH, LOW).transpose(0, 2, 1).reshape(cycles, PIX)


def general_device(coeffs, legendre, m_order, sector_len):
    slot_count, north_count, degree_count = legendre.shape[1:]
    order_count = m_order.shape[0]
    group_count = lax.axis_size("chan")
    block_count = lax.axis_size("blk")
    device_count = group_count * block_count
    channels = coeffs.shape[0] * group_count
    cycles = sector_len.shape[0]
    first_slot = (lax.axis_index("blk") * group_count + lax.axis_index("chan")) * slot_count
    orders = lax.dynamic_slice_in_dim(m_order, first_slot, slot_count, 0)
    operator = legendre[0]
    degree = order_count - degree_count + lax.iota(jnp.int32, degree_count)
    valid_mask = degree[None, :] >= orders[:, None]
    parity = (degree[None, :] + orders[:, None]) % 2
    keep = jnp.stack([valid_mask & (parity == 0), valid_mask & (parity == 1)])
    zero_value = jnp.zeros((), coeffs.dtype)
    order_joined = (
        m_order.reshape(block_count, group_count, slot_count).transpose(1, 0, 2).reshape(-1)
    )
    received = []
    for p in range(2):
        part = lax.all_to_all(coeffs[:, p], "chan", split_axis=1, concat_axis=0, tiled=True)
        masked = jnp.where(keep[:, None], part[None], zero_value)
        sums = jnp.einsum("ecsl,srl->secr", masked, operator, preferred_element_type=jnp.float32)
        even_sum, odd_sum = sums[:, 0], sums[:, 1]
        spectra = jnp.concatenate([even_sum + odd_sum, even_sum - odd_sum], axis=2)
        spectra = spectra.reshape(slot_count, channels, device_count, cycles)
        spectra = spectra.transpose(2, 0, 1, 3).reshape(
            device_count, slot_count, channels * cycles
        )
        spectra = lax.all_to_all(
            spectra, ("chan", "blk"), split_axis=0, concat_axis=0, tiled=True
        )
        received.append(
            sort_orders(order_joined, spectra.reshape(order_count, channels * cycles))
        )
    return synthesize(received[0], received[1], channels, cycles, sector_len)


def per_device(coeffs, legendre, m_order, sector_len):
    slots, north, _ = legendre.shape[1:]
    groups = lax.axis_size("chan")
    blocks = lax.axis_size("blk")
    channels = coeffs.shape[0] * groups
    cycles = sector_len.shape[0]
    fits = (
        slots % CHUNK_SLOTS == 0 and CHUNK_SLOTS < slots <= LOW and blocks == 8 and cycles * blocks == LOW
        and 2 * north == groups * LOW and channels == 12 and groups == 4
    )
    if not fits:
        return general_device(coeffs, legendre, m_order, sector_len)
    data, scale, place = exchange(coeffs, legendre[0], m_order, groups, blocks)
    return combine(data, scale, place.reshape(-1), sector_len, channels, groups)


def solution(mesh):
    placed = (
        P("chan", None, "blk", None),
        P("chan", "blk", None, None),
        P(),
        P(("chan", "blk"), None),
    )
    return jax.shard_map(
        per_device, mesh=mesh, in_specs=placed, out_specs=P(("chan", "blk"), None), check_vma=False
    )
```
